32 devices in a mesh: region: 8 (over y, x, core), tile: 4 (over z).
Axes of the slice: x: 2, y: 2, z: 4, core: 2. Of those that a mesh axis runs over, the one named last changes fastest.
Arguments:
- params: float32 [256, 59, 128], P(('region', 'tile')), may hold values from -6 to 6
- first_moment: float32 [256, 59, 128], P(('region', 'tile')), may hold values from -0.006 to 0.006
- second_moment: float32 [256, 59, 128], P(('region', 'tile')), may hold values from 1e-09 to 2e-05
- view_basis: float32 [16], replicated, may hold values from -1.5 to 1.5
- target: float32 [32, 3, 1024], P(('region', 'tile')), may hold values from 0 to 1
- tile_blocks: int32 [32, 4], P(('region', 'tile')), may hold values from 0 to 31, as said below
- moving: int32 [32, 4], P(('region', 'tile')), may hold values from 0 to 7, as said below
Outputs:
- new_params: float32 [256, 59, 128], P(('region', 'tile'))
- new_first: float32 [256, 59, 128], P(('region', 'tile'))
- new_second: float32 [256, 59, 128], P(('region', 'tile'))
- image: float32 [32, 3, 1024], P(('region', 'tile'))
The draws below stay inside these ranges and needn't reach their ends.
Inputs may be any that keep to these rules, and one draw needn't show every extreme that they name: `tile_blocks`: row i lists the blocks of the tile of device i front to back, as ids within that device's region; it names exactly one block of each of the region's 4 devices, the device at tile index k owning ids k * 8 to (k + 1) * 8 - 1. `moving`: row i names 4 different blocks of device i, counted from 0 within the device.
All inputs are finite; a program needn't handle non-finite values.
Results may differ from the reference program's by a relative error of at most 0.0003.
Values sent between devices are 32-bit elements; how exact they have to be, the bound alone decides.
No kernel may reach another device: no remote copies, remote signals or barrier semaphores. Data moves between devices by JAX's collectives and lax.ppermute only.
A program may use at most 64 MiB of HBM per device.

```python
import math
import jax
import jax.numpy as jnp
from jax import lax

G = 128
NPARAM = 59
SH = 16
NPROJ = 9
TILE_SIDE = 32
BLK_DEV = 8
PIX = 1024
LIST = 4
MOVE_DEV = 4
BLOCKS = 256
TILES = 32
N_REGION = 8
N_TILE = 4


def draw_params(key, part):
    key_base = jax.random.fold_in(key, 31)
    key_opacity = jax.random.fold_in(key, 32)
    base = jnp.clip(jax.random.normal(key_base, (BLOCKS, NPARAM, G), jnp.float32), -6.0, 6.0)
    logits = jax.random.uniform(key_opacity, (BLOCKS, G), jnp.float32, -6.0, -5.0)
    return base.at[:, 10, :].set(logits)


def draw_tile_blocks(key, part):
    key_order = jax.random.fold_in(key, 11)
    key_pick = jax.random.fold_in(key, 12)
    orders = jax.vmap(lambda one_key: jax.random.permutation(one_key, LIST))(jax.random.split(key_order, TILES))
    picks = jax.random.randint(key_pick, (TILES, LIST), 0, BLK_DEV)
    first_row = jnp.where(orders[0] == 0, 0, jnp.where(orders[0] == LIST - 1, BLK_DEV - 1, picks[0]))
    picks = picks.at[0].set(first_row)
    return (orders * BLK_DEV + picks).astype(jnp.int32)


def draw_moving(key, part):
    key_move = jax.random.fold_in(key, 21)
    shuffled = jax.vmap(lambda one_key: jax.random.permutation(one_key, BLK_DEV))(jax.random.split(key_move, TILES))
    chosen = shuffled[:, :MOVE_DEV]
    chosen = chosen.at[0].set(BLK_DEV - 1 - jnp.arange(MOVE_DEV)).at[1].set(jnp.arange(MOVE_DEV))
    return chosen.astype(jnp.int32)


def block_scale(rng, shape, shards, low, high):
    def one(dim, parts):
        heights = jax.random.uniform(jax.random.fold_in(jax.random.fold_in(rng, 6), dim), (parts,), jnp.float32, low / len(shards), high / len(shards))
        return jnp.repeat(jnp.exp(heights), shape[dim] // parts).reshape((-1,) + (1,) * (len(shape) - dim - 1))

    loudness = one(*shards[0])
    for cut in shards[1:]:
        loudness = loudness * one(*cut)
    return loudness


def normal_values(stream_key, shape, spread, reach, cuts=(), dtype=jnp.bfloat16):
    drawn = jax.random.normal(stream_key, shape, jnp.float32) * spread
    if len(cuts) > 0:
        drawn = block_scale(stream_key, shape, cuts, -0.22, 0.18) * drawn
    return jnp.clip(drawn, min=-reach, max=reach).astype(dtype)


def setup_inputs(seed: int = 0) -> dict:
    seeds = jax.random.split(jax.random.key(seed), 8)
    params = draw_params(jax.random.fold_in(seeds[7], 71), 0)
    first_moment = normal_values(seeds[1], (BLOCKS, NPARAM, G), 0.001, 0.006, ((0, 32),), jnp.float32)
    second_moment = jnp.clip(jnp.exp(math.log(1.9999999494757503e-05) - 9.9034876 * jax.random.uniform(seeds[2], (BLOCKS, NPARAM, G), jnp.float32) ** block_scale(seeds[2], (BLOCKS, NPARAM, G), ((0, 32),), -0.2, 0.2)), 9.999999717180685e-10, 1.9999999494757503e-05)
    view_basis = normal_values(seeds[3], (SH,), SH ** -0.5, 1.5, (), jnp.float32)
    target = jnp.clip(1.0 * jax.random.uniform(seeds[4], (TILES, 3, PIX), jnp.float32) ** block_scale(seeds[4], (TILES, 3, PIX), ((0, 32),), -0.2, 0.2), 0.0, 1.0)
    tile_blocks = draw_tile_blocks(jax.random.fold_in(seeds[7], 71), 0)
    moving = draw_moving(jax.random.fold_in(seeds[7], 71), 0)
    return {"params": params, "first_moment": first_moment, "second_moment": second_moment, "view_basis": view_basis, "target": target, "tile_blocks": tile_blocks, "moving": moving}


beta_one = 0.9
beta_two = 0.999
adam_eps = 1e-08
adam_step = 10.0

def step_rates():
    return jnp.concatenate([jnp.full((3,), 0.002, jnp.float32), jnp.full((3,), 0.005, jnp.float32), jnp.full((4,), 0.001, jnp.float32), jnp.full((1,), 0.05, jnp.float32), jnp.full((3 * SH,), 0.0025, jnp.float32)])

def project(values, view_basis):
    side = float(TILE_SIDE)
    mean_x = 0.5 * side + 0.375 * side * jnp.tanh(values[..., 0, :])
    mean_y = 0.5 * side + 0.375 * side * jnp.tanh(values[..., 1, :])
    zoom_factor = 3.0 / (1.0 + jax.nn.softplus(values[..., 2, :]))
    extent = side / 32.0 * 1.5 * jnp.exp(jnp.tanh(values[..., 3:6, :]))
    extent_sq = extent * extent
    rotation = values[..., 6:10, :]
    rot_norm = jnp.sqrt(lax.optimization_barrier(jnp.sum(rotation * rotation, axis=-2, keepdims=True)))
    rotation = rotation / jnp.maximum(rot_norm, 1.0)
    quat_w = rotation[..., 0, :]
    quat_x = rotation[..., 1, :]
    quat_y = rotation[..., 2, :]
    quat_z = rotation[..., 3, :]
    upper_row = [1.0 - 2.0 * (quat_y * quat_y + quat_z * quat_z), 2.0 * (quat_x * quat_y - quat_w * quat_z), 2.0 * (quat_x * quat_z + quat_w * quat_y)]
    lower_row = [2.0 * (quat_x * quat_y + quat_w * quat_z), 1.0 - 2.0 * (quat_x * quat_x + quat_z * quat_z), 2.0 * (quat_y * quat_z - quat_w * quat_x)]
    zoom_sq = zoom_factor * zoom_factor
    cov_xx = zoom_sq * (upper_row[0] * upper_row[0] * extent_sq[..., 0, :] + upper_row[1] * upper_row[1] * extent_sq[..., 1, :] + upper_row[2] * upper_row[2] * extent_sq[..., 2, :]) + 0.3
    cov_yy = zoom_sq * (lower_row[0] * lower_row[0] * extent_sq[..., 0, :] + lower_row[1] * lower_row[1] * extent_sq[..., 1, :] + lower_row[2] * lower_row[2] * extent_sq[..., 2, :]) + 0.3
    cov_xy = zoom_sq * (upper_row[0] * lower_row[0] * extent_sq[..., 0, :] + upper_row[1] * lower_row[1] * extent_sq[..., 1, :] + upper_row[2] * lower_row[2] * extent_sq[..., 2, :])
    determinant = cov_xx * cov_yy - cov_xy * cov_xy
    opacity = 0.99 * jax.nn.sigmoid(values[..., 10, :] - 4.0)
    harmonics = values[..., 11:, :].reshape(values.shape[:-2] + (3, SH, values.shape[-1]))
    colours = jax.nn.sigmoid(jnp.einsum('...ckg,k->...cg', harmonics, view_basis, precision=lax.Precision.HIGHEST))
    return jnp.stack([mean_x, mean_y, cov_yy / determinant, -cov_xy / determinant, cov_xx / determinant, opacity, colours[..., 0, :], colours[..., 1, :], colours[..., 2, :]], axis=-2)

def render(splat_list):
    flattened = jnp.transpose(splat_list, (1, 0, 2)).reshape(NPROJ, -1)
    pixels = jnp.arange(PIX)
    centre_x = (pixels % TILE_SIDE).astype(jnp.float32) + 0.5
    centre_y = (pixels // TILE_SIDE).astype(jnp.float32) + 0.5
    offset_x = centre_x[:, None] - flattened[0][None, :]
    offset_y = centre_y[:, None] - flattened[1][None, :]
    exponent = -0.5 * (flattened[2] * offset_x * offset_x + 2.0 * flattened[3] * offset_x * offset_y + flattened[4] * offset_y * offset_y)
    alphas = flattened[5] * jnp.exp(exponent)
    log_keep = jnp.log1p(-alphas)
    log_trans = jnp.cumsum(log_keep, axis=1) - log_keep
    weight = alphas * jnp.exp(log_trans)
    return jnp.dot(weight, flattened[6:9].T, precision=lax.Precision.HIGHEST).T

def handoff(values, moving):
    by_device = values.reshape(TILES, BLK_DEV, NPARAM, G)
    leaving = jnp.take_along_axis(by_device, moving[:, :, None, None], axis=1)
    arrived = jnp.roll(leaving.reshape(N_REGION, N_TILE, MOVE_DEV, NPARAM, G), 1, axis=0).reshape(TILES, MOVE_DEV, NPARAM, G)
    row_index = jnp.arange(TILES)[:, None]
    return by_device.at[row_index, moving].set(arrived).reshape(BLOCKS, NPARAM, G)

def reference(params, first_moment, second_moment, view_basis, target, tile_blocks, moving):
    projected = project(params, view_basis)
    region_of = jnp.arange(TILES) // N_TILE
    global_ids = (tile_blocks + (region_of * (N_TILE * BLK_DEV))[:, None]).astype(jnp.int32)

    def per_tile(inputs):
        listed, wanted = inputs
        splat_list = jnp.take(projected, listed, axis=0)
        picture, pullback = jax.vjp(render, splat_list)
        splat_grads = pullback(2.0 * (picture - wanted))[0]
        return (picture, splat_grads)
    images, splat_grads = lax.map(per_tile, (global_ids, target))
    proj_grads = jnp.zeros_like(projected).at[global_ids.reshape(-1)].add(splat_grads.reshape(-1, NPROJ, G))
    _, pullback = jax.vjp(lambda values: project(values, view_basis), params)
    gradient = pullback(proj_grads)[0]
    rates = step_rates()[:, None]
    moment_one = beta_one * first_moment + (1.0 - beta_one) * gradient
    moment_two = beta_two * second_moment + (1.0 - beta_two) * gradient * gradient
    stepped = params - rates * (moment_one / (1.0 - beta_one ** adam_step)) / (jnp.sqrt(moment_two / (1.0 - beta_two ** adam_step)) + adam_eps)
    return (handoff(stepped, moving), handoff(moment_one, moving), handoff(moment_two, moving), images)
```

```python
import functools
import math
import jax
import jax.numpy as jnp
import numpy as np
from jax import lax
from jax.experimental import pallas as pl
from jax.experimental.pallas import tpu as pltpu
from jax.sharding import PartitionSpec as P

SH = 16
TILE_SIDE = 32
NPROJ = 9
GRADS = 16
HALF = TILE_SIDE / 2.0

beta_one = 0.9
beta_two = 0.999
adam_eps = 1e-08
adam_step = 10.0
LOG2E = math.log2(math.e)


def rate_of(row):
    if row < 3:
        return 0.002
    if row < 6:
        return 0.005
    if row < 10:
        return 0.001
    if row < 11:
        return 0.05
    return 0.0025


def sigmoid(x):
    return 1.0 / (1.0 + jnp.exp(-x))


def geometry(p):
    v = {}
    v["tx"] = jnp.tanh(p(0))
    v["ty"] = jnp.tanh(p(1))
    depth = p(2)
    softplus = jnp.maximum(depth, 0.0) + jnp.log(1.0 + jnp.exp(-jnp.abs(depth)))
    v["f"] = 3.0 / (1.0 + softplus)
    v["z"] = v["f"] * v["f"]
    v["ts"] = [jnp.tanh(p(3 + k)) for k in range(3)]
    v["e"] = [2.25 * jnp.exp(2.0 * t) for t in v["ts"]]
    q = [p(6 + k) for k in range(4)]
    norm = jnp.sqrt((q[0] * q[0] + q[1] * q[1]) + (q[2] * q[2] + q[3] * q[3]))
    inv = 1.0 / jnp.maximum(norm, 1.0)
    v["norm"] = norm
    v["inv"] = inv
    w, x, y, z = [a * inv for a in q]
    v["q"] = (w, x, y, z)
    U = [1.0 - 2.0 * (y * y + z * z), 2.0 * (x * y - w * z), 2.0 * (x * z + w * y)]
    L = [2.0 * (x * y + w * z), 1.0 - 2.0 * (x * x + z * z), 2.0 * (y * z - w * x)]
    v["U"], v["L"] = U, L
    e = v["e"]
    v["sxx"] = U[0] * U[0] * e[0] + U[1] * U[1] * e[1] + U[2] * U[2] * e[2]
    v["syy"] = L[0] * L[0] * e[0] + L[1] * L[1] * e[1] + L[2] * L[2] * e[2]
    v["sxy"] = U[0] * L[0] * e[0] + U[1] * L[1] * e[1] + U[2] * L[2] * e[2]
    v["xx"] = v["z"] * v["sxx"] + 0.3
    v["yy"] = v["z"] * v["syy"] + 0.3
    v["xy"] = v["z"] * v["sxy"]
    v["idet"] = 1.0 / (v["xx"] * v["yy"] - v["xy"] * v["xy"])
    v["A"] = v["yy"] * v["idet"]
    v["B"] = -v["xy"] * v["idet"]
    v["C"] = v["xx"] * v["idet"]
    v["so"] = sigmoid(p(10) - 4.0)
    return v


def colour(p, c, basis):
    total = p(11 + SH * c) * basis(0)
    for k in range(1, SH):
        total = total + p(11 + SH * c + k) * basis(k)
    return sigmoid(total)


def project_kernel(moving_ref, basis_ref, p_ref, f_ref, s_ref, proj_ref, leave_ref):
    rows, blocks, lanes = p_ref.shape
    moves = leave_ref.shape[1]
    p = lambda i: p_ref[i]
    v = geometry(p)
    proj_ref[0] = 0.375 * TILE_SIDE * v["tx"]
    proj_ref[1] = 0.375 * TILE_SIDE * v["ty"]
    proj_ref[2] = v["A"]
    proj_ref[3] = v["B"]
    proj_ref[4] = v["C"]
    proj_ref[5] = 0.99 * v["so"]
    for c in range(3):
        proj_ref[6 + c] = colour(p, c, lambda k: basis_ref[k])
    slot = lax.broadcasted_iota(jnp.int32, (blocks, lanes), 0)
    pick = jnp.zeros((blocks, lanes), jnp.int32)
    for m in range(moves):
        pick = jnp.where(slot == m, moving_ref[0, m], pick)
    for a, ref in enumerate((p_ref, f_ref, s_ref)):
        for i in range(rows):
            leave_ref[a * rows + i] = jnp.take_along_axis(ref[i], pick, axis=0)[:moves]


def composite_kernel(meta_ref, *refs):
    peers = meta_ref.shape[0] // 2
    sources = refs[:peers]
    target_ref = refs[peers]
    image_ref = refs[peers + 1]
    grad_refs = refs[peers + 2 : 2 * peers + 2]
    pbuf, abuf, wbuf, ebuf, colq, errbuf, gbuf = refs[2 * peers + 2 :]
    lanes = pbuf.shape[2]
    width = colq.shape[1]
    chunks = abuf.shape[0] // width
    for d in range(peers):
        pos = meta_ref[d]
        loc = meta_ref[peers + d]
        for r in range(NPROJ):
            pbuf[pos, pl.ds(r, 1), :] = sources[d][r, pl.ds(loc, 1), :]

    lane = lax.broadcasted_iota(jnp.int32, (8, lanes), 1)
    px = (lane % TILE_SIDE).astype(jnp.float32) + (0.5 - HALF)
    py = (lane // TILE_SIDE).astype(jnp.float32) + (0.5 - HALF)
    step = float(lanes // TILE_SIDE)

    def alphas(j, _):
        block = pbuf[j]
        scale = jnp.concatenate(
            [
                jnp.full((2, lanes), 1.0, jnp.float32),
                jnp.full((1, lanes), -0.5 * LOG2E, jnp.float32),
                jnp.full((1, lanes), -LOG2E, jnp.float32),
                jnp.full((1, lanes), -0.5 * LOG2E, jnp.float32),
                jnp.full((11, lanes), 1.0, jnp.float32),
            ],
            axis=0,
        )
        columns = (block * scale).T
        for u in range(lanes // 8):
            part = columns[u * 8 : (u + 1) * 8]
            wide = lambda k: jnp.broadcast_to(part[:, k : k + 1], (8, lanes))
            row = pl.multiple_of(j * lanes + u * 8, 8)
            dx = px - wide(0)
            ax = wide(2) * dx * dx
            bx = wide(3) * dx
            dy0 = py - wide(1)
            conic = wide(4)
            opacity = wide(5)
            for k in range(3):
                colq[k, pl.ds(row, 8), :] = wide(6 + k)
            for c in range(chunks):
                dy = dy0 + step * c
                power = (conic * dy + bx) * dy + ax
                abuf[pl.ds(c * width + row, 8), :] = opacity * jnp.exp2(power)
        return 0

    lax.fori_loop(0, width // lanes, alphas, 0)

    unroll = 8

    def forward(i, running):
        trans, image = running
        for u in range(unroll):
            g = i * unroll + u
            alpha = abuf[pl.ds(g, chunks, stride=width), :]
            weight = trans * alpha
            trans = trans * (1.0 - alpha)
            wbuf[pl.ds(g, chunks, stride=width), :] = weight
            image = tuple(
                image[k] + weight * jnp.broadcast_to(colq[k, pl.ds(g, 1), :], (chunks, lanes)) for k in range(3)
            )
        return (trans, image)

    zero = jnp.zeros((chunks, lanes), jnp.float32)
    _, image = lax.fori_loop(0, width // unroll, forward, (zero + 1.0, (zero, zero, zero)))
    errors = []
    errbuf[...] = jnp.zeros_like(errbuf)
    for k in range(3):
        image_ref[k] = image[k]
        errors.append(2.0 * (image[k] - target_ref[k]))
        errbuf[k * chunks : (k + 1) * chunks, :] = errors[k]

    def backward(i, behind):
        for u in range(unroll):
            g = width - 1 - (i * unroll + u)
            shade = [errors[k] * jnp.broadcast_to(colq[k, pl.ds(g, 1), :], (chunks, lanes)) for k in range(3)]
            alpha = abuf[pl.ds(g, chunks, stride=width), :]
            weight = wbuf[pl.ds(g, chunks, stride=width), :]
            ahead = (shade[0] + shade[1]) + shade[2] - behind
            behind = behind + alpha * ahead
            ebuf[pl.ds(g, chunks, stride=width), :] = weight * ahead
        return behind

    lax.fori_loop(0, width // unroll, backward, zero)

    which = lax.broadcasted_iota(jnp.int32, (8, lanes), 0)
    dot = functools.partial(
        lax.dot_general,
        dimension_numbers=(((1,), (1,)), ((), ())),
        precision=lax.Precision.HIGHEST,
        preferred_element_type=jnp.float32,
    )
    moments = jnp.zeros((8, width), jnp.float32)
    shades = jnp.zeros((8, width), jnp.float32)
    for c in range(chunks):
        y = py + step * c
        basis = jnp.where(which == 0, 1.0, 0.0)
        for r, value in enumerate((px, y, px * px, px * y, y * y)):
            basis = jnp.where(which == r + 1, value, basis)
        moments = moments + dot(basis, ebuf[c * width : (c + 1) * width, :])
        shades = shades + dot(errbuf[pl.ds(c, 8, stride=chunks), :], wbuf[c * width : (c + 1) * width, :])
    for j in range(width // lanes):
        part = moments[:, j * lanes : (j + 1) * lanes]
        m0, m1x, m1y, mxx, mxy, myy = [part[r : r + 1] for r in range(6)]
        mx, my, ca, cb, cc, op = [pbuf[j, r : r + 1, :] for r in range(6)]
        sx = m1x - mx * m0
        sy = m1y - my * m0
        sxx = mxx - mx * m1x - mx * sx
        sxy = mxy - mx * m1y - my * sx
        syy = myy - my * m1y - my * sy
        gbuf[j, 0:1, :] = ca * sx + cb * sy
        gbuf[j, 1:2, :] = cb * sx + cc * sy
        gbuf[j, 2:3, :] = -0.5 * sxx
        gbuf[j, 3:4, :] = -sxy
        gbuf[j, 4:5, :] = -0.5 * syy
        gbuf[j, 5:6, :] = m0 / op
        gbuf[j, 6:9, :] = shades[0:3, j * lanes : (j + 1) * lanes]
        gbuf[j, 9:16, :] = jnp.zeros((7, lanes), jnp.float32)
    for d in range(peers):
        grad_refs[d][...] = gbuf[meta_ref[d]]
        grad_refs[d][NPROJ : NPROJ + 1, :] = jnp.full((1, lanes), 1, jnp.float32) * meta_ref[peers + d].astype(jnp.float32)


def owner_kernel(moving_ref, *refs):
    sources = refs[:-2]
    dense_ref, leave_ref = refs[-2:]
    _, blocks, lanes = dense_ref.shape
    moves = leave_ref.shape[1]
    slot = lax.broadcasted_iota(jnp.int32, (blocks, lanes), 0)
    slots = slot.astype(jnp.float32)
    pick = jnp.zeros((blocks, lanes), jnp.int32)
    for m in range(moves):
        pick = jnp.where(slot == m, moving_ref[0, m], pick)
    masks = [slots == jnp.broadcast_to(ref[NPROJ : NPROJ + 1, :], (blocks, lanes)) for ref in sources]
    for r in range(NPROJ):
        total = jnp.zeros((blocks, lanes), jnp.float32)
        for mask, ref in zip(masks, sources):
            total = total + jnp.where(mask, jnp.broadcast_to(ref[r : r + 1, :], (blocks, lanes)), 0.0)
        dense_ref[r] = total
        leave_ref[r] = jnp.take_along_axis(total, pick, axis=0)[:moves]


def update_kernel(moving_ref, basis_ref, p_ref, f_ref, s_ref, came_ref, dense_ref, carried_ref, np_ref, nf_ref, ns_ref, ubuf, kbuf):
    rows, blocks, lanes = p_ref.shape
    moves = came_ref.shape[1]
    slot = lax.broadcasted_iota(jnp.int32, (blocks, lanes), 0)
    pick = jnp.zeros((blocks, lanes), jnp.int32)
    taken = jnp.zeros((blocks, lanes), jnp.bool_)
    for m in range(moves):
        here = slot == moving_ref[0, m]
        pick = jnp.where(here, m, pick)
        taken = jnp.logical_or(taken, here)

    def mixed(own, arrived, k):
        kbuf[k, 0:moves, :] = arrived
        return jnp.where(taken, jnp.take_along_axis(kbuf[k], pick, axis=0), own)

    for i in range(rows):
        ubuf[i] = mixed(p_ref[i], came_ref[i], i % 8)
    grads = [mixed(dense_ref[r], carried_ref[r], r % 8) for r in range(NPROJ)]
    p = lambda i: ubuf[i]

    def store(i, grad):
        first = mixed(f_ref[i], came_ref[rows + i], i % 8)
        second = mixed(s_ref[i], came_ref[2 * rows + i], (i + 4) % 8)
        one = beta_one * first + (1.0 - beta_one) * grad
        two = beta_two * second + (1.0 - beta_two) * grad * grad
        nf_ref[i] = one
        ns_ref[i] = two
        scaled = (rate_of(i) / (1.0 - beta_one**adam_step)) * one
        np_ref[i] = p(i) - scaled / (jnp.sqrt(two * (1.0 / (1.0 - beta_two**adam_step))) + adam_eps)

    v = geometry(p)
    gmx, gmy, ga, gb, gc, gop = grads[:6]
    store(0, gmx * (0.375 * TILE_SIDE) * (1.0 - v["tx"] * v["tx"]))
    store(1, gmy * (0.375 * TILE_SIDE) * (1.0 - v["ty"] * v["ty"]))
    gdet = -(ga * v["A"] + gb * v["B"] + gc * v["C"]) * v["idet"]
    gxx = gc * v["idet"] + gdet * v["yy"]
    gyy = ga * v["idet"] + gdet * v["xx"]
    gxy = -gb * v["idet"] - 2.0 * gdet * v["xy"]
    gz = gxx * v["sxx"] + gyy * v["syy"] + gxy * v["sxy"]
    f = v["f"]
    store(2, gz * (-2.0 / 3.0) * f * f * f * sigmoid(p(2)))
    U, L, e = v["U"], v["L"], v["e"]
    gU, gL = [], []
    for k in range(3):
        ge = v["z"] * (gxx * U[k] * U[k] + gyy * L[k] * L[k] + gxy * U[k] * L[k])
        t = v["ts"][k]
        store(3 + k, 2.0 * ge * e[k] * (1.0 - t * t))
        ze = v["z"] * e[k]
        gU.append(ze * (2.0 * gxx * U[k] + gxy * L[k]))
        gL.append(ze * (2.0 * gyy * L[k] + gxy * U[k]))
    w, x, y, z = v["q"]
    gq = [
        2.0 * (z * (gL[0] - gU[1]) + y * gU[2] - x * gL[2]),
        2.0 * (y * (gU[1] + gL[0]) + z * gU[2] - 2.0 * x * gL[1] - w * gL[2]),
        2.0 * (x * (gU[1] + gL[0]) - 2.0 * y * gU[0] + w * gU[2] + z * gL[2]),
        2.0 * (w * (gL[0] - gU[1]) - 2.0 * z * (gU[0] + gL[1]) + x * gU[2] + y * gL[2]),
    ]
    share = jnp.where(v["norm"] > 1.0, 1.0, jnp.where(v["norm"] == 1.0, 0.5, 0.0))
    along = share * (w * gq[0] + x * gq[1] + y * gq[2] + z * gq[3])
    for k, unit in enumerate((w, x, y, z)):
        store(6 + k, (gq[k] - unit * along) * v["inv"])
    store(10, gop * 0.99 * v["so"] * (1.0 - v["so"]))
    for c in range(3):
        shade = colour(p, c, lambda k: basis_ref[k])
        logit = grads[6 + c] * shade * (1.0 - shade)
        for k in range(SH):
            store(11 + SH * c + k, logit * basis_ref[k])


def on_device(params, first_moment, second_moment, view_basis, target, tile_blocks, moving):
    blocks, rows, lanes = params.shape
    peers = lax.axis_size("tile")
    listed = tile_blocks.shape[1]
    moves = moving.shape[1]
    pixels = target.shape[2]
    chunks = pixels // lanes
    width = listed * lanes
    f32 = jnp.float32
    smem = pl.BlockSpec(memory_space=pltpu.SMEM)
    vmem = pl.BlockSpec(memory_space=pltpu.VMEM)
    sds = jax.ShapeDtypeStruct

    me = lax.axis_index("tile")
    partner = jnp.bitwise_xor(me, jnp.arange(peers, dtype=jnp.int32))
    matches = (tile_blocks[0][None, :] // blocks) == partner[:, None]
    pos = jnp.sum(jnp.where(matches, jnp.arange(listed, dtype=jnp.int32)[None, :], 0), axis=1)
    loc = jnp.sum(jnp.where(matches, (tile_blocks[0] % blocks)[None, :], 0), axis=1)
    meta = jnp.concatenate([pos, loc]).astype(jnp.int32)

    turned = [jnp.transpose(a, (1, 0, 2)) for a in (params, first_moment, second_moment)]
    projected, leaving = pl.pallas_call(
        project_kernel,
        out_shape=(sds((NPROJ, blocks, lanes), f32), sds((3 * rows, moves, lanes), f32)),
        in_specs=[smem, smem, vmem, vmem, vmem],
        out_specs=(vmem, vmem),
        name="project",
    )(moving, view_basis, *turned)

    def swapped(value, d):
        return lax.ppermute(value, "tile", [(i, i ^ d) for i in range(peers)])

    regions = lax.axis_size("region")
    onward = lambda value: lax.ppermute(value, "region", [(i, (i + 1) % regions) for i in range(regions)])

    sources = [projected] + [swapped(projected, d) for d in range(1, peers)]
    came = onward(leaving)
    image, *splat_grads = pl.pallas_call(
        composite_kernel,
        out_shape=(sds((3, chunks, lanes), f32),) + (sds((GRADS, lanes), f32),) * peers,
        in_specs=[smem] + [vmem] * (peers + 1),
        out_specs=(vmem,) * (peers + 1),
        scratch_shapes=[
            pltpu.VMEM((listed, GRADS, lanes), f32),
            pltpu.VMEM((chunks * width, lanes), f32),
            pltpu.VMEM((chunks * width, lanes), f32),
            pltpu.VMEM((chunks * width, lanes), f32),
            pltpu.VMEM((3, width, lanes), f32),
            pltpu.VMEM((8 * chunks, lanes), f32),
            pltpu.VMEM((listed, GRADS, lanes), f32),
        ],
        compiler_params=pltpu.CompilerParams(vmem_limit_bytes=(3 * chunks + 3) * width * lanes * 4 + (8 << 20)),
        name="composite",
    )(meta, *sources, target.reshape(3, chunks, lanes))
    arrived = [splat_grads[0]] + [swapped(splat_grads[d], d) for d in range(1, peers)]
    dense, outgoing = pl.pallas_call(
        owner_kernel,
        out_shape=(sds((NPROJ, blocks, lanes), f32), sds((NPROJ, moves, lanes), f32)),
        in_specs=[smem] + [vmem] * peers,
        out_specs=(vmem, vmem),
        name="owner",
    )(moving, *arrived)
    carried = onward(outgoing)
    updated = pl.pallas_call(
        update_kernel,
        out_shape=(sds((rows, blocks, lanes), f32),) * 3,
        in_specs=[smem, smem] + [vmem] * 6,
        out_specs=(vmem,) * 3,
        scratch_shapes=[pltpu.VMEM((rows, blocks, lanes), f32), pltpu.VMEM((8, blocks, lanes), f32)],
        name="update",
    )(moving, view_basis, *turned, came, dense, carried)
    updated = [jnp.transpose(a, (1, 0, 2)) for a in updated]
    return (*updated, image.reshape(1, 3, pixels))


def solution(mesh):
    three = P(("region", "tile"), None, None)
    two = P(("region", "tile"), None)
    return jax.shard_map(
        on_device,
        mesh=mesh,
        in_specs=(three, three, three, P(), three, two, two),
        out_specs=(three, three, three, three),
        check_vma=False,
    )
```

```python
import functools
import math
import jax
import jax.numpy as jnp
import numpy as np
from jax import lax
from jax.experimental import pallas as pl
from jax.experimental.pallas import tpu as pltpu
from jax.sharding import PartitionSpec as P

SH = 16
TILE_SIDE = 32
NPROJ = 9
GRADS = 16
HALF = TILE_SIDE / 2.0

beta_one = 0.9
beta_two = 0.999
adam_eps = 1e-08
adam_step = 10.0
LOG2E = math.log2(math.e)


def rate_of(row):
    if row < 3:
        return 0.002
    if row < 6:
        return 0.005
    if row < 10:
        return 0.001
    if row < 11:
        return 0.05
    return 0.0025


def sigmoid(x):
    return 1.0 / (1.0 + jnp.exp(-x))


def geometry(p):
    v = {}
    v["tx"] = jnp.tanh(p(0))
    v["ty"] = jnp.tanh(p(1))
    depth = p(2)
    softplus = jnp.maximum(depth, 0.0) + jnp.log(1.0 + jnp.exp(-jnp.abs(depth)))
    v["f"] = 3.0 / (1.0 + softplus)
    v["z"] = v["f"] * v["f"]
    v["ts"] = [jnp.tanh(p(3 + k)) for k in range(3)]
    v["e"] = [2.25 * jnp.exp(2.0 * t) for t in v["ts"]]
    q = [p(6 + k) for k in range(4)]
    norm = jnp.sqrt((q[0] * q[0] + q[1] * q[1]) + (q[2] * q[2] + q[3] * q[3]))
    inv = 1.0 / jnp.maximum(norm, 1.0)
    v["norm"] = norm
    v["inv"] = inv
    w, x, y, z = [a * inv for a in q]
    v["q"] = (w, x, y, z)
    U = [1.0 - 2.0 * (y * y + z * z), 2.0 * (x * y - w * z), 2.0 * (x * z + w * y)]
    L = [2.0 * (x * y + w * z), 1.0 - 2.0 * (x * x + z * z), 2.0 * (y * z - w * x)]
    v["U"], v["L"] = U, L
    e = v["e"]
    v["sxx"] = U[0] * U[0] * e[0] + U[1] * U[1] * e[1] + U[2] * U[2] * e[2]
    v["syy"] = L[0] * L[0] * e[0] + L[1] * L[1] * e[1] + L[2] * L[2] * e[2]
    v["sxy"] = U[0] * L[0] * e[0] + U[1] * L[1] * e[1] + U[2] * L[2] * e[2]
    v["xx"] = v["z"] * v["sxx"] + 0.3
    v["yy"] = v["z"] * v["syy"] + 0.3
    v["xy"] = v["z"] * v["sxy"]
    v["idet"] = 1.0 / (v["xx"] * v["yy"] - v["xy"] * v["xy"])
    v["A"] = v["yy"] * v["idet"]
    v["B"] = -v["xy"] * v["idet"]
    v["C"] = v["xx"] * v["idet"]
    v["so"] = sigmoid(p(10) - 4.0)
    return v


def colour(p, c, basis):
    total = p(11 + SH * c) * basis(0)
    for k in range(1, SH):
        total = total + p(11 + SH * c + k) * basis(k)
    return sigmoid(total)


def project_kernel(moving_ref, basis_ref, p_ref, f_ref, s_ref, proj_ref, leave_ref):
    rows, blocks, lanes = p_ref.shape
    moves = leave_ref.shape[1]
    p = lambda i: p_ref[i]
    v = geometry(p)
    proj_ref[0] = 0.375 * TILE_SIDE * v["tx"]
    proj_ref[1] = 0.375 * TILE_SIDE * v["ty"]
    proj_ref[2] = v["A"]
    proj_ref[3] = v["B"]
    proj_ref[4] = v["C"]
    proj_ref[5] = 0.99 * v["so"]
    for c in range(3):
        proj_ref[6 + c] = colour(p, c, lambda k: basis_ref[k])
    slot = lax.broadcasted_iota(jnp.int32, (blocks, lanes), 0)
    pick = jnp.zeros((blocks, lanes), jnp.int32)
    for m in range(moves):
        pick = jnp.where(slot == m, moving_ref[0, m], pick)
    for a, ref in enumerate((p_ref, f_ref, s_ref)):
        for i in range(rows):
            leave_ref[a * rows + i] = jnp.take_along_axis(ref[i], pick, axis=0)[:moves]


def composite_kernel(meta_ref, *refs):
    peers = meta_ref.shape[0] // 2
    sources = refs[:peers]
    target_ref = refs[peers]
    image_ref = refs[peers + 1]
    grad_refs = refs[peers + 2 : 2 * peers + 2]
    pbuf, abuf, wbuf, ebuf, colq, errbuf, gbuf, rbuf = refs[2 * peers + 2 :]
    lanes = pbuf.shape[2]
    width = colq.shape[1]
    chunks = abuf.shape[0] // width
    for d in range(peers):
        pos = meta_ref[d]
        loc = meta_ref[peers + d]
        for r in range(NPROJ):
            pbuf[pos, pl.ds(r, 1), :] = sources[d][r, pl.ds(loc, 1), :]

    lane = lax.broadcasted_iota(jnp.int32, (8, lanes), 1)
    px = (lane % TILE_SIDE).astype(jnp.float32) + (0.5 - HALF)
    py = (lane // TILE_SIDE).astype(jnp.float32) + (0.5 - HALF)
    step = float(lanes // TILE_SIDE)

    def alphas(j, _):
        block = pbuf[j]
        scale = jnp.concatenate(
            [
                jnp.full((2, lanes), 1.0, jnp.float32),
                jnp.full((1, lanes), -0.5 * LOG2E, jnp.float32),
                jnp.full((1, lanes), -LOG2E, jnp.float32),
                jnp.full((1, lanes), -0.5 * LOG2E, jnp.float32),
                jnp.full((11, lanes), 1.0, jnp.float32),
            ],
            axis=0,
        )
        columns = (block * scale).T
        for u in range(lanes // 8):
            part = columns[u * 8 : (u + 1) * 8]
            wide = lambda k: jnp.broadcast_to(part[:, k : k + 1], (8, lanes))
            row = pl.multiple_of(j * lanes + u * 8, 8)
            dx = px - wide(0)
            ax = wide(2) * dx * dx
            bx = wide(3) * dx
            dy0 = py - wide(1)
            conic = wide(4)
            opacity = wide(5)
            for k in range(3):
                colq[k, pl.ds(row, 8), :] = wide(6 + k)
            for c in range(chunks):
                dy = dy0 + step * c
                power = (conic * dy + bx) * dy + ax
                abuf[pl.ds(row * chunks + c * 8, 8), :] = opacity * jnp.exp2(power)
        return 0

    lax.fori_loop(0, width // lanes, alphas, 0)

    def forward(i, running):
        trans, image = running
        base = pl.multiple_of(i * (8 * chunks), 8 * chunks)
        for u in range(8):
            g = i * 8 + u
            alpha = abuf[pl.ds(base + u, chunks, stride=8), :]
            weight = trans * alpha
            trans = trans * (1.0 - alpha)
            wbuf[pl.ds(base + u * chunks, chunks), :] = weight
            image = tuple(
                image[k] + weight * jnp.broadcast_to(colq[k, pl.ds(g, 1), :], (chunks, lanes)) for k in range(3)
            )
        return (trans, image)

    zero = jnp.zeros((chunks, lanes), jnp.float32)
    _, image = lax.fori_loop(0, width // 8, forward, (zero + 1.0, (zero, zero, zero)))
    errors = []
    errbuf[...] = jnp.zeros_like(errbuf)
    for k in range(3):
        image_ref[k] = image[k]
        errors.append(2.0 * (image[k] - target_ref[k]))
        errbuf[k * chunks : (k + 1) * chunks, :] = errors[k]

    def backward(i, behind):
        group = width // 8 - 1 - i
        base = pl.multiple_of(group * (8 * chunks), 8 * chunks)
        for u in reversed(range(8)):
            g = group * 8 + u
            shade = [errors[k] * jnp.broadcast_to(colq[k, pl.ds(g, 1), :], (chunks, lanes)) for k in range(3)]
            alpha = abuf[pl.ds(base + u, chunks, stride=8), :]
            weight = wbuf[pl.ds(base + u * chunks, chunks), :]
            ahead = (shade[0] + shade[1]) + shade[2] - behind
            behind = behind + alpha * ahead
            ebuf[pl.ds(base + u * chunks, chunks), :] = weight * ahead
        return behind

    lax.fori_loop(0, width // 8, backward, zero)

    half = chunks // 2

    def reduce_pixels(u, _):
        row = pl.multiple_of(u * 8, 8)
        part = [ebuf[pl.ds(row * chunks + c, 8, stride=chunks), :] for c in range(chunks)]
        even = [part[c] + part[chunks - 1 - c] for c in range(half)]
        odd = [part[chunks - 1 - c] - part[c] for c in range(half)]
        centre = (chunks - 1) / 2.0
        sums = [
            sum(even[1:], even[0]),
            sum([(centre - c) * odd[c] for c in range(1, half)], centre * odd[0]),
            sum([(centre - c) ** 2 * even[c] for c in range(1, half)], centre**2 * even[0]),
        ]
        part = [wbuf[pl.ds(row * chunks + c, 8, stride=chunks), :] for c in range(chunks)]
        for k in range(3):
            lit = [part[c] * jnp.broadcast_to(errbuf[pl.ds(k * chunks + c, 1), :], (8, lanes)) for c in range(chunks)]
            sums.append(((lit[0] + lit[1]) + (lit[2] + lit[3])) + ((lit[4] + lit[5]) + (lit[6] + lit[7])))
        for i, value in enumerate(sums):
            rbuf[pl.ds(row, 8), i * lanes : (i + 1) * lanes] = value
        return 0

    lax.fori_loop(0, width // 8, reduce_pixels, 0)

    which = lax.broadcasted_iota(jnp.int32, (GRADS, lanes), 0)
    lane = lax.broadcasted_iota(jnp.int32, (GRADS, lanes), 1)
    bx = (lane % TILE_SIDE).astype(jnp.float32) + (0.5 - HALF)
    by = (lane // TILE_SIDE).astype(jnp.float32) + (0.5 - step / 2.0)
    one = jnp.ones_like(bx)

    def table(**entries):
        out = jnp.zeros_like(bx)
        for name, value in entries.items():
            out = jnp.where(which == int(name[1:]), value, out)
        return out

    basis = jnp.concatenate(
        [
            table(r0=one, r1=bx, r2=by, r3=(bx * bx - 0.25) * 0.5, r4=bx * by, r5=by * by),
            table(r2=step * one, r4=step * bx, r5=2.0 * step * by),
            table(r5=step * step * one),
            table(r6=one),
            table(r7=one),
            table(r8=one),
        ],
        axis=1,
    ).astype(jnp.bfloat16)
    whole = rbuf[...]
    totals = jnp.zeros((width, GRADS), jnp.float32)
    for _ in range(3):
        piece = whole.astype(jnp.bfloat16)
        whole = whole - piece.astype(jnp.float32)
        totals = totals + lax.dot_general(
            piece, basis, (((1,), (1,)), ((), ())), preferred_element_type=jnp.float32
        )
    for j in range(width // lanes):
        part = totals[j * lanes : (j + 1) * lanes].T
        m0, m1x, m1y, mxx, mxy, myy = [part[r : r + 1] for r in range(6)]
        mxx = 2.0 * mxx + 0.25 * m0
        mx, my, ca, cb, cc, op = [pbuf[j, r : r + 1, :] for r in range(6)]
        sx = m1x - mx * m0
        sy = m1y - my * m0
        sxx = mxx - mx * m1x - mx * sx
        sxy = mxy - mx * m1y - my * sx
        syy = myy - my * m1y - my * sy
        gbuf[j, 0:1, :] = ca * sx + cb * sy
        gbuf[j, 1:2, :] = cb * sx + cc * sy
        gbuf[j, 2:3, :] = -0.5 * sxx
        gbuf[j, 3:4, :] = -sxy
        gbuf[j, 4:5, :] = -0.5 * syy
        gbuf[j, 5:6, :] = m0 / op
        gbuf[j, 6:9, :] = part[6:9]
        gbuf[j, 9:16, :] = jnp.zeros((7, lanes), jnp.float32)
    for d in range(peers):
        grad_refs[d][...] = gbuf[meta_ref[d]]
        grad_refs[d][NPROJ : NPROJ + 1, :] = jnp.full((1, lanes), 1, jnp.float32) * meta_ref[peers + d].astype(jnp.float32)


def owner_kernel(moving_ref, *refs):
    sources = refs[:-2]
    dense_ref, leave_ref = refs[-2:]
    _, blocks, lanes = dense_ref.shape
    moves = leave_ref.shape[1]
    slot = lax.broadcasted_iota(jnp.int32, (blocks, lanes), 0)
    slots = slot.astype(jnp.float32)
    pick = jnp.zeros((blocks, lanes), jnp.int32)
    for m in range(moves):
        pick = jnp.where(slot == m, moving_ref[0, m], pick)
    masks = [slots == jnp.broadcast_to(ref[NPROJ : NPROJ + 1, :], (blocks, lanes)) for ref in sources]
    for r in range(NPROJ):
        total = jnp.zeros((blocks, lanes), jnp.float32)
        for mask, ref in zip(masks, sources):
            total = total + jnp.where(mask, jnp.broadcast_to(ref[r : r + 1, :], (blocks, lanes)), 0.0)
        dense_ref[r] = total
        leave_ref[r] = jnp.take_along_axis(total, pick, axis=0)[:moves]


def update_kernel(moving_ref, basis_ref, p_ref, f_ref, s_ref, came_ref, dense_ref, carried_ref, np_ref, nf_ref, ns_ref, ubuf, kbuf):
    rows, blocks, lanes = p_ref.shape
    moves = came_ref.shape[1]
    slot = lax.broadcasted_iota(jnp.int32, (blocks, lanes), 0)
    pick = jnp.zeros((blocks, lanes), jnp.int32)
    taken = jnp.zeros((blocks, lanes), jnp.bool_)
    for m in range(moves):
        here = slot == moving_ref[0, m]
        pick = jnp.where(here, m, pick)
        taken = jnp.logical_or(taken, here)

    def mixed(own, arrived, k):
        kbuf[k, 0:moves, :] = arrived
        return jnp.where(taken, jnp.take_along_axis(kbuf[k], pick, axis=0), own)

    for i in range(rows):
        ubuf[i] = mixed(p_ref[i], came_ref[i], i % 8)
    grads = [mixed(dense_ref[r], carried_ref[r], r % 8) for r in range(NPROJ)]
    p = lambda i: ubuf[i]

    def store(i, grad):
        first = mixed(f_ref[i], came_ref[rows + i], i % 8)
        second = mixed(s_ref[i], came_ref[2 * rows + i], (i + 4) % 8)
        one = beta_one * first + (1.0 - beta_one) * grad
        two = beta_two * second + (1.0 - beta_two) * grad * grad
        nf_ref[i] = one
        ns_ref[i] = two
        scaled = (rate_of(i) / (1.0 - beta_one**adam_step)) * one
        np_ref[i] = p(i) - scaled / (jnp.sqrt(two * (1.0 / (1.0 - beta_two**adam_step))) + adam_eps)

    v = geometry(p)
    gmx, gmy, ga, gb, gc, gop = grads[:6]
    store(0, gmx * (0.375 * TILE_SIDE) * (1.0 - v["tx"] * v["tx"]))
    store(1, gmy * (0.375 * TILE_SIDE) * (1.0 - v["ty"] * v["ty"]))
    gdet = -(ga * v["A"] + gb * v["B"] + gc * v["C"]) * v["idet"]
    gxx = gc * v["idet"] + gdet * v["yy"]
    gyy = ga * v["idet"] + gdet * v["xx"]
    gxy = -gb * v["idet"] - 2.0 * gdet * v["xy"]
    gz = gxx * v["sxx"] + gyy * v["syy"] + gxy * v["sxy"]
    f = v["f"]
    store(2, gz * (-2.0 / 3.0) * f * f * f * sigmoid(p(2)))
    U, L, e = v["U"], v["L"], v["e"]
    gU, gL = [], []
    for k in range(3):
        ge = v["z"] * (gxx * U[k] * U[k] + gyy * L[k] * L[k] + gxy * U[k] * L[k])
        t = v["ts"][k]
        store(3 + k, 2.0 * ge * e[k] * (1.0 - t * t))
        ze = v["z"] * e[k]
        gU.append(ze * (2.0 * gxx * U[k] + gxy * L[k]))
        gL.append(ze * (2.0 * gyy * L[k] + gxy * U[k]))
    w, x, y, z = v["q"]
    gq = [
        2.0 * (z * (gL[0] - gU[1]) + y * gU[2] - x * gL[2]),
        2.0 * (y * (gU[1] + gL[0]) + z * gU[2] - 2.0 * x * gL[1] - w * gL[2]),
        2.0 * (x * (gU[1] + gL[0]) - 2.0 * y * gU[0] + w * gU[2] + z * gL[2]),
        2.0 * (w * (gL[0] - gU[1]) - 2.0 * z * (gU[0] + gL[1]) + x * gU[2] + y * gL[2]),
    ]
    share = jnp.where(v["norm"] > 1.0, 1.0, jnp.where(v["norm"] == 1.0, 0.5, 0.0))
    along = share * (w * gq[0] + x * gq[1] + y * gq[2] + z * gq[3])
    for k, unit in enumerate((w, x, y, z)):
        store(6 + k, (gq[k] - unit * along) * v["inv"])
    store(10, gop * 0.99 * v["so"] * (1.0 - v["so"]))
    for c in range(3):
        shade = colour(p, c, lambda k: basis_ref[k])
        logit = grads[6 + c] * shade * (1.0 - shade)
        for k in range(SH):
            store(11 + SH * c + k, logit * basis_ref[k])


def on_device(params, first_moment, second_moment, view_basis, target, tile_blocks, moving):
    blocks, rows, lanes = params.shape
    peers = lax.axis_size("tile")
    listed = tile_blocks.shape[1]
    moves = moving.shape[1]
    pixels = target.shape[2]
    chunks = pixels // lanes
    width = listed * lanes
    f32 = jnp.float32
    smem = pl.BlockSpec(memory_space=pltpu.SMEM)
    vmem = pl.BlockSpec(memory_space=pltpu.VMEM)
    sds = jax.ShapeDtypeStruct

    me = lax.axis_index("tile")
    partner = jnp.bitwise_xor(me, jnp.arange(peers, dtype=jnp.int32))
    matches = (tile_blocks[0][None, :] // blocks) == partner[:, None]
    pos = jnp.sum(jnp.where(matches, jnp.arange(listed, dtype=jnp.int32)[None, :], 0), axis=1)
    loc = jnp.sum(jnp.where(matches, (tile_blocks[0] % blocks)[None, :], 0), axis=1)
    meta = jnp.concatenate([pos, loc]).astype(jnp.int32)

    turned = [jnp.transpose(a, (1, 0, 2)) for a in (params, first_moment, second_moment)]
    projected, leaving = pl.pallas_call(
        project_kernel,
        out_shape=(sds((NPROJ, blocks, lanes), f32), sds((3 * rows, moves, lanes), f32)),
        in_specs=[smem, smem, vmem, vmem, vmem],
        out_specs=(vmem, vmem),
        compiler_params=pltpu.CompilerParams(vmem_limit_bytes=4 << 20),
        name="project",
    )(moving, view_basis, *turned)

    def swapped(value, d):
        return lax.ppermute(value, "tile", [(i, i ^ d) for i in range(peers)])

    regions = lax.axis_size("region")
    onward = lambda value: lax.ppermute(value, "region", [(i, (i + 1) % regions) for i in range(regions)])

    sources = [projected] + [swapped(projected, d) for d in range(1, peers)]
    came = onward(leaving)
    image, *splat_grads = pl.pallas_call(
        composite_kernel,
        out_shape=(sds((3, chunks, lanes), f32),) + (sds((GRADS, lanes), f32),) * peers,
        in_specs=[smem] + [vmem] * (peers + 1),
        out_specs=(vmem,) * (peers + 1),
        scratch_shapes=[
            pltpu.VMEM((listed, GRADS, lanes), f32),
            pltpu.VMEM((chunks * width, lanes), f32),
            pltpu.VMEM((chunks * width, lanes), f32),
            pltpu.VMEM((chunks * width, lanes), f32),
            pltpu.VMEM((3, width, lanes), f32),
            pltpu.VMEM((8 * chunks, lanes), f32),
            pltpu.VMEM((listed, GRADS, lanes), f32),
            pltpu.VMEM((width, 6 * lanes), f32),
        ],
        compiler_params=pltpu.CompilerParams(vmem_limit_bytes=(3 * chunks + 12) * width * lanes * 4 + (8 << 20)),
        name="composite",
    )(meta, *sources, target.reshape(3, chunks, lanes))
    arrived = [splat_grads[0]] + [swapped(splat_grads[d], d) for d in range(1, peers)]
    dense, outgoing = pl.pallas_call(
        owner_kernel,
        out_shape=(sds((NPROJ, blocks, lanes), f32), sds((NPROJ, moves, lanes), f32)),
        in_specs=[smem] + [vmem] * peers,
        out_specs=(vmem, vmem),
        compiler_params=pltpu.CompilerParams(vmem_limit_bytes=1 << 20),
        name="owner",
    )(moving, *arrived)
    carried = onward(outgoing)
    updated = pl.pallas_call(
        update_kernel,
        out_shape=(sds((rows, blocks, lanes), f32),) * 3,
        in_specs=[smem, smem] + [vmem] * 6,
        out_specs=(vmem,) * 3,
        scratch_shapes=[pltpu.VMEM((rows, blocks, lanes), f32), pltpu.VMEM((8, blocks, lanes), f32)],
        compiler_params=pltpu.CompilerParams(vmem_limit_bytes=6 << 20),
        name="update",
    )(moving, view_basis, *turned, came, dense, carried)
    updated = [jnp.transpose(a, (1, 0, 2)) for a in updated]
    return (*updated, image.reshape(1, 3, pixels))


def solution(mesh):
    three = P(("region", "tile"), None, None)
    two = P(("region", "tile"), None)
    return jax.shard_map(
        on_device,
        mesh=mesh,
        in_specs=(three, three, three, P(), three, two, two),
        out_specs=(three, three, three, three),
        check_vma=False,
    )
```

```python
import functools
import math
import jax
import jax.numpy as jnp
import numpy as np
from jax import lax
from jax.experimental import pallas as pl
from jax.experimental.pallas import tpu as pltpu
from jax.sharding import PartitionSpec as P

SH = 16
TILE_SIDE = 32
NPROJ = 9
GRADS = 16
HALF = TILE_SIDE / 2.0

beta_one = 0.9
beta_two = 0.999
adam_eps = 1e-08
adam_step = 10.0
LOG2E = math.log2(math.e)


def rate_of(row):
    if row < 3:
        return 0.002
    if row < 6:
        return 0.005
    if row < 10:
        return 0.001
    if row < 11:
        return 0.05
    return 0.0025


def sigmoid(x):
    return 1.0 / (1.0 + jnp.exp(-x))


def geometry(p):
    v = {}
    v["tx"] = jnp.tanh(p(0))
    v["ty"] = jnp.tanh(p(1))
    depth = p(2)
    softplus = jnp.maximum(depth, 0.0) + jnp.log(1.0 + jnp.exp(-jnp.abs(depth)))
    v["f"] = 3.0 / (1.0 + softplus)
    v["z"] = v["f"] * v["f"]
    v["ts"] = [jnp.tanh(p(3 + k)) for k in range(3)]
    v["e"] = [2.25 * jnp.exp(2.0 * t) for t in v["ts"]]
    q = [p(6 + k) for k in range(4)]
    norm = jnp.sqrt((q[0] * q[0] + q[1] * q[1]) + (q[2] * q[2] + q[3] * q[3]))
    inv = 1.0 / jnp.maximum(norm, 1.0)
    v["norm"] = norm
    v["inv"] = inv
    w, x, y, z = [a * inv for a in q]
    v["q"] = (w, x, y, z)
    U = [1.0 - 2.0 * (y * y + z * z), 2.0 * (x * y - w * z), 2.0 * (x * z + w * y)]
    L = [2.0 * (x * y + w * z), 1.0 - 2.0 * (x * x + z * z), 2.0 * (y * z - w * x)]
    v["U"], v["L"] = U, L
    e = v["e"]
    v["sxx"] = U[0] * U[0] * e[0] + U[1] * U[1] * e[1] + U[2] * U[2] * e[2]
    v["syy"] = L[0] * L[0] * e[0] + L[1] * L[1] * e[1] + L[2] * L[2] * e[2]
    v["sxy"] = U[0] * L[0] * e[0] + U[1] * L[1] * e[1] + U[2] * L[2] * e[2]
    v["xx"] = v["z"] * v["sxx"] + 0.3
    v["yy"] = v["z"] * v["syy"] + 0.3
    v["xy"] = v["z"] * v["sxy"]
    v["idet"] = 1.0 / (v["xx"] * v["yy"] - v["xy"] * v["xy"])
    v["A"] = v["yy"] * v["idet"]
    v["B"] = -v["xy"] * v["idet"]
    v["C"] = v["xx"] * v["idet"]
    v["so"] = sigmoid(p(10) - 4.0)
    return v


def colour(p, c, basis):
    total = p(11 + SH * c) * basis(0)
    for k in range(1, SH):
        total = total + p(11 + SH * c + k) * basis(k)
    return sigmoid(total)


def project_kernel(basis_hbm, p_hbm, proj_ref, p_ref, basis_ref, sems):
    head = 11
    copies = [
        pltpu.make_async_copy(p_hbm.at[:head], p_ref.at[:head], sems.at[0]),
        pltpu.make_async_copy(p_hbm.at[head:], p_ref.at[head:], sems.at[1]),
        pltpu.make_async_copy(basis_hbm, basis_ref, sems.at[2]),
    ]
    for copy in copies:
        copy.start()
    p = lambda i: p_ref[i]
    copies[0].wait()
    v = geometry(p)
    proj_ref[0] = 0.375 * TILE_SIDE * v["tx"]
    proj_ref[1] = 0.375 * TILE_SIDE * v["ty"]
    proj_ref[2] = v["A"]
    proj_ref[3] = v["B"]
    proj_ref[4] = v["C"]
    proj_ref[5] = 0.99 * v["so"]
    copies[1].wait()
    copies[2].wait()
    for c in range(3):
        proj_ref[6 + c] = colour(p, c, lambda k: basis_ref[k])


def picks(moving_ref, blocks, lanes):
    slot = lax.broadcasted_iota(jnp.int32, (blocks, lanes), 0)
    source = jnp.zeros((blocks, lanes), jnp.int32)
    taken = jnp.zeros((blocks, lanes), jnp.bool_)
    for m in range(moving_ref.shape[1]):
        here = slot == moving_ref[0, m]
        source = jnp.where(here, m, source)
        taken = jnp.logical_or(taken, here)
    return source, taken


def pack_kernel(moving_ref, p_hbm, f_hbm, s_hbm, leave_ref, state_ref, sems):
    total, moves, lanes = leave_ref.shape
    rows, blocks, _ = p_hbm.shape
    copies = [
        pltpu.make_async_copy(ref, state_ref.at[a * rows : (a + 1) * rows], sems.at[a])
        for a, ref in enumerate((p_hbm, f_hbm, s_hbm))
    ]
    for copy in copies:
        copy.start()
    slot = lax.broadcasted_iota(jnp.int32, (blocks, lanes), 0)
    pick = jnp.zeros((blocks, lanes), jnp.int32)
    for m in range(moves):
        pick = jnp.where(slot == m, moving_ref[0, m], pick)
    leave_ref[total - 1] = pick[:moves].astype(jnp.float32)
    for a in range(3):
        copies[a].wait()
        for i in range(a * rows, (a + 1) * rows):
            leave_ref[i] = jnp.take_along_axis(state_ref[i], pick, axis=0)[:moves]


def split(value):
    high = value.astype(jnp.bfloat16).astype(jnp.float32)
    rest = value - high
    middle = rest.astype(jnp.bfloat16).astype(jnp.float32)
    return high, middle, rest - middle


def composite_kernel(meta_ref, *refs):
    peers = meta_ref.shape[0] // 2
    sources = refs[:peers]
    target_ref = refs[peers]
    image_ref = refs[peers + 1]
    slots_ref = refs[peers + 2]
    pbuf, qbuf, abuf, wbuf, ebuf, shbuf, errbuf, rbuf, gbuf, basis, lbuf = refs[peers + 3 :]
    listed, _, lanes = pbuf.shape
    width = listed * lanes
    groups = width // 8
    chunks = errbuf.shape[0] // 8
    spreads = qbuf.shape[0]
    assert chunks == 8
    for d in range(peers):
        pos = meta_ref[d]
        loc = meta_ref[peers + d]
        for r in range(NPROJ):
            pbuf[pos, pl.ds(r, 1), :] = sources[d][r, pl.ds(loc, 1), :]

    lane = lax.broadcasted_iota(jnp.int32, (8, lanes), 1)
    which = lax.broadcasted_iota(jnp.int32, (8, lanes), 0)
    px = (lane % TILE_SIDE).astype(jnp.float32) + (0.5 - HALF)
    py = (lane // TILE_SIDE).astype(jnp.float32) + (0.5 - HALF)
    step = float(lanes // TILE_SIDE)
    middle = py + step * ((chunks - 1) / 2.0)
    zero = jnp.zeros((8, lanes), jnp.float32)
    one = zero + 1.0

    def rows(*values):
        out = zero
        for r, value in enumerate(values):
            out = jnp.where(which == r, value, out)
        return out

    blank = jnp.zeros((24, lanes), jnp.bfloat16)
    for c in range(chunks):
        y = py + step * c
        high, low, _ = split(px * y)
        mono = rows(one, px, y, (px * px - 0.25) * 0.5, (y * y - 0.25) * 0.5, high, low)
        part = jnp.concatenate([mono, mono, mono], axis=0).astype(jnp.bfloat16)
        basis[0:24, c * lanes : (c + 1) * lanes] = part
        basis[24:48, c * lanes : (c + 1) * lanes] = blank
    for k in range(spreads):
        pick = jnp.where(which == k, one, zero)
        at = (chunks + k) * lanes
        basis[0:24, at : at + lanes] = blank
        basis[24:48, at : at + lanes] = jnp.concatenate([pick, pick, pick], axis=0).astype(jnp.bfloat16)

    def product(left, right):
        return jnp.dot(left, right, preferred_element_type=jnp.float32)

    def alphas(j, _):
        mx, my, ca, cb, cc, op = [pbuf[j, r : r + 1, :] for r in range(6)]
        a = -0.5 * LOG2E * ca
        b = -LOG2E * cb
        c = -0.5 * LOG2E * cc
        bx = b * mx
        by = b * my
        ax = a * mx
        cy = c * my
        flat = (ax + by) * mx + cy * my + 0.25 * (a + c) + jnp.log(op) * LOG2E
        power = rows(flat, -(2.0 * ax + by), -(2.0 * cy + bx), 2.0 * a, 2.0 * c, b, b)
        plain = rows(mx, my, *[pbuf[j, 6 + k : 7 + k, :] for k in range(3)])
        colours = rows(*[pbuf[j, 6 + k : 7 + k, :] for k in range(3)])
        high, mid, low = split(colours)
        left = jnp.concatenate([*split(power), *split(plain)], axis=0).T.astype(jnp.bfloat16)
        lbuf[pl.ds(pl.multiple_of(j * lanes, lanes), lanes), :] = jnp.concatenate(
            [high, high, mid, mid, high, low], axis=0
        ).T.astype(jnp.bfloat16)
        out = product(left, basis[...])
        for u in range(lanes // 8):
            row = pl.multiple_of(j * lanes + u * 8, 8)
            for n in range(chunks):
                part = out[u * 8 : (u + 1) * 8, n * lanes : (n + 1) * lanes]
                abuf[pl.ds(row * chunks + n * 8, 8), :] = jnp.exp2(part)
            for k in range(spreads):
                qbuf[k, pl.ds(row, 8), :] = out[u * 8 : (u + 1) * 8, (chunks + k) * lanes : (chunks + k + 1) * lanes]
        return 0

    lax.fori_loop(0, listed, alphas, 0, unroll=min(listed, 4))

    batch = 16

    def forward(n, running):
        trans, image = running
        base = pl.multiple_of(n * (batch * chunks), batch * chunks)
        for i in range(batch):
            alpha = abuf[pl.ds(base + (i // 8) * (8 * chunks) + i % 8, chunks, stride=8), :]
            weight = trans * alpha
            trans = trans * (1.0 - alpha)
            wbuf[pl.ds(base + i * chunks, chunks), :] = weight
            image = tuple(
                image[k] + weight * jnp.broadcast_to(qbuf[2 + k, pl.ds(n * batch + i, 1), :], (chunks, lanes))
                for k in range(3)
            )
        return (trans, image)

    _, image = lax.fori_loop(0, width // batch, forward, (one, (zero, zero, zero)))
    for k in range(8):
        if k < 3:
            image_ref[k] = image[k]
            errbuf[k * chunks : (k + 1) * chunks, :] = 2.0 * (image[k] - target_ref[k])
        else:
            errbuf[k * chunks : (k + 1) * chunks, :] = zero
    for c in range(chunks):
        high, mid, low = split(errbuf[pl.ds(c, 8, stride=chunks), :])
        basis[:, c * lanes : (c + 1) * lanes] = jnp.concatenate([high, mid, high, mid, low, high], axis=0).astype(
            jnp.bfloat16
        )

    def shading(j, _):
        out = product(lbuf[pl.ds(pl.multiple_of(j * lanes, lanes), lanes), :], basis[:, : chunks * lanes])
        for u in range(lanes // 8):
            row = pl.multiple_of(j * lanes + u * 8, 8)
            for n in range(chunks):
                shbuf[pl.ds(row * chunks + n * 8, 8), :] = out[u * 8 : (u + 1) * 8, n * lanes : (n + 1) * lanes]
        return 0

    lax.fori_loop(0, listed, shading, 0, unroll=min(listed, 4))
    for buf in (wbuf, ebuf):
        buf[pl.ds(width * chunks, 8 * chunks), :] = jnp.zeros((8 * chunks, lanes), jnp.float32)
    for k in range(2):
        qbuf[k, pl.ds(width, 8), :] = zero

    def reduce_pixels(u):
        row = pl.multiple_of(u * 8, 8)
        base = pl.multiple_of(u * (8 * chunks), 8 * chunks)
        part = [ebuf[pl.ds(base + c, 8, stride=chunks), :] for c in range(chunks)]
        light = [wbuf[pl.ds(base + c, 8, stride=chunks), :] for c in range(chunks)]
        dx = px - qbuf[0, pl.ds(row, 8), :]
        dy = middle - qbuf[1, pl.ds(row, 8), :]
        half = chunks // 2
        away = [((chunks - 1) / 2.0 - c) * step for c in range(half)]
        even = [part[c] + part[chunks - 1 - c] for c in range(half)]
        odd = [part[chunks - 1 - c] - part[c] for c in range(half)]
        plain = (even[0] + even[1]) + (even[2] + even[3])
        tilt = (away[0] * odd[0] + away[1] * odd[1]) + (away[2] * odd[2] + away[3] * odd[3])
        bend = (away[0] ** 2 * even[0] + away[1] ** 2 * even[1]) + (away[2] ** 2 * even[2] + away[3] ** 2 * even[3])
        sum_y = dy * plain + tilt
        sum_yy = dy * (sum_y + tilt) + bend
        sum_x = dx * plain
        sums = [plain, sum_x, sum_y, dx * sum_x, dx * sum_y, sum_yy]
        for k in range(3):
            lit = [light[c] * jnp.broadcast_to(errbuf[pl.ds(k * chunks + c, 1), :], (8, lanes)) for c in range(chunks)]
            sums.append(((lit[0] + lit[1]) + (lit[2] + lit[3])) + ((lit[4] + lit[5]) + (lit[6] + lit[7])))
        for r, value in enumerate(sums):
            rbuf[r, pl.ds(row, 8), :] = value

    def backward(n, behind):
        u = groups - 1 - n
        base = pl.multiple_of(u * (8 * chunks), 8 * chunks)
        reduce_pixels(u + 1)
        for i in reversed(range(8)):
            alpha = abuf[pl.ds(base + i, chunks, stride=8), :]
            ahead = shbuf[pl.ds(base + i, chunks, stride=8), :] - behind
            behind = behind + alpha * ahead
            ebuf[pl.ds(base + i * chunks, chunks), :] = wbuf[pl.ds(base + i * chunks, chunks), :] * ahead
        return behind

    lax.fori_loop(0, groups, backward, zero, unroll=2)
    reduce_pixels(0)

    def finish(j, _):
        at = pl.ds(pl.multiple_of(j * lanes, lanes), lanes)
        part = [jnp.sum(rbuf[r, at, :].T, axis=0, keepdims=True) for r in range(NPROJ)]
        s0, sx, sy, sxx, sxy, syy = part[:6]
        ca, cb, cc, op = [pbuf[j, r : r + 1, :] for r in range(2, 6)]
        gbuf[j, 0:1, :] = ca * sx + cb * sy
        gbuf[j, 1:2, :] = cb * sx + cc * sy
        gbuf[j, 2:3, :] = -0.5 * sxx
        gbuf[j, 3:4, :] = -sxy
        gbuf[j, 4:5, :] = -0.5 * syy
        gbuf[j, 5:6, :] = s0 / op
        for k in range(3):
            gbuf[j, 6 + k : 7 + k, :] = part[6 + k]
        gbuf[j, 9:16, :] = jnp.zeros((7, lanes), jnp.float32)
        return 0

    lax.fori_loop(0, listed, finish, 0, unroll=min(listed, 4))
    for d in range(peers):
        slots_ref[d] = gbuf[meta_ref[d]]
        slots_ref[d, NPROJ : NPROJ + 1, :] = jnp.full((1, lanes), 1, jnp.float32) * meta_ref[peers + d].astype(jnp.float32)


TERMS = 2 + 3 * 8 + 1 + 3


def prepare_kernel(moving_ref, basis_ref, state_ref, came_ref, mixed_ref, slope_ref, kbuf):
    total, blocks, lanes = state_ref.shape
    rows = total // 3
    moves = came_ref.shape[1]
    source, taken = picks(moving_ref, blocks, lanes)

    def arrived(i):
        kbuf[i % 8, 0:moves, :] = came_ref[i]
        return jnp.take_along_axis(kbuf[i % 8], source, axis=0)

    for a, factor in enumerate((None, beta_one, beta_two)):
        for i in range(a * rows, (a + 1) * rows):
            value = jnp.where(taken, arrived(i), state_ref[i])
            mixed_ref[i] = value if factor is None else factor * value
    slot = lax.broadcasted_iota(jnp.int32, (blocks, lanes), 0).astype(jnp.float32)
    slope_ref[TERMS] = jnp.where(taken, arrived(total), slot)
    slope_ref[TERMS + 1] = taken.astype(jnp.float32)

    part = 1.0 - beta_one
    p = lambda i: mixed_ref[i]
    v = geometry(p)
    slope_ref[0] = part * 0.375 * TILE_SIDE * (1.0 - v["tx"] * v["tx"])
    slope_ref[1] = part * 0.375 * TILE_SIDE * (1.0 - v["ty"] * v["ty"])
    slope_ref[TERMS - 4] = part * 0.99 * v["so"] * (1.0 - v["so"])
    for c in range(3):
        shade = colour(p, c, lambda k: basis_ref[k])
        slope_ref[TERMS - 3 + c] = part * shade * (1.0 - shade)
    U, L, e, f, idet = v["U"], v["L"], v["e"], v["f"], v["idet"]
    w, x, y, z = v["q"]
    share = jnp.where(v["norm"] > 1.0, 1.0, jnp.where(v["norm"] == 1.0, 0.5, 0.0))
    depth = (-2.0 / 3.0) * f * f * f * sigmoid(p(2)) * part
    for n, name in enumerate("ABC"):
        gdet = -v[name] * idet
        gxx = gdet * v["yy"]
        gyy = gdet * v["xx"]
        gxy = -2.0 * gdet * v["xy"]
        if name == "A":
            gyy = gyy + idet
        elif name == "B":
            gxy = gxy - idet
        else:
            gxx = gxx + idet
        slope_ref[2 + n] = (gxx * v["sxx"] + gyy * v["syy"] + gxy * v["sxy"]) * depth
        gU, gL = [], []
        for k in range(3):
            t = v["ts"][k]
            ze = v["z"] * e[k]
            ge = gxx * U[k] * U[k] + gyy * L[k] * L[k] + gxy * U[k] * L[k]
            slope_ref[5 + 3 * k + n] = (2.0 * part) * ge * ze * (1.0 - t * t)
            gU.append(ze * (2.0 * gxx * U[k] + gxy * L[k]))
            gL.append(ze * (2.0 * gyy * L[k] + gxy * U[k]))
        gq = [
            2.0 * (z * (gL[0] - gU[1]) + y * gU[2] - x * gL[2]),
            2.0 * (y * (gU[1] + gL[0]) + z * gU[2] - 2.0 * x * gL[1] - w * gL[2]),
            2.0 * (x * (gU[1] + gL[0]) - 2.0 * y * gU[0] + w * gU[2] + z * gL[2]),
            2.0 * (w * (gL[0] - gU[1]) - 2.0 * z * (gU[0] + gL[1]) + x * gU[2] + y * gL[2]),
        ]
        along = share * (w * gq[0] + x * gq[1] + y * gq[2] + z * gq[3])
        for k, unit in enumerate((w, x, y, z)):
            slope_ref[14 + 3 * k + n] = part * (gq[k] - unit * along) * v["inv"]


def update_kernel(basis_ref, mixed_ref, slope_ref, image_ref, *refs):
    sources = refs[:-9]
    outs = refs[-9:-6]
    picture_hbm = refs[-6]
    stages = refs[-5:-2]
    sems, picture_sem = refs[-2:]
    total, blocks, lanes = mixed_ref.shape
    rows = total // 3
    picture = pltpu.make_async_copy(image_ref, picture_hbm, picture_sem.at[0])
    picture.start()
    want = slope_ref[TERMS]
    taken = slope_ref[TERMS + 1] > 0.5
    wide = lambda row: jnp.broadcast_to(row, (blocks, lanes))
    grads = [jnp.zeros((blocks, lanes), jnp.float32) for _ in range(NPROJ)]
    for ref in sources:
        for side in range(2):
            mask = jnp.logical_and(want == wide(ref[side, NPROJ : NPROJ + 1, :]), taken if side else ~taken)
            for r in range(NPROJ):
                grads[r] = grads[r] + jnp.where(mask, wide(ref[side, r : r + 1, :]), 0.0)

    def store(i, grad):
        one = mixed_ref[rows + i] + grad
        two = mixed_ref[2 * rows + i] + ((1.0 - beta_two) / (1.0 - beta_one) ** 2) * (grad * grad)
        scaled = (rate_of(i) / (1.0 - beta_one**adam_step)) * one
        stages[0][i] = mixed_ref[i] - scaled / (jnp.sqrt(two * (1.0 / (1.0 - beta_two**adam_step))) + adam_eps)
        stages[1][i] = one
        stages[2][i] = two

    copies = []

    def ship(low, high):
        for a in range(3):
            copy = pltpu.make_async_copy(
                stages[a].at[low:high], outs[a].at[low:high], sems.at[len(copies)]
            )
            copy.start()
            copies.append(copy)

    for c in range(3):
        logit = grads[6 + c] * slope_ref[TERMS - 3 + c]
        for k in range(SH):
            store(11 + SH * c + k, logit * basis_ref[k])
        ship(11 + SH * c, 11 + SH * (c + 1))
    store(0, grads[0] * slope_ref[0])
    store(1, grads[1] * slope_ref[1])
    for i in range(8):
        at = 2 + 3 * i
        store(2 + i, grads[2] * slope_ref[at] + grads[3] * slope_ref[at + 1] + grads[4] * slope_ref[at + 2])
    store(10, grads[5] * slope_ref[TERMS - 4])
    ship(0, 11)
    for copy in copies:
        copy.wait()
    picture.wait()


def on_device(params, first_moment, second_moment, view_basis, target, tile_blocks, moving):
    blocks, rows, lanes = params.shape
    peers = lax.axis_size("tile")
    listed = tile_blocks.shape[1]
    moves = moving.shape[1]
    pixels = target.shape[2]
    chunks = pixels // lanes
    width = listed * lanes
    f32 = jnp.float32
    smem = pl.BlockSpec(memory_space=pltpu.SMEM)
    vmem = pl.BlockSpec(memory_space=pltpu.VMEM)
    sds = jax.ShapeDtypeStruct

    me = lax.axis_index("tile")
    partner = jnp.bitwise_xor(me, jnp.arange(peers, dtype=jnp.int32))
    matches = (tile_blocks[0][None, :] // blocks) == partner[:, None]
    pos = jnp.sum(jnp.where(matches, jnp.arange(listed, dtype=jnp.int32)[None, :], 0), axis=1)
    loc = jnp.sum(jnp.where(matches, (tile_blocks[0] % blocks)[None, :], 0), axis=1)
    meta = jnp.concatenate([pos, loc]).astype(jnp.int32)

    hbm = pl.BlockSpec(memory_space=pltpu.HBM)
    stay = lambda value: pltpu.with_memory_space_constraint(value, pltpu.HBM)
    dma = pltpu.SemaphoreType.DMA
    turned = [jnp.transpose(a, (1, 0, 2)) for a in (params, first_moment, second_moment)]
    projected = pl.pallas_call(
        project_kernel,
        out_shape=sds((NPROJ, blocks, lanes), f32),
        in_specs=[hbm, hbm],
        out_specs=vmem,
        scratch_shapes=[pltpu.VMEM((rows, blocks, lanes), f32), pltpu.SMEM(view_basis.shape, f32), dma((3,))],
        compiler_params=pltpu.CompilerParams(vmem_limit_bytes=2 << 20),
        name="project",
    )(stay(view_basis), stay(turned[0]))
    leaving, state = pl.pallas_call(
        pack_kernel,
        out_shape=(sds((3 * rows + 1, moves, lanes), f32), sds((3 * rows, blocks, lanes), f32)),
        in_specs=[smem, hbm, hbm, hbm],
        out_specs=(vmem, vmem),
        scratch_shapes=[dma((3,))],
        compiler_params=pltpu.CompilerParams(vmem_limit_bytes=4 << 20),
        name="pack",
    )(moving, *[stay(a) for a in turned])

    def swapped(value, d):
        return lax.ppermute(value, "tile", [(i, i ^ d) for i in range(peers)])

    regions = lax.axis_size("region")
    onward = lambda value: lax.ppermute(value, "region", [(i, (i + 1) % regions) for i in range(regions)])

    away = {d: swapped(projected, d) for d in reversed(range(1, peers))}
    came = onward(leaving)
    image, slots = pl.pallas_call(
        composite_kernel,
        out_shape=(sds((3, chunks, lanes), f32), sds((peers, GRADS, lanes), f32)),
        in_specs=[smem] + [vmem] * (peers + 1),
        out_specs=(vmem, vmem),
        scratch_shapes=[
            pltpu.VMEM((listed, GRADS, lanes), f32),
            pltpu.VMEM((5, width + 8, lanes), f32),
            pltpu.VMEM((chunks * width, lanes), f32),
            pltpu.VMEM((chunks * (width + 8), lanes), f32),
            pltpu.VMEM((chunks * (width + 8), lanes), f32),
            pltpu.VMEM((chunks * width, lanes), f32),
            pltpu.VMEM((8 * chunks, lanes), f32),
            pltpu.VMEM((NPROJ, width + 8, lanes), f32),
            pltpu.VMEM((listed, GRADS, lanes), f32),
            pltpu.VMEM((48, (chunks + 5) * lanes), jnp.bfloat16),
            pltpu.VMEM((width, 48), jnp.bfloat16),
        ],
        compiler_params=pltpu.CompilerParams(vmem_limit_bytes=(4 * chunks + 20) * (width + 8) * lanes * 4 + (3 << 20)),
        name="composite",
    )(meta, projected, *[away[d] for d in range(1, peers)], target.reshape(3, chunks, lanes))
    mixed, slope = pl.pallas_call(
        prepare_kernel,
        out_shape=(sds((3 * rows, blocks, lanes), f32), sds((TERMS + 2, blocks, lanes), f32)),
        in_specs=[smem, smem, vmem, vmem],
        out_specs=(vmem, vmem),
        scratch_shapes=[pltpu.VMEM((8, blocks, lanes), f32)],
        compiler_params=pltpu.CompilerParams(vmem_limit_bytes=5 << 20),
        name="prepare",
    )(moving, view_basis, state, came)
    pairs = jnp.stack([slots, onward(slots)], axis=1)
    gathered = {0: pairs[0]}
    for d in reversed(range(1, peers)):
        gathered[d] = swapped(pairs[d], d)
    updated = pl.pallas_call(
        update_kernel,
        out_shape=(sds((rows, blocks, lanes), f32),) * 3 + (sds(image.shape, f32),),
        in_specs=[smem] + [vmem] * (3 + peers),
        out_specs=(hbm,) * 4,
        scratch_shapes=[pltpu.VMEM((rows, blocks, lanes), f32)] * 3 + [dma((12,)), dma((1,))],
        compiler_params=pltpu.CompilerParams(vmem_limit_bytes=5 << 20),
        name="update",
    )(view_basis, mixed, slope, image, *[gathered[d] for d in range(peers)])
    turned_back = [jnp.transpose(a, (1, 0, 2)) for a in updated[:3]]
    return (*turned_back, updated[3].reshape(1, 3, pixels))


def solution(mesh):
    three = P(("region", "tile"), None, None)
    two = P(("region", "tile"), None)
    return jax.shard_map(
        on_device,
        mesh=mesh,
        in_specs=(three, three, three, P(), three, two, two),
        out_specs=(three, three, three, three),
        check_vma=False,
    )
```

```python
import functools
import math
import jax
import jax.numpy as jnp
import numpy as np
from jax import lax
from jax.experimental import pallas as pl
from jax.experimental.pallas import tpu as pltpu
from jax.sharding import PartitionSpec as P

SH = 16
TILE_SIDE = 32
NPROJ = 9
GRADS = 16
HALF = TILE_SIDE / 2.0

beta_one = 0.9
beta_two = 0.999
adam_eps = 1e-08
adam_step = 10.0
LOG2E = math.log2(math.e)


def rate_of(row):
    if row < 3:
        return 0.002
    if row < 6:
        return 0.005
    if row < 10:
        return 0.001
    if row < 11:
        return 0.05
    return 0.0025


def sigmoid(x):
    return 1.0 / (1.0 + jnp.exp(-x))


def geometry(p):
    v = {}
    v["tx"] = jnp.tanh(p(0))
    v["ty"] = jnp.tanh(p(1))
    depth = p(2)
    softplus = jnp.maximum(depth, 0.0) + jnp.log(1.0 + jnp.exp(-jnp.abs(depth)))
    v["f"] = 3.0 / (1.0 + softplus)
    v["z"] = v["f"] * v["f"]
    v["ts"] = [jnp.tanh(p(3 + k)) for k in range(3)]
    v["e"] = [2.25 * jnp.exp(2.0 * t) for t in v["ts"]]
    q = [p(6 + k) for k in range(4)]
    norm = jnp.sqrt((q[0] * q[0] + q[1] * q[1]) + (q[2] * q[2] + q[3] * q[3]))
    inv = 1.0 / jnp.maximum(norm, 1.0)
    v["norm"] = norm
    v["inv"] = inv
    w, x, y, z = [a * inv for a in q]
    v["q"] = (w, x, y, z)
    U = [1.0 - 2.0 * (y * y + z * z), 2.0 * (x * y - w * z), 2.0 * (x * z + w * y)]
    L = [2.0 * (x * y + w * z), 1.0 - 2.0 * (x * x + z * z), 2.0 * (y * z - w * x)]
    v["U"], v["L"] = U, L
    e = v["e"]
    v["sxx"] = U[0] * U[0] * e[0] + U[1] * U[1] * e[1] + U[2] * U[2] * e[2]
    v["syy"] = L[0] * L[0] * e[0] + L[1] * L[1] * e[1] + L[2] * L[2] * e[2]
    v["sxy"] = U[0] * L[0] * e[0] + U[1] * L[1] * e[1] + U[2] * L[2] * e[2]
    v["xx"] = v["z"] * v["sxx"] + 0.3
    v["yy"] = v["z"] * v["syy"] + 0.3
    v["xy"] = v["z"] * v["sxy"]
    v["idet"] = 1.0 / (v["xx"] * v["yy"] - v["xy"] * v["xy"])
    v["A"] = v["yy"] * v["idet"]
    v["B"] = -v["xy"] * v["idet"]
    v["C"] = v["xx"] * v["idet"]
    v["so"] = sigmoid(p(10) - 4.0)
    return v


def colour(p, c, basis):
    total = p(11 + SH * c) * basis(0)
    for k in range(1, SH):
        total = total + p(11 + SH * c + k) * basis(k)
    return sigmoid(total)


def project_kernel(peers, basis_hbm, listed_hbm, p_hbm, proj_ref, meta_ref, p_ref, basis_ref, listed_ref, sems):
    head = 11
    blocks = p_ref.shape[1]
    copies = [
        pltpu.make_async_copy(p_hbm.at[:head], p_ref.at[:head], sems.at[0]),
        pltpu.make_async_copy(basis_hbm, basis_ref, sems.at[1]),
        pltpu.make_async_copy(listed_hbm, listed_ref, sems.at[2]),
    ]
    for c in range(3):
        span = pl.ds(head + SH * c, SH)
        copies.append(pltpu.make_async_copy(p_hbm.at[span], p_ref.at[span], sems.at[3 + c]))
    for copy in copies:
        copy.start()
    p = lambda i: p_ref[i]
    copies[0].wait()
    v = geometry(p)
    proj_ref[0] = 0.375 * TILE_SIDE * v["tx"]
    proj_ref[1] = 0.375 * TILE_SIDE * v["ty"]
    proj_ref[2] = v["A"]
    proj_ref[3] = v["B"]
    proj_ref[4] = v["C"]
    proj_ref[5] = 0.99 * v["so"]
    copies[2].wait()
    me = lax.axis_index("tile")
    for n in range(listed_ref.shape[1]):
        listed = listed_ref[0, n]
        distance = jnp.bitwise_xor(listed // blocks, me)
        meta_ref[distance] = n
        meta_ref[peers + distance] = listed % blocks
    copies[1].wait()
    for c in range(3):
        copies[3 + c].wait()
        proj_ref[6 + c] = colour(p, c, lambda k: basis_ref[k])


def picks(moving_ref, blocks, lanes):
    slot = lax.broadcasted_iota(jnp.int32, (blocks, lanes), 0)
    source = jnp.zeros((blocks, lanes), jnp.int32)
    taken = jnp.zeros((blocks, lanes), jnp.bool_)
    for m in range(moving_ref.shape[1]):
        here = slot == moving_ref[0, m]
        source = jnp.where(here, m, source)
        taken = jnp.logical_or(taken, here)
    return source, taken


PIECES = 4


def pieces(rows):
    cuts = [rows * n // PIECES for n in range(PIECES + 1)]
    return list(zip(cuts[:-1], cuts[1:]))


def pack_kernel(moving_hbm, p_hbm, f_hbm, s_hbm, leave_ref, state_ref, moving_ref, sems):
    total, moves, lanes = leave_ref.shape
    rows, blocks, _ = p_hbm.shape
    ids = pltpu.make_async_copy(moving_hbm, moving_ref, sems.at[3 * PIECES])
    ids.start()
    spans = []
    copies = []
    for a, ref in enumerate((p_hbm, f_hbm, s_hbm)):
        for low, high in pieces(rows):
            span = (a * rows + low, a * rows + high)
            copy = pltpu.make_async_copy(ref.at[low:high], state_ref.at[span[0] : span[1]], sems.at[len(copies)])
            copy.start()
            spans.append(span)
            copies.append(copy)
    ids.wait()
    slot = lax.broadcasted_iota(jnp.int32, (blocks, lanes), 0)
    pick = jnp.zeros((blocks, lanes), jnp.int32)
    for m in range(moves):
        pick = jnp.where(slot == m, moving_ref[0, m], pick)
    leave_ref[total - 1] = pick[:moves].astype(jnp.float32)
    for copy, span in zip(copies, spans):
        copy.wait()
        for i in range(*span):
            leave_ref[i] = jnp.take_along_axis(state_ref[i], pick, axis=0)[:moves]


def split(value):
    high = value.astype(jnp.bfloat16).astype(jnp.float32)
    rest = value - high
    middle = rest.astype(jnp.bfloat16).astype(jnp.float32)
    return high, middle, rest - middle


def composite_kernel(meta_ref, *refs):
    peers = meta_ref.shape[0] // 2
    sources = refs[:peers][::-1]
    target_ref = refs[peers]
    image_ref = refs[peers + 1]
    slots_ref = refs[peers + 2]
    pbuf, qbuf, abuf, wbuf, ebuf, shbuf, errbuf, rbuf, gbuf, basis, lbuf = refs[peers + 3 :]
    listed, _, lanes = pbuf.shape
    width = listed * lanes
    groups = width // 8
    chunks = errbuf.shape[0] // 8
    spreads = qbuf.shape[0]
    assert chunks == 8
    for d in range(peers):
        pos = meta_ref[d]
        loc = meta_ref[peers + d]
        for r in range(NPROJ):
            pbuf[pos, pl.ds(r, 1), :] = sources[d][r, pl.ds(loc, 1), :]

    lane = lax.broadcasted_iota(jnp.int32, (8, lanes), 1)
    which = lax.broadcasted_iota(jnp.int32, (8, lanes), 0)
    px = (lane % TILE_SIDE).astype(jnp.float32) + (0.5 - HALF)
    py = (lane // TILE_SIDE).astype(jnp.float32) + (0.5 - HALF)
    step = float(lanes // TILE_SIDE)
    middle = py + step * ((chunks - 1) / 2.0)
    zero = jnp.zeros((8, lanes), jnp.float32)
    one = zero + 1.0

    def rows(*values):
        out = zero
        for r, value in enumerate(values):
            out = jnp.where(which == r, value, out)
        return out

    blank = jnp.zeros((24, lanes), jnp.bfloat16)
    for c in range(chunks):
        y = py + step * c
        high, low, _ = split(px * y)
        mono = rows(one, px, y, (px * px - 0.25) * 0.5, (y * y - 0.25) * 0.5, high, low)
        part = jnp.concatenate([mono, mono, mono], axis=0).astype(jnp.bfloat16)
        basis[0:24, c * lanes : (c + 1) * lanes] = part
        basis[24:48, c * lanes : (c + 1) * lanes] = blank
    for k in range(spreads):
        pick = jnp.where(which == k, one, zero)
        at = (chunks + k) * lanes
        basis[0:24, at : at + lanes] = blank
        basis[24:48, at : at + lanes] = jnp.concatenate([pick, pick, pick], axis=0).astype(jnp.bfloat16)

    def product(left, right):
        return jnp.dot(left, right, preferred_element_type=jnp.float32)

    def alphas(j, _):
        mx, my, ca, cb, cc, op = [pbuf[j, r : r + 1, :] for r in range(6)]
        a = -0.5 * LOG2E * ca
        b = -LOG2E * cb
        c = -0.5 * LOG2E * cc
        bx = b * mx
        by = b * my
        ax = a * mx
        cy = c * my
        flat = (ax + by) * mx + cy * my + 0.25 * (a + c) + jnp.log(op) * LOG2E
        power = rows(flat, -(2.0 * ax + by), -(2.0 * cy + bx), 2.0 * a, 2.0 * c, b, b)
        plain = rows(mx, my, *[pbuf[j, 6 + k : 7 + k, :] for k in range(3)])
        colours = rows(*[pbuf[j, 6 + k : 7 + k, :] for k in range(3)])
        high, mid, low = split(colours)
        left = jnp.concatenate([*split(power), *split(plain)], axis=0).T.astype(jnp.bfloat16)
        lbuf[pl.ds(pl.multiple_of(j * lanes, lanes), lanes), :] = jnp.concatenate(
            [high, high, mid, mid, high, low], axis=0
        ).T.astype(jnp.bfloat16)
        out = product(left, basis[...])
        for u in range(lanes // 8):
            row = pl.multiple_of(j * lanes + u * 8, 8)
            for n in range(chunks):
                part = out[u * 8 : (u + 1) * 8, n * lanes : (n + 1) * lanes]
                abuf[pl.ds(row * chunks + n * 8, 8), :] = jnp.exp2(part)
            for k in range(spreads):
                qbuf[k, pl.ds(row, 8), :] = out[u * 8 : (u + 1) * 8, (chunks + k) * lanes : (chunks + k + 1) * lanes]
        return 0

    lax.fori_loop(0, listed, alphas, 0, unroll=min(listed, 4))

    batch = 16

    def forward(n, running):
        trans, image = running
        base = pl.multiple_of(n * (batch * chunks), batch * chunks)
        for i in range(batch):
            alpha = abuf[pl.ds(base + (i // 8) * (8 * chunks) + i % 8, chunks, stride=8), :]
            weight = trans * alpha
            trans = trans * (1.0 - alpha)
            wbuf[pl.ds(base + i * chunks, chunks), :] = weight
            image = tuple(
                image[k] + weight * jnp.broadcast_to(qbuf[2 + k, pl.ds(n * batch + i, 1), :], (chunks, lanes))
                for k in range(3)
            )
        return (trans, image)

    _, image = lax.fori_loop(0, width // batch, forward, (one, (zero, zero, zero)))
    for k in range(8):
        if k < 3:
            image_ref[k] = image[k]
            errbuf[k * chunks : (k + 1) * chunks, :] = 2.0 * (image[k] - target_ref[k])
        else:
            errbuf[k * chunks : (k + 1) * chunks, :] = zero
    for c in range(chunks):
        high, mid, low = split(errbuf[pl.ds(c, 8, stride=chunks), :])
        basis[:, c * lanes : (c + 1) * lanes] = jnp.concatenate([high, mid, high, mid, low, high], axis=0).astype(
            jnp.bfloat16
        )

    def shading(j, _):
        out = product(lbuf[pl.ds(pl.multiple_of(j * lanes, lanes), lanes), :], basis[:, : chunks * lanes])
        for u in range(lanes // 8):
            row = pl.multiple_of(j * lanes + u * 8, 8)
            for n in range(chunks):
                shbuf[pl.ds(row * chunks + n * 8, 8), :] = out[u * 8 : (u + 1) * 8, n * lanes : (n + 1) * lanes]
        return 0

    lax.fori_loop(0, listed, shading, 0, unroll=min(listed, 4))
    for buf in (wbuf, ebuf):
        buf[pl.ds(width * chunks, 8 * chunks), :] = jnp.zeros((8 * chunks, lanes), jnp.float32)
    for k in range(2):
        qbuf[k, pl.ds(width, 8), :] = zero

    def reduce_pixels(u):
        row = pl.multiple_of(u * 8, 8)
        base = pl.multiple_of(u * (8 * chunks), 8 * chunks)
        part = [ebuf[pl.ds(base + c, 8, stride=chunks), :] for c in range(chunks)]
        light = [wbuf[pl.ds(base + c, 8, stride=chunks), :] for c in range(chunks)]
        dx = px - qbuf[0, pl.ds(row, 8), :]
        dy = middle - qbuf[1, pl.ds(row, 8), :]
        half = chunks // 2
        away = [((chunks - 1) / 2.0 - c) * step for c in range(half)]
        even = [part[c] + part[chunks - 1 - c] for c in range(half)]
        odd = [part[chunks - 1 - c] - part[c] for c in range(half)]
        plain = (even[0] + even[1]) + (even[2] + even[3])
        tilt = (away[0] * odd[0] + away[1] * odd[1]) + (away[2] * odd[2] + away[3] * odd[3])
        bend = (away[0] ** 2 * even[0] + away[1] ** 2 * even[1]) + (away[2] ** 2 * even[2] + away[3] ** 2 * even[3])
        sum_y = dy * plain + tilt
        sum_yy = dy * (sum_y + tilt) + bend
        sum_x = dx * plain
        sums = [plain, sum_x, sum_y, dx * sum_x, dx * sum_y, sum_yy]
        for k in range(3):
            lit = [light[c] * jnp.broadcast_to(errbuf[pl.ds(k * chunks + c, 1), :], (8, lanes)) for c in range(chunks)]
            sums.append(((lit[0] + lit[1]) + (lit[2] + lit[3])) + ((lit[4] + lit[5]) + (lit[6] + lit[7])))
        for r, value in enumerate(sums):
            rbuf[r, pl.ds(row, 8), :] = value

    def backward(n, behind):
        u = groups - 1 - n
        base = pl.multiple_of(u * (8 * chunks), 8 * chunks)
        reduce_pixels(u + 1)
        for i in reversed(range(8)):
            alpha = abuf[pl.ds(base + i, chunks, stride=8), :]
            ahead = shbuf[pl.ds(base + i, chunks, stride=8), :] - behind
            behind = behind + alpha * ahead
            ebuf[pl.ds(base + i * chunks, chunks), :] = wbuf[pl.ds(base + i * chunks, chunks), :] * ahead
        return behind

    lax.fori_loop(0, groups, backward, zero, unroll=2)
    reduce_pixels(0)

    def finish(j, _):
        at = pl.ds(pl.multiple_of(j * lanes, lanes), lanes)
        part = [jnp.sum(rbuf[r, at, :].T, axis=0, keepdims=True) for r in range(NPROJ)]
        s0, sx, sy, sxx, sxy, syy = part[:6]
        ca, cb, cc, op = [pbuf[j, r : r + 1, :] for r in range(2, 6)]
        gbuf[j, 0:1, :] = ca * sx + cb * sy
        gbuf[j, 1:2, :] = cb * sx + cc * sy
        gbuf[j, 2:3, :] = -0.5 * sxx
        gbuf[j, 3:4, :] = -sxy
        gbuf[j, 4:5, :] = -0.5 * syy
        gbuf[j, 5:6, :] = s0 / op
        for k in range(3):
            gbuf[j, 6 + k : 7 + k, :] = part[6 + k]
        gbuf[j, 9:16, :] = jnp.zeros((7, lanes), jnp.float32)
        return 0

    lax.fori_loop(0, listed, finish, 0, unroll=min(listed, 4))
    for d in range(peers):
        slots_ref[d] = gbuf[meta_ref[d]]
        slots_ref[d, NPROJ : NPROJ + 1, :] = jnp.full((1, lanes), 1, jnp.float32) * meta_ref[peers + d].astype(jnp.float32)


TERMS = 2 + 3 * 8 + 1 + 3


def prepare_kernel(moving_ref, basis_ref, state_ref, came_ref, mixed_ref, slope_ref, kbuf):
    total, blocks, lanes = state_ref.shape
    rows = total // 3
    moves = came_ref.shape[1]
    source, taken = picks(moving_ref, blocks, lanes)

    def arrived(i):
        kbuf[i % 8, 0:moves, :] = came_ref[i]
        return jnp.take_along_axis(kbuf[i % 8], source, axis=0)

    for a, factor in enumerate((None, beta_one, beta_two)):
        for i in range(a * rows, (a + 1) * rows):
            value = jnp.where(taken, arrived(i), state_ref[i])
            mixed_ref[i] = value if factor is None else factor * value
    slot = lax.broadcasted_iota(jnp.int32, (blocks, lanes), 0).astype(jnp.float32)
    slope_ref[TERMS] = jnp.where(taken, arrived(total), slot)
    slope_ref[TERMS + 1] = taken.astype(jnp.float32)

    part = 1.0 - beta_one
    p = lambda i: mixed_ref[i]
    v = geometry(p)
    slope_ref[0] = part * 0.375 * TILE_SIDE * (1.0 - v["tx"] * v["tx"])
    slope_ref[1] = part * 0.375 * TILE_SIDE * (1.0 - v["ty"] * v["ty"])
    slope_ref[TERMS - 4] = part * 0.99 * v["so"] * (1.0 - v["so"])
    for c in range(3):
        shade = colour(p, c, lambda k: basis_ref[k])
        slope_ref[TERMS - 3 + c] = part * shade * (1.0 - shade)
    U, L, e, f, idet = v["U"], v["L"], v["e"], v["f"], v["idet"]
    w, x, y, z = v["q"]
    share = jnp.where(v["norm"] > 1.0, 1.0, jnp.where(v["norm"] == 1.0, 0.5, 0.0))
    depth = (-2.0 / 3.0) * f * f * f * sigmoid(p(2)) * part
    for n, name in enumerate("ABC"):
        gdet = -v[name] * idet
        gxx = gdet * v["yy"]
        gyy = gdet * v["xx"]
        gxy = -2.0 * gdet * v["xy"]
        if name == "A":
            gyy = gyy + idet
        elif name == "B":
            gxy = gxy - idet
        else:
            gxx = gxx + idet
        slope_ref[2 + n] = (gxx * v["sxx"] + gyy * v["syy"] + gxy * v["sxy"]) * depth
        gU, gL = [], []
        for k in range(3):
            t = v["ts"][k]
            ze = v["z"] * e[k]
            ge = gxx * U[k] * U[k] + gyy * L[k] * L[k] + gxy * U[k] * L[k]
            slope_ref[5 + 3 * k + n] = (2.0 * part) * ge * ze * (1.0 - t * t)
            gU.append(ze * (2.0 * gxx * U[k] + gxy * L[k]))
            gL.append(ze * (2.0 * gyy * L[k] + gxy * U[k]))
        gq = [
            2.0 * (z * (gL[0] - gU[1]) + y * gU[2] - x * gL[2]),
            2.0 * (y * (gU[1] + gL[0]) + z * gU[2] - 2.0 * x * gL[1] - w * gL[2]),
            2.0 * (x * (gU[1] + gL[0]) - 2.0 * y * gU[0] + w * gU[2] + z * gL[2]),
            2.0 * (w * (gL[0] - gU[1]) - 2.0 * z * (gU[0] + gL[1]) + x * gU[2] + y * gL[2]),
        ]
        along = share * (w * gq[0] + x * gq[1] + y * gq[2] + z * gq[3])
        for k, unit in enumerate((w, x, y, z)):
            slope_ref[14 + 3 * k + n] = part * (gq[k] - unit * along) * v["inv"]


def update_kernel(basis_ref, mixed_ref, slope_ref, image_ref, *refs):
    sources = refs[:-9]
    outs = refs[-9:-6]
    picture_hbm = refs[-6]
    stages = refs[-5:-2]
    sems, picture_sem = refs[-2:]
    total, blocks, lanes = mixed_ref.shape
    rows = total // 3
    picture = pltpu.make_async_copy(image_ref, picture_hbm, picture_sem.at[0])
    picture.start()
    want = slope_ref[TERMS]
    taken = slope_ref[TERMS + 1] > 0.5
    wide = lambda row: jnp.broadcast_to(row, (blocks, lanes))
    grads = [jnp.zeros((blocks, lanes), jnp.float32) for _ in range(NPROJ)]
    for ref in sources:
        for side in range(2):
            mask = jnp.logical_and(want == wide(ref[side, NPROJ : NPROJ + 1, :]), taken if side else ~taken)
            for r in range(NPROJ):
                grads[r] = grads[r] + jnp.where(mask, wide(ref[side, r : r + 1, :]), 0.0)

    def store(i, grad):
        one = mixed_ref[rows + i] + grad
        two = mixed_ref[2 * rows + i] + ((1.0 - beta_two) / (1.0 - beta_one) ** 2) * (grad * grad)
        scaled = (rate_of(i) / (1.0 - beta_one**adam_step)) * one
        stages[0][i] = mixed_ref[i] - scaled / (jnp.sqrt(two * (1.0 / (1.0 - beta_two**adam_step))) + adam_eps)
        stages[1][i] = one
        stages[2][i] = two

    copies = []

    def ship(low, high):
        for a in range(3):
            copy = pltpu.make_async_copy(
                stages[a].at[low:high], outs[a].at[low:high], sems.at[len(copies)]
            )
            copy.start()
            copies.append(copy)

    for c in range(3):
        logit = grads[6 + c] * slope_ref[TERMS - 3 + c]
        for k in range(SH):
            store(11 + SH * c + k, logit * basis_ref[k])
        ship(11 + SH * c, 11 + SH * (c + 1))
    store(0, grads[0] * slope_ref[0])
    store(1, grads[1] * slope_ref[1])
    for i in range(8):
        at = 2 + 3 * i
        store(2 + i, grads[2] * slope_ref[at] + grads[3] * slope_ref[at + 1] + grads[4] * slope_ref[at + 2])
    store(10, grads[5] * slope_ref[TERMS - 4])
    ship(0, 11)
    for copy in copies:
        copy.wait()
    picture.wait()


def on_device(params, first_moment, second_moment, view_basis, target, tile_blocks, moving):
    blocks, rows, lanes = params.shape
    peers = lax.axis_size("tile")
    listed = tile_blocks.shape[1]
    moves = moving.shape[1]
    pixels = target.shape[2]
    chunks = pixels // lanes
    width = listed * lanes
    f32 = jnp.float32
    smem = pl.BlockSpec(memory_space=pltpu.SMEM)
    vmem = pl.BlockSpec(memory_space=pltpu.VMEM)
    sds = jax.ShapeDtypeStruct

    hbm = pl.BlockSpec(memory_space=pltpu.HBM)
    stay = lambda value: pltpu.with_memory_space_constraint(value, pltpu.HBM)
    dma = pltpu.SemaphoreType.DMA
    turned = [jnp.transpose(a, (1, 0, 2)) for a in (params, first_moment, second_moment)]
    projected, meta = pl.pallas_call(
        functools.partial(project_kernel, peers),
        out_shape=(sds((NPROJ, blocks, lanes), f32), sds((2 * peers,), jnp.int32)),
        in_specs=[hbm, hbm, hbm],
        out_specs=(vmem, smem),
        scratch_shapes=[
            pltpu.VMEM((rows, blocks, lanes), f32),
            pltpu.SMEM(view_basis.shape, f32),
            pltpu.SMEM(tile_blocks.shape, jnp.int32),
            dma((6,)),
        ],
        compiler_params=pltpu.CompilerParams(vmem_limit_bytes=2 << 20),
        name="project",
    )(stay(view_basis), stay(tile_blocks), stay(turned[0]))
    def swapped(value, d):
        return lax.ppermute(value, "tile", [(i, i ^ d) for i in range(peers)])

    regions = lax.axis_size("region")
    onward = lambda value: lax.ppermute(value, "region", [(i, (i + 1) % regions) for i in range(regions)])

    away = {0: projected}
    for d in range(1, peers):
        away[d] = swapped(projected, d)
    held, away[peers - 1] = lax.optimization_barrier((moving, away[peers - 1]))
    leaving, state = pl.pallas_call(
        pack_kernel,
        out_shape=(sds((3 * rows + 1, moves, lanes), f32), sds((3 * rows, blocks, lanes), f32)),
        in_specs=[hbm] * 4,
        out_specs=(vmem, vmem),
        scratch_shapes=[pltpu.SMEM(moving.shape, jnp.int32), dma((3 * PIECES + 1,))],
        compiler_params=pltpu.CompilerParams(vmem_limit_bytes=4 << 20),
        cost_estimate=pl.CostEstimate(flops=0, transcendentals=0, bytes_accessed=4 * 3 * rows * lanes * (2 * blocks + moves)),
        name="pack",
    )(stay(held), *[stay(a) for a in turned])
    came = onward(leaving)
    image, slots = pl.pallas_call(
        composite_kernel,
        out_shape=(sds((3, chunks, lanes), f32), sds((peers, GRADS, lanes), f32)),
        in_specs=[smem] + [vmem] * (peers + 1),
        out_specs=(vmem, vmem),
        scratch_shapes=[
            pltpu.VMEM((listed, GRADS, lanes), f32),
            pltpu.VMEM((5, width + 8, lanes), f32),
            pltpu.VMEM((chunks * width, lanes), f32),
            pltpu.VMEM((chunks * (width + 8), lanes), f32),
            pltpu.VMEM((chunks * (width + 8), lanes), f32),
            pltpu.VMEM((chunks * width, lanes), f32),
            pltpu.VMEM((8 * chunks, lanes), f32),
            pltpu.VMEM((NPROJ, width + 8, lanes), f32),
            pltpu.VMEM((listed, GRADS, lanes), f32),
            pltpu.VMEM((48, (chunks + 5) * lanes), jnp.bfloat16),
            pltpu.VMEM((width, 48), jnp.bfloat16),
        ],
        compiler_params=pltpu.CompilerParams(vmem_limit_bytes=(4 * chunks + 20) * (width + 8) * lanes * 4 + (3 << 20)),
        name="composite",
    )(meta, *[away[d] for d in reversed(range(peers))], target.reshape(3, chunks, lanes))
    passed = onward(slots)
    mixed, slope = pl.pallas_call(
        prepare_kernel,
        out_shape=(sds((3 * rows, blocks, lanes), f32), sds((TERMS + 2, blocks, lanes), f32)),
        in_specs=[smem, smem, vmem, vmem],
        out_specs=(vmem, vmem),
        scratch_shapes=[pltpu.VMEM((8, blocks, lanes), f32)],
        compiler_params=pltpu.CompilerParams(vmem_limit_bytes=5 << 20),
        name="prepare",
    )(moving, view_basis, state, came)
    pairs = jnp.stack([slots, passed], axis=1)
    gathered = {0: pairs[0]}
    for d in range(1, peers):
        gathered[d] = swapped(pairs[d], d)
    updated = pl.pallas_call(
        update_kernel,
        out_shape=(sds((rows, blocks, lanes), f32),) * 3 + (sds(image.shape, f32),),
        in_specs=[smem] + [vmem] * (3 + peers),
        out_specs=(hbm,) * 4,
        scratch_shapes=[pltpu.VMEM((rows, blocks, lanes), f32)] * 3 + [dma((12,)), dma((1,))],
        compiler_params=pltpu.CompilerParams(vmem_limit_bytes=5 << 20),
        name="update",
    )(view_basis, mixed, slope, image, *[gathered[d] for d in reversed(range(peers))])
    turned_back = [jnp.transpose(a, (1, 0, 2)) for a in updated[:3]]
    return (*turned_back, updated[3].reshape(1, 3, pixels))


def solution(mesh):
    three = P(("region", "tile"), None, None)
    two = P(("region", "tile"), None)
    return jax.shard_map(
        on_device,
        mesh=mesh,
        in_specs=(three, three, three, P(), three, two, two),
        out_specs=(three, three, three, three),
        check_vma=False,
    )
```

```python
import functools
import math
import jax
import jax.numpy as jnp
import numpy as np
from jax import lax
from jax.experimental import pallas as pl
from jax.experimental.pallas import tpu as pltpu
from jax.sharding import PartitionSpec as P

SH = 16
TILE_SIDE = 32
NPROJ = 9
GRADS = 16
HALF = TILE_SIDE / 2.0

beta_one = 0.9
beta_two = 0.999
adam_eps = 1e-08
adam_step = 10.0
LOG2E = math.log2(math.e)


def rate_of(row):
    if row < 3:
        return 0.002
    if row < 6:
        return 0.005
    if row < 10:
        return 0.001
    if row < 11:
        return 0.05
    return 0.0025


def sigmoid(x):
    return 1.0 / (1.0 + jnp.exp(-x))


def geometry(p):
    v = {}
    v["tx"] = jnp.tanh(p(0))
    v["ty"] = jnp.tanh(p(1))
    depth = p(2)
    softplus = jnp.maximum(depth, 0.0) + jnp.log(1.0 + jnp.exp(-jnp.abs(depth)))
    v["f"] = 3.0 / (1.0 + softplus)
    v["z"] = v["f"] * v["f"]
    v["ts"] = [jnp.tanh(p(3 + k)) for k in range(3)]
    v["e"] = [2.25 * jnp.exp(2.0 * t) for t in v["ts"]]
    q = [p(6 + k) for k in range(4)]
    norm = jnp.sqrt((q[0] * q[0] + q[1] * q[1]) + (q[2] * q[2] + q[3] * q[3]))
    inv = 1.0 / jnp.maximum(norm, 1.0)
    v["norm"] = norm
    v["inv"] = inv
    w, x, y, z = [a * inv for a in q]
    v["q"] = (w, x, y, z)
    U = [1.0 - 2.0 * (y * y + z * z), 2.0 * (x * y - w * z), 2.0 * (x * z + w * y)]
    L = [2.0 * (x * y + w * z), 1.0 - 2.0 * (x * x + z * z), 2.0 * (y * z - w * x)]
    v["U"], v["L"] = U, L
    e = v["e"]
    v["sxx"] = U[0] * U[0] * e[0] + U[1] * U[1] * e[1] + U[2] * U[2] * e[2]
    v["syy"] = L[0] * L[0] * e[0] + L[1] * L[1] * e[1] + L[2] * L[2] * e[2]
    v["sxy"] = U[0] * L[0] * e[0] + U[1] * L[1] * e[1] + U[2] * L[2] * e[2]
    v["xx"] = v["z"] * v["sxx"] + 0.3
    v["yy"] = v["z"] * v["syy"] + 0.3
    v["xy"] = v["z"] * v["sxy"]
    v["idet"] = 1.0 / (v["xx"] * v["yy"] - v["xy"] * v["xy"])
    v["A"] = v["yy"] * v["idet"]
    v["B"] = -v["xy"] * v["idet"]
    v["C"] = v["xx"] * v["idet"]
    v["so"] = sigmoid(p(10) - 4.0)
    return v


def colour(p, c, basis):
    total = p(11 + SH * c) * basis(0)
    for k in range(1, SH):
        total = total + p(11 + SH * c + k) * basis(k)
    return sigmoid(total)


def project_kernel(basis_hbm, p_hbm, proj_ref, p_ref, basis_ref, sems):
    head = 11
    copies = [
        pltpu.make_async_copy(p_hbm.at[:head], p_ref.at[:head], sems.at[0]),
        pltpu.make_async_copy(basis_hbm, basis_ref, sems.at[1]),
    ]
    for c in range(3):
        span = pl.ds(head + SH * c, SH)
        copies.append(pltpu.make_async_copy(p_hbm.at[span], p_ref.at[span], sems.at[2 + c]))
    for copy in copies:
        copy.start()
    p = lambda i: p_ref[i]
    copies[0].wait()
    v = geometry(p)
    proj_ref[0] = 0.375 * TILE_SIDE * v["tx"]
    proj_ref[1] = 0.375 * TILE_SIDE * v["ty"]
    proj_ref[2] = v["A"]
    proj_ref[3] = v["B"]
    proj_ref[4] = v["C"]
    proj_ref[5] = 0.99 * v["so"]
    copies[1].wait()
    for c in range(3):
        copies[2 + c].wait()
        proj_ref[6 + c] = colour(p, c, lambda k: basis_ref[k])


def picks(moving_ref, blocks, lanes):
    slot = lax.broadcasted_iota(jnp.int32, (blocks, lanes), 0)
    source = jnp.zeros((blocks, lanes), jnp.int32)
    taken = jnp.zeros((blocks, lanes), jnp.bool_)
    for m in range(moving_ref.shape[1]):
        here = slot == moving_ref[0, m]
        source = jnp.where(here, m, source)
        taken = jnp.logical_or(taken, here)
    return source, taken


PIECES = 4


def pieces(rows):
    cuts = [rows * n // PIECES for n in range(PIECES + 1)]
    return list(zip(cuts[:-1], cuts[1:]))


def pack_kernel(moving_hbm, listed_hbm, p_hbm, f_hbm, s_hbm, leave_ref, state_ref, moving_ref, listed_ref, sems):
    total, moves, lanes = leave_ref.shape
    rows, blocks, _ = p_hbm.shape
    ids = pltpu.make_async_copy(moving_hbm, moving_ref, sems.at[3 * PIECES])
    ids.start()
    lists = pltpu.make_async_copy(listed_hbm, listed_ref, sems.at[3 * PIECES + 1])
    lists.start()
    spans = []
    copies = []
    for a, ref in enumerate((p_hbm, f_hbm, s_hbm)):
        for low, high in pieces(rows):
            span = (a * rows + low, a * rows + high)
            copy = pltpu.make_async_copy(ref.at[low:high], state_ref.at[span[0] : span[1]], sems.at[len(copies)])
            copy.start()
            spans.append(span)
            copies.append(copy)
    ids.wait()
    lists.wait()
    slot = lax.broadcasted_iota(jnp.int32, (blocks, lanes), 0)
    pick = jnp.zeros((blocks, lanes), jnp.int32)
    for m in range(moves):
        pick = jnp.where(slot == m, moving_ref[0, m], pick)
    leave_ref[total - 1] = pick[:moves].astype(jnp.float32)
    for copy, span in zip(copies, spans):
        copy.wait()
        for i in range(*span):
            leave_ref[i] = jnp.take_along_axis(state_ref[i], pick, axis=0)[:moves]


def split(value):
    high = value.astype(jnp.bfloat16).astype(jnp.float32)
    rest = value - high
    middle = rest.astype(jnp.bfloat16).astype(jnp.float32)
    return high, middle, rest - middle


def composite_kernel(peers, listed_ref, *refs):
    sources = refs[:peers][::-1]
    target_ref = refs[peers]
    image_ref = refs[peers + 1]
    slots_ref = refs[peers + 2]
    pbuf, qbuf, abuf, wbuf, ebuf, shbuf, errbuf, rbuf, gbuf, basis, lbuf = refs[peers + 3 :]
    listed, _, lanes = pbuf.shape
    width = listed * lanes
    groups = width // 8
    chunks = errbuf.shape[0] // 8
    spreads = qbuf.shape[0]
    assert chunks == 8
    blocks = sources[0].shape[1]
    me = lax.axis_index("tile")
    places, ids = [], []
    for d in range(peers):
        pos, loc = jnp.int32(0), jnp.int32(0)
        for n in range(listed):
            named = listed_ref[0, n]
            here = lax.div(named, jnp.int32(blocks)) == jnp.bitwise_xor(me, d)
            pos = jnp.where(here, n, pos)
            loc = jnp.where(here, lax.rem(named, jnp.int32(blocks)), loc)
        places.append(pos)
        ids.append(loc)
        for r in range(NPROJ):
            pbuf[pos, pl.ds(r, 1), :] = sources[d][r, pl.ds(loc, 1), :]

    lane = lax.broadcasted_iota(jnp.int32, (8, lanes), 1)
    which = lax.broadcasted_iota(jnp.int32, (8, lanes), 0)
    px = (lane % TILE_SIDE).astype(jnp.float32) + (0.5 - HALF)
    py = (lane // TILE_SIDE).astype(jnp.float32) + (0.5 - HALF)
    step = float(lanes // TILE_SIDE)
    middle = py + step * ((chunks - 1) / 2.0)
    zero = jnp.zeros((8, lanes), jnp.float32)
    one = zero + 1.0

    def rows(*values):
        out = zero
        for r, value in enumerate(values):
            out = jnp.where(which == r, value, out)
        return out

    blank = jnp.zeros((24, lanes), jnp.bfloat16)
    for c in range(chunks):
        y = py + step * c
        high, low, _ = split(px * y)
        mono = rows(one, px, y, (px * px - 0.25) * 0.5, (y * y - 0.25) * 0.5, high, low)
        part = jnp.concatenate([mono, mono, mono], axis=0).astype(jnp.bfloat16)
        basis[0:24, c * lanes : (c + 1) * lanes] = part
        basis[24:48, c * lanes : (c + 1) * lanes] = blank
    for k in range(spreads):
        pick = jnp.where(which == k, one, zero)
        at = (chunks + k) * lanes
        basis[0:24, at : at + lanes] = blank
        basis[24:48, at : at + lanes] = jnp.concatenate([pick, pick, pick], axis=0).astype(jnp.bfloat16)

    def product(left, right):
        return jnp.dot(left, right, preferred_element_type=jnp.float32)

    def alphas(j, _):
        mx, my, ca, cb, cc, op = [pbuf[j, r : r + 1, :] for r in range(6)]
        a = -0.5 * LOG2E * ca
        b = -LOG2E * cb
        c = -0.5 * LOG2E * cc
        bx = b * mx
        by = b * my
        ax = a * mx
        cy = c * my
        flat = (ax + by) * mx + cy * my + 0.25 * (a + c) + jnp.log(op) * LOG2E
        power = rows(flat, -(2.0 * ax + by), -(2.0 * cy + bx), 2.0 * a, 2.0 * c, b, b)
        plain = rows(mx, my, *[pbuf[j, 6 + k : 7 + k, :] for k in range(3)])
        colours = rows(*[pbuf[j, 6 + k : 7 + k, :] for k in range(3)])
        high, mid, low = split(colours)
        left = jnp.concatenate([*split(power), *split(plain)], axis=0).T.astype(jnp.bfloat16)
        lbuf[pl.ds(pl.multiple_of(j * lanes, lanes), lanes), :] = jnp.concatenate(
            [high, high, mid, mid, high, low], axis=0
        ).T.astype(jnp.bfloat16)
        out = product(left, basis[...])
        for u in range(lanes // 8):
            row = pl.multiple_of(j * lanes + u * 8, 8)
            for n in range(chunks):
                part = out[u * 8 : (u + 1) * 8, n * lanes : (n + 1) * lanes]
                abuf[pl.ds(row * chunks + n * 8, 8), :] = jnp.exp2(part)
            for k in range(spreads):
                qbuf[k, pl.ds(row, 8), :] = out[u * 8 : (u + 1) * 8, (chunks + k) * lanes : (chunks + k + 1) * lanes]
        return 0

    lax.fori_loop(0, listed, alphas, 0, unroll=min(listed, 4))

    batch = 16

    def forward(n, running):
        trans, image = running
        base = pl.multiple_of(n * (batch * chunks), batch * chunks)
        for i in range(batch):
            alpha = abuf[pl.ds(base + (i // 8) * (8 * chunks) + i % 8, chunks, stride=8), :]
            weight = trans * alpha
            trans = trans * (1.0 - alpha)
            wbuf[pl.ds(base + i * chunks, chunks), :] = weight
            image = tuple(
                image[k] + weight * jnp.broadcast_to(qbuf[2 + k, pl.ds(n * batch + i, 1), :], (chunks, lanes))
                for k in range(3)
            )
        return (trans, image)

    _, image = lax.fori_loop(0, width // batch, forward, (one, (zero, zero, zero)))
    for k in range(8):
        if k < 3:
            image_ref[k] = image[k]
            errbuf[k * chunks : (k + 1) * chunks, :] = 2.0 * (image[k] - target_ref[k])
        else:
            errbuf[k * chunks : (k + 1) * chunks, :] = zero
    for c in range(chunks):
        high, mid, low = split(errbuf[pl.ds(c, 8, stride=chunks), :])
        basis[:, c * lanes : (c + 1) * lanes] = jnp.concatenate([high, mid, high, mid, low, high], axis=0).astype(
            jnp.bfloat16
        )

    def shading(j, _):
        out = product(lbuf[pl.ds(pl.multiple_of(j * lanes, lanes), lanes), :], basis[:, : chunks * lanes])
        for u in range(lanes // 8):
            row = pl.multiple_of(j * lanes + u * 8, 8)
            for n in range(chunks):
                shbuf[pl.ds(row * chunks + n * 8, 8), :] = out[u * 8 : (u + 1) * 8, n * lanes : (n + 1) * lanes]
        return 0

    lax.fori_loop(0, listed, shading, 0, unroll=min(listed, 4))
    for buf in (wbuf, ebuf):
        buf[pl.ds(width * chunks, 8 * chunks), :] = jnp.zeros((8 * chunks, lanes), jnp.float32)
    for k in range(2):
        qbuf[k, pl.ds(width, 8), :] = zero

    def reduce_pixels(u):
        row = pl.multiple_of(u * 8, 8)
        base = pl.multiple_of(u * (8 * chunks), 8 * chunks)
        part = [ebuf[pl.ds(base + c, 8, stride=chunks), :] for c in range(chunks)]
        light = [wbuf[pl.ds(base + c, 8, stride=chunks), :] for c in range(chunks)]
        dx = px - qbuf[0, pl.ds(row, 8), :]
        dy = middle - qbuf[1, pl.ds(row, 8), :]
        half = chunks // 2
        away = [((chunks - 1) / 2.0 - c) * step for c in range(half)]
        even = [part[c] + part[chunks - 1 - c] for c in range(half)]
        odd = [part[chunks - 1 - c] - part[c] for c in range(half)]
        plain = (even[0] + even[1]) + (even[2] + even[3])
        tilt = (away[0] * odd[0] + away[1] * odd[1]) + (away[2] * odd[2] + away[3] * odd[3])
        bend = (away[0] ** 2 * even[0] + away[1] ** 2 * even[1]) + (away[2] ** 2 * even[2] + away[3] ** 2 * even[3])
        sum_y = dy * plain + tilt
        sum_yy = dy * (sum_y + tilt) + bend
        sum_x = dx * plain
        sums = [plain, sum_x, sum_y, dx * sum_x, dx * sum_y, sum_yy]
        for k in range(3):
            lit = [light[c] * jnp.broadcast_to(errbuf[pl.ds(k * chunks + c, 1), :], (8, lanes)) for c in range(chunks)]
            sums.append(((lit[0] + lit[1]) + (lit[2] + lit[3])) + ((lit[4] + lit[5]) + (lit[6] + lit[7])))
        for r, value in enumerate(sums):
            rbuf[r, pl.ds(row, 8), :] = value

    def backward(n, behind):
        u = groups - 1 - n
        base = pl.multiple_of(u * (8 * chunks), 8 * chunks)
        reduce_pixels(u + 1)
        for i in reversed(range(8)):
            alpha = abuf[pl.ds(base + i, chunks, stride=8), :]
            ahead = shbuf[pl.ds(base + i, chunks, stride=8), :] - behind
            behind = behind + alpha * ahead
            ebuf[pl.ds(base + i * chunks, chunks), :] = wbuf[pl.ds(base + i * chunks, chunks), :] * ahead
        return behind

    lax.fori_loop(0, groups, backward, zero, unroll=2)
    reduce_pixels(0)

    def finish(j, _):
        at = pl.ds(pl.multiple_of(j * lanes, lanes), lanes)
        part = [jnp.sum(rbuf[r, at, :].T, axis=0, keepdims=True) for r in range(NPROJ)]
        s0, sx, sy, sxx, sxy, syy = part[:6]
        ca, cb, cc, op = [pbuf[j, r : r + 1, :] for r in range(2, 6)]
        gbuf[j, 0:1, :] = ca * sx + cb * sy
        gbuf[j, 1:2, :] = cb * sx + cc * sy
        gbuf[j, 2:3, :] = -0.5 * sxx
        gbuf[j, 3:4, :] = -sxy
        gbuf[j, 4:5, :] = -0.5 * syy
        gbuf[j, 5:6, :] = s0 / op
        for k in range(3):
            gbuf[j, 6 + k : 7 + k, :] = part[6 + k]
        gbuf[j, 9:16, :] = jnp.zeros((7, lanes), jnp.float32)
        return 0

    lax.fori_loop(0, listed, finish, 0, unroll=min(listed, 4))
    for d in range(peers):
        slots_ref[d] = gbuf[places[d]]
        slots_ref[d, NPROJ : NPROJ + 1, :] = jnp.full((1, lanes), 1, jnp.float32) * ids[d].astype(jnp.float32)


TERMS = 2 + 3 * 8 + 1 + 3


def prepare_kernel(moving_ref, basis_ref, state_ref, came_ref, mixed_ref, slope_ref, kbuf):
    total, blocks, lanes = state_ref.shape
    rows = total // 3
    moves = came_ref.shape[1]
    source, taken = picks(moving_ref, blocks, lanes)

    def arrived(i):
        kbuf[i % 8, 0:moves, :] = came_ref[i]
        return jnp.take_along_axis(kbuf[i % 8], source, axis=0)

    for a, factor in enumerate((None, beta_one, beta_two)):
        for i in range(a * rows, (a + 1) * rows):
            value = jnp.where(taken, arrived(i), state_ref[i])
            mixed_ref[i] = value if factor is None else factor * value
    slot = lax.broadcasted_iota(jnp.int32, (blocks, lanes), 0).astype(jnp.float32)
    slope_ref[TERMS] = jnp.where(taken, arrived(total), slot)
    slope_ref[TERMS + 1] = taken.astype(jnp.float32)

    part = 1.0 - beta_one
    p = lambda i: mixed_ref[i]
    v = geometry(p)
    slope_ref[0] = part * 0.375 * TILE_SIDE * (1.0 - v["tx"] * v["tx"])
    slope_ref[1] = part * 0.375 * TILE_SIDE * (1.0 - v["ty"] * v["ty"])
    slope_ref[TERMS - 4] = part * 0.99 * v["so"] * (1.0 - v["so"])
    for c in range(3):
        shade = colour(p, c, lambda k: basis_ref[k])
        slope_ref[TERMS - 3 + c] = part * shade * (1.0 - shade)
    U, L, e, f, idet = v["U"], v["L"], v["e"], v["f"], v["idet"]
    w, x, y, z = v["q"]
    share = jnp.where(v["norm"] > 1.0, 1.0, jnp.where(v["norm"] == 1.0, 0.5, 0.0))
    depth = (-2.0 / 3.0) * f * f * f * sigmoid(p(2)) * part
    for n, name in enumerate("ABC"):
        gdet = -v[name] * idet
        gxx = gdet * v["yy"]
        gyy = gdet * v["xx"]
        gxy = -2.0 * gdet * v["xy"]
        if name == "A":
            gyy = gyy + idet
        elif name == "B":
            gxy = gxy - idet
        else:
            gxx = gxx + idet
        slope_ref[2 + n] = (gxx * v["sxx"] + gyy * v["syy"] + gxy * v["sxy"]) * depth
        gU, gL = [], []
        for k in range(3):
            t = v["ts"][k]
            ze = v["z"] * e[k]
            ge = gxx * U[k] * U[k] + gyy * L[k] * L[k] + gxy * U[k] * L[k]
            slope_ref[5 + 3 * k + n] = (2.0 * part) * ge * ze * (1.0 - t * t)
            gU.append(ze * (2.0 * gxx * U[k] + gxy * L[k]))
            gL.append(ze * (2.0 * gyy * L[k] + gxy * U[k]))
        gq = [
            2.0 * (z * (gL[0] - gU[1]) + y * gU[2] - x * gL[2]),
            2.0 * (y * (gU[1] + gL[0]) + z * gU[2] - 2.0 * x * gL[1] - w * gL[2]),
            2.0 * (x * (gU[1] + gL[0]) - 2.0 * y * gU[0] + w * gU[2] + z * gL[2]),
            2.0 * (w * (gL[0] - gU[1]) - 2.0 * z * (gU[0] + gL[1]) + x * gU[2] + y * gL[2]),
        ]
        along = share * (w * gq[0] + x * gq[1] + y * gq[2] + z * gq[3])
        for k, unit in enumerate((w, x, y, z)):
            slope_ref[14 + 3 * k + n] = part * (gq[k] - unit * along) * v["inv"]


def update_kernel(basis_ref, mixed_ref, slope_ref, image_ref, *refs):
    sources = refs[:-9]
    outs = refs[-9:-6]
    picture_hbm = refs[-6]
    stages = refs[-5:-2]
    sems, picture_sem = refs[-2:]
    total, blocks, lanes = mixed_ref.shape
    rows = total // 3
    picture = pltpu.make_async_copy(image_ref, picture_hbm, picture_sem.at[0])
    picture.start()
    want = slope_ref[TERMS]
    taken = slope_ref[TERMS + 1] > 0.5
    wide = lambda row: jnp.broadcast_to(row, (blocks, lanes))
    grads = [jnp.zeros((blocks, lanes), jnp.float32) for _ in range(NPROJ)]
    for ref in sources:
        for side in range(2):
            mask = jnp.logical_and(want == wide(ref[side, NPROJ : NPROJ + 1, :]), taken if side else ~taken)
            for r in range(NPROJ):
                grads[r] = grads[r] + jnp.where(mask, wide(ref[side, r : r + 1, :]), 0.0)

    def store(i, grad):
        one = mixed_ref[rows + i] + grad
        two = mixed_ref[2 * rows + i] + ((1.0 - beta_two) / (1.0 - beta_one) ** 2) * (grad * grad)
        scaled = (rate_of(i) / (1.0 - beta_one**adam_step)) * one
        stages[0][i] = mixed_ref[i] - scaled / (jnp.sqrt(two * (1.0 / (1.0 - beta_two**adam_step))) + adam_eps)
        stages[1][i] = one
        stages[2][i] = two

    copies = []

    def ship(low, high):
        for a in range(3):
            copy = pltpu.make_async_copy(
                stages[a].at[low:high], outs[a].at[low:high], sems.at[len(copies)]
            )
            copy.start()
            copies.append(copy)

    for c in range(3):
        logit = grads[6 + c] * slope_ref[TERMS - 3 + c]
        for k in range(SH):
            store(11 + SH * c + k, logit * basis_ref[k])
        ship(11 + SH * c, 11 + SH * (c + 1))
    store(0, grads[0] * slope_ref[0])
    store(1, grads[1] * slope_ref[1])
    for i in range(8):
        at = 2 + 3 * i
        store(2 + i, grads[2] * slope_ref[at] + grads[3] * slope_ref[at + 1] + grads[4] * slope_ref[at + 2])
    store(10, grads[5] * slope_ref[TERMS - 4])
    ship(0, 11)
    for copy in copies:
        copy.wait()
    picture.wait()


def on_device(params, first_moment, second_moment, view_basis, target, tile_blocks, moving):
    blocks, rows, lanes = params.shape
    peers = lax.axis_size("tile")
    listed = tile_blocks.shape[1]
    moves = moving.shape[1]
    pixels = target.shape[2]
    chunks = pixels // lanes
    width = listed * lanes
    f32 = jnp.float32
    smem = pl.BlockSpec(memory_space=pltpu.SMEM)
    vmem = pl.BlockSpec(memory_space=pltpu.VMEM)
    sds = jax.ShapeDtypeStruct

    hbm = pl.BlockSpec(memory_space=pltpu.HBM)
    stay = lambda value: pltpu.with_memory_space_constraint(value, pltpu.HBM)
    dma = pltpu.SemaphoreType.DMA
    turned = [jnp.transpose(a, (1, 0, 2)) for a in (params, first_moment, second_moment)]
    projected = pl.pallas_call(
        project_kernel,
        out_shape=sds((NPROJ, blocks, lanes), f32),
        in_specs=[hbm, hbm],
        out_specs=vmem,
        scratch_shapes=[pltpu.VMEM((rows, blocks, lanes), f32), pltpu.SMEM(view_basis.shape, f32), dma((5,))],
        compiler_params=pltpu.CompilerParams(vmem_limit_bytes=2 << 20),
        name="project",
    )(stay(view_basis), stay(turned[0]))

    def swapped(value, d):
        return lax.ppermute(value, "tile", [(i, i ^ d) for i in range(peers)])

    regions = lax.axis_size("region")
    onward = lambda value: lax.ppermute(value, "region", [(i, (i + 1) % regions) for i in range(regions)])

    leaving, state, moved, named = pl.pallas_call(
        pack_kernel,
        out_shape=(
            sds((3 * rows + 1, moves, lanes), f32),
            sds((3 * rows, blocks, lanes), f32),
            sds(moving.shape, jnp.int32),
            sds(tile_blocks.shape, jnp.int32),
        ),
        in_specs=[hbm] * 5,
        out_specs=(vmem, vmem, smem, smem),
        scratch_shapes=[dma((3 * PIECES + 2,))],
        compiler_params=pltpu.CompilerParams(vmem_limit_bytes=4 << 20),
        name="pack",
    )(stay(moving), stay(tile_blocks), *[stay(a) for a in turned])
    away = {0: projected}
    for d in range(1, peers):
        away[d] = swapped(projected, d)
    leaving, *rest = lax.optimization_barrier((leaving, *[away[d] for d in range(1, peers)]))
    for d in range(1, peers):
        away[d] = rest[d - 1]
    came = onward(leaving)
    image, slots = pl.pallas_call(
        functools.partial(composite_kernel, peers),
        out_shape=(sds((3, chunks, lanes), f32), sds((peers, GRADS, lanes), f32)),
        in_specs=[smem] + [vmem] * (peers + 1),
        out_specs=(vmem, vmem),
        scratch_shapes=[
            pltpu.VMEM((listed, GRADS, lanes), f32),
            pltpu.VMEM((5, width + 8, lanes), f32),
            pltpu.VMEM((chunks * width, lanes), f32),
            pltpu.VMEM((chunks * (width + 8), lanes), f32),
            pltpu.VMEM((chunks * (width + 8), lanes), f32),
            pltpu.VMEM((chunks * width, lanes), f32),
            pltpu.VMEM((8 * chunks, lanes), f32),
            pltpu.VMEM((NPROJ, width + 8, lanes), f32),
            pltpu.VMEM((listed, GRADS, lanes), f32),
            pltpu.VMEM((48, (chunks + 5) * lanes), jnp.bfloat16),
            pltpu.VMEM((width, 48), jnp.bfloat16),
        ],
        compiler_params=pltpu.CompilerParams(vmem_limit_bytes=(4 * chunks + 20) * (width + 8) * lanes * 4 + (3 << 20)),
        cost_estimate=pl.CostEstimate(
            flops=64 * width * pixels, transcendentals=width * pixels, bytes_accessed=48 * width * pixels
        ),
        name="composite",
    )(named, *[away[d] for d in reversed(range(peers))], target.reshape(3, chunks, lanes))
    passed = onward(slots)
    mixed, slope = pl.pallas_call(
        prepare_kernel,
        out_shape=(sds((3 * rows, blocks, lanes), f32), sds((TERMS + 2, blocks, lanes), f32)),
        in_specs=[smem, smem, vmem, vmem],
        out_specs=(vmem, vmem),
        scratch_shapes=[pltpu.VMEM((8, blocks, lanes), f32)],
        compiler_params=pltpu.CompilerParams(vmem_limit_bytes=5 << 20),
        name="prepare",
    )(moved, view_basis, state, came)
    pairs = jnp.stack([slots, passed], axis=1)
    gathered = {0: pairs[0]}
    for d in range(1, peers):
        gathered[d] = swapped(pairs[d], d)
    updated = pl.pallas_call(
        update_kernel,
        out_shape=(sds((rows, blocks, lanes), f32),) * 3 + (sds(image.shape, f32),),
        in_specs=[smem] + [vmem] * (3 + peers),
        out_specs=(hbm,) * 4,
        scratch_shapes=[pltpu.VMEM((rows, blocks, lanes), f32)] * 3 + [dma((12,)), dma((1,))],
        compiler_params=pltpu.CompilerParams(vmem_limit_bytes=5 << 20),
        name="update",
    )(view_basis, mixed, slope, image, *[gathered[d] for d in reversed(range(peers))])
    turned_back = [jnp.transpose(a, (1, 0, 2)) for a in updated[:3]]
    return (*turned_back, updated[3].reshape(1, 3, pixels))


def solution(mesh):
    three = P(("region", "tile"), None, None)
    two = P(("region", "tile"), None)
    return jax.shard_map(
        on_device,
        mesh=mesh,
        in_specs=(three, three, three, P(), three, two, two),
        out_specs=(three, three, three, three),
        check_vma=False,
    )
```

```python
import functools
import math
import jax
import jax.numpy as jnp
import numpy as np
from jax import lax
from jax.experimental import pallas as pl
from jax.experimental.pallas import tpu as pltpu
from jax.sharding import PartitionSpec as P

SH = 16
TILE_SIDE = 32
NPROJ = 9
GRADS = 16
HALF = TILE_SIDE / 2.0

beta_one = 0.9
beta_two = 0.999
adam_eps = 1e-08
adam_step = 10.0
LOG2E = math.log2(math.e)


def rate_of(row):
    if row < 3:
        return 0.002
    if row < 6:
        return 0.005
    if row < 10:
        return 0.001
    if row < 11:
        return 0.05
    return 0.0025


def sigmoid(x):
    return 1.0 / (1.0 + jnp.exp(-x))


def geometry(p):
    v = {}
    v["tx"] = jnp.tanh(p(0))
    v["ty"] = jnp.tanh(p(1))
    depth = p(2)
    softplus = jnp.maximum(depth, 0.0) + jnp.log(1.0 + jnp.exp(-jnp.abs(depth)))
    v["f"] = 3.0 / (1.0 + softplus)
    v["z"] = v["f"] * v["f"]
    v["ts"] = [jnp.tanh(p(3 + k)) for k in range(3)]
    v["e"] = [2.25 * jnp.exp(2.0 * t) for t in v["ts"]]
    q = [p(6 + k) for k in range(4)]
    norm = jnp.sqrt((q[0] * q[0] + q[1] * q[1]) + (q[2] * q[2] + q[3] * q[3]))
    inv = 1.0 / jnp.maximum(norm, 1.0)
    v["norm"] = norm
    v["inv"] = inv
    w, x, y, z = [a * inv for a in q]
    v["q"] = (w, x, y, z)
    U = [1.0 - 2.0 * (y * y + z * z), 2.0 * (x * y - w * z), 2.0 * (x * z + w * y)]
    L = [2.0 * (x * y + w * z), 1.0 - 2.0 * (x * x + z * z), 2.0 * (y * z - w * x)]
    v["U"], v["L"] = U, L
    e = v["e"]
    v["sxx"] = U[0] * U[0] * e[0] + U[1] * U[1] * e[1] + U[2] * U[2] * e[2]
    v["syy"] = L[0] * L[0] * e[0] + L[1] * L[1] * e[1] + L[2] * L[2] * e[2]
    v["sxy"] = U[0] * L[0] * e[0] + U[1] * L[1] * e[1] + U[2] * L[2] * e[2]
    v["xx"] = v["z"] * v["sxx"] + 0.3
    v["yy"] = v["z"] * v["syy"] + 0.3
    v["xy"] = v["z"] * v["sxy"]
    v["idet"] = 1.0 / (v["xx"] * v["yy"] - v["xy"] * v["xy"])
    v["A"] = v["yy"] * v["idet"]
    v["B"] = -v["xy"] * v["idet"]
    v["C"] = v["xx"] * v["idet"]
    v["so"] = sigmoid(p(10) - 4.0)
    return v


def colour(p, c, basis):
    total = p(11 + SH * c) * basis(0)
    for k in range(1, SH):
        total = total + p(11 + SH * c + k) * basis(k)
    return sigmoid(total)


def project_kernel(basis_hbm, p_hbm, proj_ref, p_ref, basis_ref, sems):
    head = 11
    copies = [
        pltpu.make_async_copy(p_hbm.at[:head], p_ref.at[:head], sems.at[0]),
        pltpu.make_async_copy(basis_hbm, basis_ref, sems.at[1]),
    ]
    for c in range(3):
        span = pl.ds(head + SH * c, SH)
        copies.append(pltpu.make_async_copy(p_hbm.at[span], p_ref.at[span], sems.at[2 + c]))
    for copy in copies:
        copy.start()
    p = lambda i: p_ref[i]
    copies[0].wait()
    v = geometry(p)
    proj_ref[0] = 0.375 * TILE_SIDE * v["tx"]
    proj_ref[1] = 0.375 * TILE_SIDE * v["ty"]
    proj_ref[2] = v["A"]
    proj_ref[3] = v["B"]
    proj_ref[4] = v["C"]
    proj_ref[5] = 0.99 * v["so"]
    copies[1].wait()
    for c in range(3):
        copies[2 + c].wait()
        proj_ref[6 + c] = colour(p, c, lambda k: basis_ref[k])


def picks(moving_ref, blocks, lanes):
    slot = lax.broadcasted_iota(jnp.int32, (blocks, lanes), 0)
    source = jnp.zeros((blocks, lanes), jnp.int32)
    taken = jnp.zeros((blocks, lanes), jnp.bool_)
    for m in range(moving_ref.shape[1]):
        here = slot == moving_ref[0, m]
        source = jnp.where(here, m, source)
        taken = jnp.logical_or(taken, here)
    return source, taken


PIECES = 4


def pieces(rows):
    cuts = [rows * n // PIECES for n in range(PIECES + 1)]
    return list(zip(cuts[:-1], cuts[1:]))


def pack_kernel(moving_hbm, listed_hbm, p_hbm, f_hbm, s_hbm, leave_ref, state_ref, moving_ref, listed_ref, sems):
    total, moves, lanes = leave_ref.shape
    rows, blocks, _ = p_hbm.shape
    ids = pltpu.make_async_copy(moving_hbm, moving_ref, sems.at[3 * PIECES])
    ids.start()
    lists = pltpu.make_async_copy(listed_hbm, listed_ref, sems.at[3 * PIECES + 1])
    lists.start()
    spans = []
    copies = []
    for a, ref in enumerate((p_hbm, f_hbm, s_hbm)):
        for low, high in pieces(rows):
            span = (a * rows + low, a * rows + high)
            copy = pltpu.make_async_copy(ref.at[low:high], state_ref.at[span[0] : span[1]], sems.at[len(copies)])
            copy.start()
            spans.append(span)
            copies.append(copy)
    ids.wait()
    lists.wait()
    slot = lax.broadcasted_iota(jnp.int32, (blocks, lanes), 0)
    pick = jnp.zeros((blocks, lanes), jnp.int32)
    for m in range(moves):
        pick = jnp.where(slot == m, moving_ref[0, m], pick)
    leave_ref[total - 1] = pick[:moves].astype(jnp.float32)
    for copy, span in zip(copies, spans):
        copy.wait()
        for i in range(*span):
            leave_ref[i] = jnp.take_along_axis(state_ref[i], pick, axis=0)[:moves]


def split(value):
    high = value.astype(jnp.bfloat16).astype(jnp.float32)
    rest = value - high
    middle = rest.astype(jnp.bfloat16).astype(jnp.float32)
    return high, middle, rest - middle


def composite_kernel(peers, listed_ref, *refs):
    sources = refs[:peers][::-1]
    target_ref = refs[peers]
    image_ref = refs[peers + 1]
    slots_ref = refs[peers + 2]
    pbuf, qbuf, abuf, wbuf, ebuf, shbuf, errbuf, rbuf, gbuf, basis, lbuf = refs[peers + 3 :]
    listed, _, lanes = pbuf.shape
    width = listed * lanes
    groups = width // 8
    chunks = errbuf.shape[0] // 8
    spreads = qbuf.shape[0]
    assert chunks == 8
    blocks = sources[0].shape[1]
    me = lax.axis_index("tile")
    places, ids = [], []
    for d in range(peers):
        pos, loc = jnp.int32(0), jnp.int32(0)
        for n in range(listed):
            named = listed_ref[0, n]
            here = lax.div(named, jnp.int32(blocks)) == jnp.bitwise_xor(me, d)
            pos = jnp.where(here, n, pos)
            loc = jnp.where(here, lax.rem(named, jnp.int32(blocks)), loc)
        places.append(pos)
        ids.append(loc)
        for r in range(NPROJ):
            pbuf[pos, pl.ds(r, 1), :] = sources[d][r, pl.ds(loc, 1), :]

    lane = lax.broadcasted_iota(jnp.int32, (8, lanes), 1)
    which = lax.broadcasted_iota(jnp.int32, (8, lanes), 0)
    px = (lane % TILE_SIDE).astype(jnp.float32) + (0.5 - HALF)
    py = (lane // TILE_SIDE).astype(jnp.float32) + (0.5 - HALF)
    step = float(lanes // TILE_SIDE)
    middle = py + step * ((chunks - 1) / 2.0)
    zero = jnp.zeros((8, lanes), jnp.float32)
    one = zero + 1.0

    def rows(*values):
        out = zero
        for r, value in enumerate(values):
            out = jnp.where(which == r, value, out)
        return out

    blank = jnp.zeros((24, lanes), jnp.bfloat16)
    for c in range(chunks):
        y = py + step * c
        high, low, _ = split(px * y)
        mono = rows(one, px, y, (px * px - 0.25) * 0.5, (y * y - 0.25) * 0.5, high, low)
        part = jnp.concatenate([mono, mono, mono], axis=0).astype(jnp.bfloat16)
        basis[0:24, c * lanes : (c + 1) * lanes] = part
        basis[24:48, c * lanes : (c + 1) * lanes] = blank
    for k in range(spreads):
        pick = jnp.where(which == k, one, zero)
        at = (chunks + k) * lanes
        basis[0:24, at : at + lanes] = blank
        basis[24:48, at : at + lanes] = jnp.concatenate([pick, pick, pick], axis=0).astype(jnp.bfloat16)

    def product(left, right):
        return jnp.dot(left, right, preferred_element_type=jnp.float32)

    def alphas(j, _):
        mx, my, ca, cb, cc, op = [pbuf[j, r : r + 1, :] for r in range(6)]
        a = -0.5 * LOG2E * ca
        b = -LOG2E * cb
        c = -0.5 * LOG2E * cc
        bx = b * mx
        by = b * my
        ax = a * mx
        cy = c * my
        flat = (ax + by) * mx + cy * my + 0.25 * (a + c) + jnp.log(op) * LOG2E
        power = rows(flat, -(2.0 * ax + by), -(2.0 * cy + bx), 2.0 * a, 2.0 * c, b, b)
        plain = rows(mx, my, *[pbuf[j, 6 + k : 7 + k, :] for k in range(3)])
        colours = rows(*[pbuf[j, 6 + k : 7 + k, :] for k in range(3)])
        high, mid, low = split(colours)
        left = jnp.concatenate([*split(power), *split(plain)], axis=0).T.astype(jnp.bfloat16)
        lbuf[pl.ds(pl.multiple_of(j * lanes, lanes), lanes), :] = jnp.concatenate(
            [high, high, mid, mid, high, low], axis=0
        ).T.astype(jnp.bfloat16)
        out = product(left, basis[...])
        for u in range(lanes // 8):
            row = pl.multiple_of(j * lanes + u * 8, 8)
            for n in range(chunks):
                part = out[u * 8 : (u + 1) * 8, n * lanes : (n + 1) * lanes]
                abuf[pl.ds(row * chunks + n * 8, 8), :] = jnp.exp2(part)
            for k in range(spreads):
                qbuf[k, pl.ds(row, 8), :] = out[u * 8 : (u + 1) * 8, (chunks + k) * lanes : (chunks + k + 1) * lanes]
        return 0

    lax.fori_loop(0, listed, alphas, 0, unroll=min(listed, 4))

    batch = 32

    def forward(n, running):
        trans, image = running
        base = pl.multiple_of(n * (batch * chunks), batch * chunks)
        for i in range(batch):
            alpha = abuf[pl.ds(base + (i // 8) * (8 * chunks) + i % 8, chunks, stride=8), :]
            weight = trans * alpha
            trans = trans * (1.0 - alpha)
            wbuf[pl.ds(base + i * chunks, chunks), :] = weight
            image = tuple(
                image[k] + weight * jnp.broadcast_to(qbuf[2 + k, pl.ds(n * batch + i, 1), :], (chunks, lanes))
                for k in range(3)
            )
        return (trans, image)

    _, image = lax.fori_loop(0, width // batch, forward, (one, (zero, zero, zero)))
    for k in range(8):
        if k < 3:
            image_ref[k] = image[k]
            errbuf[k * chunks : (k + 1) * chunks, :] = 2.0 * (image[k] - target_ref[k])
        else:
            errbuf[k * chunks : (k + 1) * chunks, :] = zero
    for c in range(chunks):
        high, mid, low = split(errbuf[pl.ds(c, 8, stride=chunks), :])
        basis[:, c * lanes : (c + 1) * lanes] = jnp.concatenate([high, mid, high, mid, low, high], axis=0).astype(
            jnp.bfloat16
        )

    def shading(j, _):
        out = product(lbuf[pl.ds(pl.multiple_of(j * lanes, lanes), lanes), :], basis[:, : chunks * lanes])
        for u in range(lanes // 8):
            row = pl.multiple_of(j * lanes + u * 8, 8)
            for n in range(chunks):
                shbuf[pl.ds(row * chunks + n * 8, 8), :] = out[u * 8 : (u + 1) * 8, n * lanes : (n + 1) * lanes]
        return 0

    lax.fori_loop(0, listed, shading, 0, unroll=min(listed, 4))
    for buf in (wbuf, ebuf):
        buf[pl.ds(width * chunks, 8 * chunks), :] = jnp.zeros((8 * chunks, lanes), jnp.float32)
    for k in range(2):
        qbuf[k, pl.ds(width, 8), :] = zero

    def reduce_pixels(u):
        row = pl.multiple_of(u * 8, 8)
        base = pl.multiple_of(u * (8 * chunks), 8 * chunks)
        part = [ebuf[pl.ds(base + c, 8, stride=chunks), :] for c in range(chunks)]
        dx = px - qbuf[0, pl.ds(row, 8), :]
        dy = middle - qbuf[1, pl.ds(row, 8), :]
        half = chunks // 2
        away = [((chunks - 1) / 2.0 - c) * step for c in range(half)]
        even = [part[c] + part[chunks - 1 - c] for c in range(half)]
        odd = [part[chunks - 1 - c] - part[c] for c in range(half)]
        plain = (even[0] + even[1]) + (even[2] + even[3])
        tilt = (away[0] * odd[0] + away[1] * odd[1]) + (away[2] * odd[2] + away[3] * odd[3])
        bend = (away[0] ** 2 * even[0] + away[1] ** 2 * even[1]) + (away[2] ** 2 * even[2] + away[3] ** 2 * even[3])
        sum_y = dy * plain + tilt
        sum_yy = dy * (sum_y + tilt) + bend
        sum_x = dx * plain
        sums = [plain, sum_x, sum_y, dx * sum_x, dx * sum_y, sum_yy]
        for r, value in enumerate(sums):
            rbuf[r, pl.ds(row, 8), :] = value

    def backward(n, behind):
        u = groups - 1 - n
        base = pl.multiple_of(u * (8 * chunks), 8 * chunks)
        reduce_pixels(u + 1)
        for i in reversed(range(8)):
            alpha = abuf[pl.ds(base + i, chunks, stride=8), :]
            shade = shbuf[pl.ds(base + i, chunks, stride=8), :]
            weight = wbuf[pl.ds(base + i * chunks, chunks), :]
            ebuf[pl.ds(base + i * chunks, chunks), :] = weight * (shade - behind)
            behind = (1.0 - alpha) * behind + alpha * shade
        return behind

    lax.fori_loop(0, groups, backward, zero, unroll=16)
    reduce_pixels(0)

    def finish(j, _):
        at = pl.ds(pl.multiple_of(j * lanes, lanes), lanes)
        part = [jnp.sum(rbuf[r, at, :].T, axis=0, keepdims=True) for r in range(6)]
        first = pl.multiple_of(j * lanes * chunks, lanes * chunks)
        lights = [wbuf[pl.ds(first + c, lanes, stride=chunks), :] for c in range(chunks)]
        lit = jnp.zeros((lanes, 48), jnp.float32)
        for n in range(2):
            terms = [light.astype(jnp.bfloat16) for light in lights]
            lights = [light - term.astype(jnp.float32) for light, term in zip(lights, terms)]
            lit = lit + lax.dot_general(
                jnp.concatenate(terms, axis=1),
                basis[:, : chunks * lanes],
                (((1,), (1,)), ((), ())),
                preferred_element_type=jnp.float32,
            )
        lit = lit.T
        part += [lit[k : k + 1] + lit[8 + k : 9 + k] + lit[32 + k : 33 + k] for k in range(3)]
        s0, sx, sy, sxx, sxy, syy = part[:6]
        ca, cb, cc, op = [pbuf[j, r : r + 1, :] for r in range(2, 6)]
        gbuf[j, 0:1, :] = ca * sx + cb * sy
        gbuf[j, 1:2, :] = cb * sx + cc * sy
        gbuf[j, 2:3, :] = -0.5 * sxx
        gbuf[j, 3:4, :] = -sxy
        gbuf[j, 4:5, :] = -0.5 * syy
        gbuf[j, 5:6, :] = s0 / op
        for k in range(3):
            gbuf[j, 6 + k : 7 + k, :] = part[6 + k]
        gbuf[j, 9:16, :] = jnp.zeros((7, lanes), jnp.float32)
        return 0

    lax.fori_loop(0, listed, finish, 0, unroll=min(listed, 4))
    for d in range(peers):
        slots_ref[d] = gbuf[places[d]]
        slots_ref[d, NPROJ : NPROJ + 1, :] = jnp.full((1, lanes), 1, jnp.float32) * ids[d].astype(jnp.float32)


TERMS = 2 + 3 * 8 + 1 + 3 * SH


def prepare_kernel(moving_ref, basis_hbm, state_ref, came_ref, mixed_ref, slope_ref, kbuf, basis_ref, sem):
    fetch = pltpu.make_async_copy(basis_hbm, basis_ref, sem.at[0])
    fetch.start()
    total, blocks, lanes = state_ref.shape
    rows = total // 3
    moves = came_ref.shape[1]
    source, taken = picks(moving_ref, blocks, lanes)

    def arrived(i):
        kbuf[i % 8, 0:moves, :] = came_ref[i]
        return jnp.take_along_axis(kbuf[i % 8], source, axis=0)

    for a, factor in enumerate((None, beta_one, beta_two)):
        for i in range(a * rows, (a + 1) * rows):
            value = jnp.where(taken, arrived(i), state_ref[i])
            mixed_ref[i] = value if factor is None else factor * value
    slot = lax.broadcasted_iota(jnp.int32, (blocks, lanes), 0).astype(jnp.float32)
    slope_ref[TERMS] = jnp.where(taken, arrived(total), slot)
    slope_ref[TERMS + 1] = taken.astype(jnp.float32)

    part = 1.0 - beta_one
    p = lambda i: mixed_ref[i]
    v = geometry(p)
    slope_ref[0] = part * 0.375 * TILE_SIDE * (1.0 - v["tx"] * v["tx"])
    slope_ref[1] = part * 0.375 * TILE_SIDE * (1.0 - v["ty"] * v["ty"])
    slope_ref[26] = part * 0.99 * v["so"] * (1.0 - v["so"])
    fetch.wait()
    for c in range(3):
        shade = colour(p, c, lambda k: basis_ref[k])
        rise = part * shade * (1.0 - shade)
        for k in range(SH):
            slope_ref[27 + SH * c + k] = rise * basis_ref[k]
    U, L, e, f, idet = v["U"], v["L"], v["e"], v["f"], v["idet"]
    w, x, y, z = v["q"]
    share = jnp.where(v["norm"] > 1.0, 1.0, jnp.where(v["norm"] == 1.0, 0.5, 0.0))
    depth = (-2.0 / 3.0) * f * f * f * sigmoid(p(2)) * part
    for n, name in enumerate("ABC"):
        gdet = -v[name] * idet
        gxx = gdet * v["yy"]
        gyy = gdet * v["xx"]
        gxy = -2.0 * gdet * v["xy"]
        if name == "A":
            gyy = gyy + idet
        elif name == "B":
            gxy = gxy - idet
        else:
            gxx = gxx + idet
        slope_ref[2 + n] = (gxx * v["sxx"] + gyy * v["syy"] + gxy * v["sxy"]) * depth
        gU, gL = [], []
        for k in range(3):
            t = v["ts"][k]
            ze = v["z"] * e[k]
            ge = gxx * U[k] * U[k] + gyy * L[k] * L[k] + gxy * U[k] * L[k]
            slope_ref[5 + 3 * k + n] = (2.0 * part) * ge * ze * (1.0 - t * t)
            gU.append(ze * (2.0 * gxx * U[k] + gxy * L[k]))
            gL.append(ze * (2.0 * gyy * L[k] + gxy * U[k]))
        gq = [
            2.0 * (z * (gL[0] - gU[1]) + y * gU[2] - x * gL[2]),
            2.0 * (y * (gU[1] + gL[0]) + z * gU[2] - 2.0 * x * gL[1] - w * gL[2]),
            2.0 * (x * (gU[1] + gL[0]) - 2.0 * y * gU[0] + w * gU[2] + z * gL[2]),
            2.0 * (w * (gL[0] - gU[1]) - 2.0 * z * (gU[0] + gL[1]) + x * gU[2] + y * gL[2]),
        ]
        along = share * (w * gq[0] + x * gq[1] + y * gq[2] + z * gq[3])
        for k, unit in enumerate((w, x, y, z)):
            slope_ref[14 + 3 * k + n] = part * (gq[k] - unit * along) * v["inv"]


def update_kernel(mixed_ref, slope_ref, image_ref, *refs):
    sources = refs[:-9]
    outs = refs[-9:-6]
    picture_hbm = refs[-6]
    stages = refs[-5:-2]
    sems, picture_sem = refs[-2:]
    total, blocks, lanes = mixed_ref.shape
    rows = total // 3
    picture = pltpu.make_async_copy(image_ref, picture_hbm, picture_sem.at[0])
    picture.start()
    want = slope_ref[TERMS]
    taken = slope_ref[TERMS + 1] > 0.5
    wide = lambda row: jnp.broadcast_to(row, (blocks, lanes))
    grads = [jnp.zeros((blocks, lanes), jnp.float32) for _ in range(NPROJ)]
    for ref in sources:
        for side in range(2):
            mask = jnp.logical_and(want == wide(ref[side, NPROJ : NPROJ + 1, :]), taken if side else ~taken)
            for r in range(NPROJ):
                grads[r] = grads[r] + jnp.where(mask, wide(ref[side, r : r + 1, :]), 0.0)

    def store(i, grad):
        one = mixed_ref[rows + i] + grad
        two = mixed_ref[2 * rows + i] + ((1.0 - beta_two) / (1.0 - beta_one) ** 2) * (grad * grad)
        scaled = (rate_of(i) / (1.0 - beta_one**adam_step)) * one
        stages[0][i] = mixed_ref[i] - scaled / (jnp.sqrt(two * (1.0 / (1.0 - beta_two**adam_step))) + adam_eps)
        stages[1][i] = one
        stages[2][i] = two

    copies = []

    def ship(low, high):
        for a in range(3):
            copy = pltpu.make_async_copy(
                stages[a].at[low:high], outs[a].at[low:high], sems.at[len(copies)]
            )
            copy.start()
            copies.append(copy)

    for c in range(3):
        for k in range(SH):
            store(11 + SH * c + k, grads[6 + c] * slope_ref[27 + SH * c + k])
        ship(11 + SH * c, 11 + SH * (c + 1))
    store(0, grads[0] * slope_ref[0])
    store(1, grads[1] * slope_ref[1])
    for i in range(8):
        at = 2 + 3 * i
        store(2 + i, grads[2] * slope_ref[at] + grads[3] * slope_ref[at + 1] + grads[4] * slope_ref[at + 2])
    store(10, grads[5] * slope_ref[26])
    ship(0, 11)
    for copy in copies:
        copy.wait()
    picture.wait()


def on_device(params, first_moment, second_moment, view_basis, target, tile_blocks, moving):
    blocks, rows, lanes = params.shape
    peers = lax.axis_size("tile")
    listed = tile_blocks.shape[1]
    moves = moving.shape[1]
    pixels = target.shape[2]
    chunks = pixels // lanes
    width = listed * lanes
    f32 = jnp.float32
    smem = pl.BlockSpec(memory_space=pltpu.SMEM)
    vmem = pl.BlockSpec(memory_space=pltpu.VMEM)
    sds = jax.ShapeDtypeStruct

    hbm = pl.BlockSpec(memory_space=pltpu.HBM)
    stay = lambda value: pltpu.with_memory_space_constraint(value, pltpu.HBM)
    dma = pltpu.SemaphoreType.DMA
    turned = [jnp.transpose(a, (1, 0, 2)) for a in (params, first_moment, second_moment)]
    projected = pl.pallas_call(
        project_kernel,
        out_shape=sds((NPROJ, blocks, lanes), f32),
        in_specs=[hbm, hbm],
        out_specs=vmem,
        scratch_shapes=[pltpu.VMEM((rows, blocks, lanes), f32), pltpu.SMEM(view_basis.shape, f32), dma((5,))],
        compiler_params=pltpu.CompilerParams(vmem_limit_bytes=2 << 20),
        name="project",
    )(stay(view_basis), stay(turned[0]))

    def swapped(value, d):
        return lax.ppermute(value, "tile", [(i, i ^ d) for i in range(peers)])

    regions = lax.axis_size("region")
    onward = lambda value: lax.ppermute(value, "region", [(i, (i + 1) % regions) for i in range(regions)])

    leaving, state, moved, named = pl.pallas_call(
        pack_kernel,
        out_shape=(
            sds((3 * rows + 1, moves, lanes), f32),
            sds((3 * rows, blocks, lanes), f32),
            sds(moving.shape, jnp.int32),
            sds(tile_blocks.shape, jnp.int32),
        ),
        in_specs=[hbm] * 5,
        out_specs=(vmem, vmem, smem, smem),
        scratch_shapes=[dma((3 * PIECES + 2,))],
        compiler_params=pltpu.CompilerParams(vmem_limit_bytes=4 << 20),
        name="pack",
    )(stay(moving), stay(tile_blocks), *[stay(a) for a in turned])
    away = {0: projected}
    for d in range(1, peers):
        away[d] = swapped(projected, d)
    leaving, *rest = lax.optimization_barrier((leaving, *[away[d] for d in range(1, peers)]))
    for d in range(1, peers):
        away[d] = rest[d - 1]
    came = onward(leaving)
    image, slots = pl.pallas_call(
        functools.partial(composite_kernel, peers),
        out_shape=(sds((3, chunks, lanes), f32), sds((peers, GRADS, lanes), f32)),
        in_specs=[smem] + [vmem] * (peers + 1),
        out_specs=(vmem, vmem),
        scratch_shapes=[
            pltpu.VMEM((listed, GRADS, lanes), f32),
            pltpu.VMEM((5, width + 8, lanes), f32),
            pltpu.VMEM((chunks * width, lanes), f32),
            pltpu.VMEM((chunks * (width + 8), lanes), f32),
            pltpu.VMEM((chunks * (width + 8), lanes), f32),
            pltpu.VMEM((chunks * width, lanes), f32),
            pltpu.VMEM((8 * chunks, lanes), f32),
            pltpu.VMEM((6, width + 8, lanes), f32),
            pltpu.VMEM((listed, GRADS, lanes), f32),
            pltpu.VMEM((48, (chunks + 5) * lanes), jnp.bfloat16),
            pltpu.VMEM((width, 48), jnp.bfloat16),
        ],
        compiler_params=pltpu.CompilerParams(vmem_limit_bytes=(4 * chunks + 20) * (width + 8) * lanes * 4 + (3 << 20)),
        cost_estimate=pl.CostEstimate(
            flops=64 * width * pixels, transcendentals=width * pixels, bytes_accessed=48 * width * pixels
        ),
        name="composite",
    )(named, *[away[d] for d in reversed(range(peers))], target.reshape(3, chunks, lanes))
    passed = onward(slots)
    mixed, slope = pl.pallas_call(
        prepare_kernel,
        out_shape=(sds((3 * rows, blocks, lanes), f32), sds((TERMS + 2, blocks, lanes), f32)),
        in_specs=[smem, hbm, vmem, vmem],
        out_specs=(vmem, vmem),
        scratch_shapes=[pltpu.VMEM((8, blocks, lanes), f32), pltpu.SMEM(view_basis.shape, f32), dma((1,))],
        compiler_params=pltpu.CompilerParams(vmem_limit_bytes=5 << 20),
        name="prepare",
    )(moved, stay(view_basis), state, came)
    pairs = jnp.stack([slots, passed], axis=1)
    gathered = {0: pairs[0]}
    for d in range(1, peers):
        gathered[d] = swapped(pairs[d], d)
    updated = pl.pallas_call(
        update_kernel,
        out_shape=(sds((rows, blocks, lanes), f32),) * 3 + (sds(image.shape, f32),),
        in_specs=[vmem] * (3 + peers),
        out_specs=(hbm,) * 4,
        scratch_shapes=[pltpu.VMEM((rows, blocks, lanes), f32)] * 3 + [dma((12,)), dma((1,))],
        compiler_params=pltpu.CompilerParams(vmem_limit_bytes=5 << 20),
        name="update",
    )(mixed, slope, image, *[gathered[d] for d in reversed(range(peers))])
    turned_back = [jnp.transpose(a, (1, 0, 2)) for a in updated[:3]]
    return (*turned_back, updated[3].reshape(1, 3, pixels))


def solution(mesh):
    three = P(("region", "tile"), None, None)
    two = P(("region", "tile"), None)
    return jax.shard_map(
        on_device,
        mesh=mesh,
        in_specs=(three, three, three, P(), three, two, two),
        out_specs=(three, three, three, three),
        check_vma=False,
    )
```

```python
import math
import jax
import jax.numpy as jnp
import numpy as np
from jax import lax
from jax.experimental import pallas as pl
from jax.experimental.pallas import tpu as pltpu
from jax.sharding import PartitionSpec as P

SH = 16
TILE_SIDE = 32
NPROJ = 9
GRADS = 16
HALF = TILE_SIDE / 2.0

beta_one = 0.9
beta_two = 0.999
adam_eps = 1e-08
adam_step = 10.0
LOG2E = math.log2(math.e)


def rate_of(row):
    if row < 3:
        return 0.002
    if row < 6:
        return 0.005
    if row < 10:
        return 0.001
    if row < 11:
        return 0.05
    return 0.0025


def sigmoid(x):
    return 1.0 / (1.0 + jnp.exp(-x))


def geometry(p):
    v = {}
    v["tx"] = jnp.tanh(p(0))
    v["ty"] = jnp.tanh(p(1))
    depth = p(2)
    softplus = jnp.maximum(depth, 0.0) + jnp.log(1.0 + jnp.exp(-jnp.abs(depth)))
    v["f"] = 3.0 / (1.0 + softplus)
    v["z"] = v["f"] * v["f"]
    v["ts"] = [jnp.tanh(p(3 + k)) for k in range(3)]
    v["e"] = [2.25 * jnp.exp(2.0 * t) for t in v["ts"]]
    q = [p(6 + k) for k in range(4)]
    norm = jnp.sqrt((q[0] * q[0] + q[1] * q[1]) + (q[2] * q[2] + q[3] * q[3]))
    inv = 1.0 / jnp.maximum(norm, 1.0)
    v["norm"] = norm
    v["inv"] = inv
    w, x, y, z = [a * inv for a in q]
    v["q"] = (w, x, y, z)
    U = [1.0 - 2.0 * (y * y + z * z), 2.0 * (x * y - w * z), 2.0 * (x * z + w * y)]
    L = [2.0 * (x * y + w * z), 1.0 - 2.0 * (x * x + z * z), 2.0 * (y * z - w * x)]
    v["U"], v["L"] = U, L
    e = v["e"]
    v["sxx"] = U[0] * U[0] * e[0] + U[1] * U[1] * e[1] + U[2] * U[2] * e[2]
    v["syy"] = L[0] * L[0] * e[0] + L[1] * L[1] * e[1] + L[2] * L[2] * e[2]
    v["sxy"] = U[0] * L[0] * e[0] + U[1] * L[1] * e[1] + U[2] * L[2] * e[2]
    v["xx"] = v["z"] * v["sxx"] + 0.3
    v["yy"] = v["z"] * v["syy"] + 0.3
    v["xy"] = v["z"] * v["sxy"]
    v["idet"] = 1.0 / (v["xx"] * v["yy"] - v["xy"] * v["xy"])
    v["A"] = v["yy"] * v["idet"]
    v["B"] = -v["xy"] * v["idet"]
    v["C"] = v["xx"] * v["idet"]
    v["so"] = sigmoid(p(10) - 4.0)
    return v


def colour(p, c, basis):
    total = p(11 + SH * c) * basis(0)
    for k in range(1, SH):
        total = total + p(11 + SH * c + k) * basis(k)
    return sigmoid(total)


def project_kernel(basis_hbm, p_hbm, proj_ref, p_ref, basis_ref, sems):
    head = 11
    copies = [
        pltpu.make_async_copy(p_hbm.at[:head], p_ref.at[:head], sems.at[0]),
        pltpu.make_async_copy(basis_hbm, basis_ref, sems.at[1]),
    ]
    for c in range(3):
        span = pl.ds(head + SH * c, SH)
        copies.append(pltpu.make_async_copy(p_hbm.at[span], p_ref.at[span], sems.at[2 + c]))
    for copy in copies:
        copy.start()
    p = lambda i: p_ref[i]
    copies[0].wait()
    v = geometry(p)
    proj_ref[0] = 0.375 * TILE_SIDE * v["tx"]
    proj_ref[1] = 0.375 * TILE_SIDE * v["ty"]
    proj_ref[2] = v["A"]
    proj_ref[3] = v["B"]
    proj_ref[4] = v["C"]
    proj_ref[5] = 0.99 * v["so"]
    copies[1].wait()
    for c in range(3):
        copies[2 + c].wait()
        proj_ref[6 + c] = colour(p, c, lambda k: basis_ref[k])


def picks(moving_ref, blocks, lanes):
    slot = lax.broadcasted_iota(jnp.int32, (blocks, lanes), 0)
    source = jnp.zeros((blocks, lanes), jnp.int32)
    taken = jnp.zeros((blocks, lanes), jnp.bool_)
    for m in range(moving_ref.shape[1]):
        here = slot == moving_ref[0, m]
        source = jnp.where(here, m, source)
        taken = jnp.logical_or(taken, here)
    return source, taken


PIECES = 4


def pieces(rows):
    cuts = [rows * n // PIECES for n in range(PIECES + 1)]
    return list(zip(cuts[:-1], cuts[1:]))


def pack_kernel(moving_hbm, listed_hbm, p_hbm, f_hbm, s_hbm, leave_ref, state_ref, mine_ref, place_ref, moving_ref, listed_ref, sems):
    total, moves, lanes = leave_ref.shape
    rows, blocks, _ = p_hbm.shape
    ids = pltpu.make_async_copy(moving_hbm, moving_ref, sems.at[3 * PIECES])
    ids.start()
    lists = pltpu.make_async_copy(listed_hbm, listed_ref, sems.at[3 * PIECES + 1])
    lists.start()
    spans = []
    copies = []
    for a, ref in enumerate((p_hbm, f_hbm, s_hbm)):
        for low, high in pieces(rows):
            span = (a * rows + low, a * rows + high)
            copy = pltpu.make_async_copy(ref.at[low:high], state_ref.at[span[0] : span[1]], sems.at[len(copies)])
            copy.start()
            spans.append(span)
            copies.append(copy)
    ids.wait()
    lists.wait()
    source, taken = picks(moving_ref, blocks, lanes)
    mine_ref[0] = source
    mine_ref[1] = taken.astype(jnp.int32)
    me = lax.axis_index("tile")
    for d in range(place_ref.shape[1]):
        place, named = jnp.int32(0), jnp.int32(0)
        for n in range(listed_ref.shape[1]):
            entry = listed_ref[0, n]
            here = lax.div(entry, jnp.int32(blocks)) == jnp.bitwise_xor(me, d)
            place = jnp.where(here, n, place)
            named = jnp.where(here, lax.rem(entry, jnp.int32(blocks)), named)
        place_ref[0, d] = jnp.zeros((blocks, lanes), jnp.int32) + place
        place_ref[1, d] = jnp.zeros((blocks, lanes), jnp.int32) + named
    slot = lax.broadcasted_iota(jnp.int32, (blocks, lanes), 0)
    pick = jnp.zeros((blocks, lanes), jnp.int32)
    for m in range(moves):
        pick = jnp.where(slot == m, moving_ref[0, m], pick)
    leave_ref[total - 1] = pick[:moves].astype(jnp.float32)
    for copy, span in zip(copies, spans):
        copy.wait()
        for i in range(*span):
            leave_ref[i] = jnp.take_along_axis(state_ref[i], pick, axis=0)[:moves]


def split(value):
    high = value.astype(jnp.bfloat16).astype(jnp.float32)
    rest = value - high
    middle = rest.astype(jnp.bfloat16).astype(jnp.float32)
    return high, middle, rest - middle


def composite_kernel(place_ref, *refs):
    peers = place_ref.shape[1]
    sources = refs[:peers][::-1]
    target_ref = refs[peers]
    image_ref = refs[peers + 1]
    slots_ref = refs[peers + 2]
    pbuf, qbuf, abuf, wbuf, ebuf, shbuf, errbuf, rbuf, gbuf, basis, lbuf = refs[peers + 3 :]
    listed, _, lanes = pbuf.shape
    width = listed * lanes
    groups = width // 8
    chunks = errbuf.shape[0] // 8
    spreads = qbuf.shape[0]
    assert chunks == 8
    at_place = [[place_ref[0, d] == j for d in range(peers)] for j in range(listed)]
    for r in range(NPROJ):
        found = [jnp.take_along_axis(sources[d][r], place_ref[1, d], axis=0) for d in range(peers)]
        for j in range(listed):
            row = found[0]
            for d in range(1, peers):
                row = jnp.where(at_place[j][d], found[d], row)
            pbuf[j, r : r + 1, :] = row[0:1]

    lane = lax.broadcasted_iota(jnp.int32, (8, lanes), 1)
    which = lax.broadcasted_iota(jnp.int32, (8, lanes), 0)
    px = (lane % TILE_SIDE).astype(jnp.float32) + (0.5 - HALF)
    py = (lane // TILE_SIDE).astype(jnp.float32) + (0.5 - HALF)
    step = float(lanes // TILE_SIDE)
    middle = py + step * ((chunks - 1) / 2.0)
    zero = jnp.zeros((8, lanes), jnp.float32)
    one = zero + 1.0

    def rows(*values):
        out = zero
        for r, value in enumerate(values):
            out = jnp.where(which == r, value, out)
        return out

    blank = jnp.zeros((24, lanes), jnp.bfloat16)
    for c in range(chunks):
        y = py + step * c
        high, low, _ = split(px * y)
        mono = rows(one, px, y, (px * px - 0.25) * 0.5, (y * y - 0.25) * 0.5, high, low)
        part = jnp.concatenate([mono, mono, mono], axis=0).astype(jnp.bfloat16)
        basis[0:24, c * lanes : (c + 1) * lanes] = part
        basis[24:48, c * lanes : (c + 1) * lanes] = blank
    for k in range(spreads):
        pick = jnp.where(which == k, one, zero)
        at = (chunks + k) * lanes
        basis[0:24, at : at + lanes] = blank
        basis[24:48, at : at + lanes] = jnp.concatenate([pick, pick, pick], axis=0).astype(jnp.bfloat16)

    def product(left, right):
        return jnp.dot(left, right, preferred_element_type=jnp.float32)

    def alphas(j, _):
        mx, my, ca, cb, cc, op = [pbuf[j, r : r + 1, :] for r in range(6)]
        a = -0.5 * LOG2E * ca
        b = -LOG2E * cb
        c = -0.5 * LOG2E * cc
        bx = b * mx
        by = b * my
        ax = a * mx
        cy = c * my
        flat = (ax + by) * mx + cy * my + 0.25 * (a + c) + jnp.log(op) * LOG2E
        power = rows(flat, -(2.0 * ax + by), -(2.0 * cy + bx), 2.0 * a, 2.0 * c, b, b)
        plain = rows(mx, my, *[pbuf[j, 6 + k : 7 + k, :] for k in range(3)])
        colours = rows(*[pbuf[j, 6 + k : 7 + k, :] for k in range(3)])
        high, mid, low = split(colours)
        left = jnp.concatenate([*split(power), *split(plain)], axis=0).T.astype(jnp.bfloat16)
        lbuf[pl.ds(pl.multiple_of(j * lanes, lanes), lanes), :] = jnp.concatenate(
            [high, high, mid, mid, high, low], axis=0
        ).T.astype(jnp.bfloat16)
        out = product(left, basis[...])
        for u in range(lanes // 8):
            row = pl.multiple_of(j * lanes + u * 8, 8)
            for n in range(chunks):
                part = out[u * 8 : (u + 1) * 8, n * lanes : (n + 1) * lanes]
                abuf[pl.ds(row * chunks + n * 8, 8), :] = jnp.exp2(part)
            for k in range(spreads):
                qbuf[k, pl.ds(row, 8), :] = out[u * 8 : (u + 1) * 8, (chunks + k) * lanes : (chunks + k + 1) * lanes]
        return 0

    lax.fori_loop(0, listed, alphas, 0, unroll=min(listed, 4))

    batch = 32

    def forward(n, running):
        trans, image = running
        base = pl.multiple_of(n * (batch * chunks), batch * chunks)
        for i in range(batch):
            alpha = abuf[pl.ds(base + (i // 8) * (8 * chunks) + i % 8, chunks, stride=8), :]
            weight = trans * alpha
            trans = trans * (1.0 - alpha)
            wbuf[pl.ds(base + i * chunks, chunks), :] = weight
            image = tuple(
                image[k] + weight * jnp.broadcast_to(qbuf[2 + k, pl.ds(n * batch + i, 1), :], (chunks, lanes))
                for k in range(3)
            )
        return (trans, image)

    _, image = lax.fori_loop(0, width // batch, forward, (one, (zero, zero, zero)))
    for k in range(8):
        if k < 3:
            image_ref[k] = image[k]
            errbuf[k * chunks : (k + 1) * chunks, :] = 2.0 * (image[k] - target_ref[k])
        else:
            errbuf[k * chunks : (k + 1) * chunks, :] = zero
    for c in range(chunks):
        high, mid, low = split(errbuf[pl.ds(c, 8, stride=chunks), :])
        basis[:, c * lanes : (c + 1) * lanes] = jnp.concatenate([high, mid, high, mid, low, high], axis=0).astype(
            jnp.bfloat16
        )

    def shading(j, _):
        out = product(lbuf[pl.ds(pl.multiple_of(j * lanes, lanes), lanes), :], basis[:, : chunks * lanes])
        for u in range(lanes // 8):
            row = pl.multiple_of(j * lanes + u * 8, 8)
            for n in range(chunks):
                shbuf[pl.ds(row * chunks + n * 8, 8), :] = out[u * 8 : (u + 1) * 8, n * lanes : (n + 1) * lanes]
        return 0

    lax.fori_loop(0, listed, shading, 0, unroll=min(listed, 4))
    for buf in (wbuf, ebuf):
        buf[pl.ds(width * chunks, 8 * chunks), :] = jnp.zeros((8 * chunks, lanes), jnp.float32)
    for k in range(2):
        qbuf[k, pl.ds(width, 8), :] = zero

    def reduce_pixels(u):
        row = pl.multiple_of(u * 8, 8)
        base = pl.multiple_of(u * (8 * chunks), 8 * chunks)
        part = [ebuf[pl.ds(base + c, 8, stride=chunks), :] for c in range(chunks)]
        dx = px - qbuf[0, pl.ds(row, 8), :]
        dy = middle - qbuf[1, pl.ds(row, 8), :]
        half = chunks // 2
        away = [((chunks - 1) / 2.0 - c) * step for c in range(half)]
        even = [part[c] + part[chunks - 1 - c] for c in range(half)]
        odd = [part[chunks - 1 - c] - part[c] for c in range(half)]
        plain = (even[0] + even[1]) + (even[2] + even[3])
        tilt = (away[0] * odd[0] + away[1] * odd[1]) + (away[2] * odd[2] + away[3] * odd[3])
        bend = (away[0] ** 2 * even[0] + away[1] ** 2 * even[1]) + (away[2] ** 2 * even[2] + away[3] ** 2 * even[3])
        sum_y = dy * plain + tilt
        sum_yy = dy * (sum_y + tilt) + bend
        sum_x = dx * plain
        sums = [plain, sum_x, sum_y, dx * sum_x, dx * sum_y, sum_yy]
        for r, value in enumerate(sums):
            rbuf[r, pl.ds(row, 8), :] = value

    def backward(n, behind):
        u = groups - 1 - n
        base = pl.multiple_of(u * (8 * chunks), 8 * chunks)
        reduce_pixels(u + 1)
        for i in reversed(range(8)):
            alpha = abuf[pl.ds(base + i, chunks, stride=8), :]
            shade = shbuf[pl.ds(base + i, chunks, stride=8), :]
            weight = wbuf[pl.ds(base + i * chunks, chunks), :]
            ebuf[pl.ds(base + i * chunks, chunks), :] = weight * (shade - behind)
            behind = (1.0 - alpha) * behind + alpha * shade
        return behind

    lax.fori_loop(0, groups, backward, zero, unroll=16)
    reduce_pixels(0)

    def finish(j, _):
        at = pl.ds(pl.multiple_of(j * lanes, lanes), lanes)
        part = [jnp.sum(rbuf[r, at, :].T, axis=0, keepdims=True) for r in range(6)]
        first = pl.multiple_of(j * lanes * chunks, lanes * chunks)
        lights = [wbuf[pl.ds(first + c, lanes, stride=chunks), :] for c in range(chunks)]
        lit = jnp.zeros((lanes, 48), jnp.float32)
        for n in range(2):
            terms = [light.astype(jnp.bfloat16) for light in lights]
            lights = [light - term.astype(jnp.float32) for light, term in zip(lights, terms)]
            lit = lit + lax.dot_general(
                jnp.concatenate(terms, axis=1),
                basis[:, : chunks * lanes],
                (((1,), (1,)), ((), ())),
                preferred_element_type=jnp.float32,
            )
        lit = lit.T
        part += [lit[k : k + 1] + lit[8 + k : 9 + k] + lit[32 + k : 33 + k] for k in range(3)]
        s0, sx, sy, sxx, sxy, syy = part[:6]
        ca, cb, cc, op = [pbuf[j, r : r + 1, :] for r in range(2, 6)]
        gbuf[j, 0:1, :] = ca * sx + cb * sy
        gbuf[j, 1:2, :] = cb * sx + cc * sy
        gbuf[j, 2:3, :] = -0.5 * sxx
        gbuf[j, 3:4, :] = -sxy
        gbuf[j, 4:5, :] = -0.5 * syy
        gbuf[j, 5:6, :] = s0 / op
        for k in range(3):
            gbuf[j, 6 + k : 7 + k, :] = part[6 + k]
        gbuf[j, 9:16, :] = jnp.zeros((7, lanes), jnp.float32)
        return 0

    lax.fori_loop(0, listed, finish, 0, unroll=min(listed, 4))
    for d in range(peers):
        for low in range(0, GRADS, 8):
            out = gbuf[0, low : low + 8, :]
            for j in range(1, listed):
                out = jnp.where(at_place[j][d], gbuf[j, low : low + 8, :], out)
            slots_ref[d, low : low + 8, :] = out
        slots_ref[d, NPROJ : NPROJ + 1, :] = place_ref[1, d][0:1].astype(jnp.float32)


TERMS = 2 + 3 * 8 + 1 + 3 * SH


def prepare_kernel(mine_ref, basis_hbm, state_ref, came_ref, mixed_ref, slope_ref, kbuf, basis_ref, sem):
    fetch = pltpu.make_async_copy(basis_hbm, basis_ref, sem.at[0])
    fetch.start()
    total, blocks, lanes = state_ref.shape
    rows = total // 3
    moves = came_ref.shape[1]
    source = mine_ref[0]
    taken = mine_ref[1] > 0

    def arrived(i):
        kbuf[i % 8, 0:moves, :] = came_ref[i]
        return jnp.take_along_axis(kbuf[i % 8], source, axis=0)

    for a, factor in enumerate((None, beta_one, beta_two)):
        for i in range(a * rows, (a + 1) * rows):
            value = jnp.where(taken, arrived(i), state_ref[i])
            mixed_ref[i] = value if factor is None else factor * value
    slot = lax.broadcasted_iota(jnp.int32, (blocks, lanes), 0).astype(jnp.float32)
    slope_ref[TERMS] = jnp.where(taken, arrived(total), slot)
    slope_ref[TERMS + 1] = taken.astype(jnp.float32)

    part = 1.0 - beta_one
    p = lambda i: mixed_ref[i]
    v = geometry(p)
    slope_ref[0] = part * 0.375 * TILE_SIDE * (1.0 - v["tx"] * v["tx"])
    slope_ref[1] = part * 0.375 * TILE_SIDE * (1.0 - v["ty"] * v["ty"])
    slope_ref[26] = part * 0.99 * v["so"] * (1.0 - v["so"])
    fetch.wait()
    for c in range(3):
        shade = colour(p, c, lambda k: basis_ref[k])
        rise = part * shade * (1.0 - shade)
        for k in range(SH):
            slope_ref[27 + SH * c + k] = rise * basis_ref[k]
    U, L, e, f, idet = v["U"], v["L"], v["e"], v["f"], v["idet"]
    w, x, y, z = v["q"]
    share = jnp.where(v["norm"] > 1.0, 1.0, jnp.where(v["norm"] == 1.0, 0.5, 0.0))
    depth = (-2.0 / 3.0) * f * f * f * sigmoid(p(2)) * part
    for n, name in enumerate("ABC"):
        gdet = -v[name] * idet
        gxx = gdet * v["yy"]
        gyy = gdet * v["xx"]
        gxy = -2.0 * gdet * v["xy"]
        if name == "A":
            gyy = gyy + idet
        elif name == "B":
            gxy = gxy - idet
        else:
            gxx = gxx + idet
        slope_ref[2 + n] = (gxx * v["sxx"] + gyy * v["syy"] + gxy * v["sxy"]) * depth
        gU, gL = [], []
        for k in range(3):
            t = v["ts"][k]
            ze = v["z"] * e[k]
            ge = gxx * U[k] * U[k] + gyy * L[k] * L[k] + gxy * U[k] * L[k]
            slope_ref[5 + 3 * k + n] = (2.0 * part) * ge * ze * (1.0 - t * t)
            gU.append(ze * (2.0 * gxx * U[k] + gxy * L[k]))
            gL.append(ze * (2.0 * gyy * L[k] + gxy * U[k]))
        gq = [
            2.0 * (z * (gL[0] - gU[1]) + y * gU[2] - x * gL[2]),
            2.0 * (y * (gU[1] + gL[0]) + z * gU[2] - 2.0 * x * gL[1] - w * gL[2]),
            2.0 * (x * (gU[1] + gL[0]) - 2.0 * y * gU[0] + w * gU[2] + z * gL[2]),
            2.0 * (w * (gL[0] - gU[1]) - 2.0 * z * (gU[0] + gL[1]) + x * gU[2] + y * gL[2]),
        ]
        along = share * (w * gq[0] + x * gq[1] + y * gq[2] + z * gq[3])
        for k, unit in enumerate((w, x, y, z)):
            slope_ref[14 + 3 * k + n] = part * (gq[k] - unit * along) * v["inv"]


def update_kernel(mixed_ref, slope_ref, image_ref, *refs):
    sources = refs[:-9]
    outs = refs[-9:-6]
    picture_hbm = refs[-6]
    stages = refs[-5:-2]
    sems, picture_sem = refs[-2:]
    total, blocks, lanes = mixed_ref.shape
    rows = total // 3
    picture = pltpu.make_async_copy(image_ref, picture_hbm, picture_sem.at[0])
    picture.start()
    want = slope_ref[TERMS]
    taken = slope_ref[TERMS + 1] > 0.5
    wide = lambda row: jnp.broadcast_to(row, (blocks, lanes))
    grads = [jnp.zeros((blocks, lanes), jnp.float32) for _ in range(NPROJ)]
    for ref in sources:
        for side in range(2):
            mask = jnp.logical_and(want == wide(ref[side, NPROJ : NPROJ + 1, :]), taken if side else ~taken)
            for r in range(NPROJ):
                grads[r] = grads[r] + jnp.where(mask, wide(ref[side, r : r + 1, :]), 0.0)

    def store(i, grad):
        one = mixed_ref[rows + i] + grad
        two = mixed_ref[2 * rows + i] + ((1.0 - beta_two) / (1.0 - beta_one) ** 2) * (grad * grad)
        scaled = (rate_of(i) / (1.0 - beta_one**adam_step)) * one
        stages[0][i] = mixed_ref[i] - scaled / (jnp.sqrt(two * (1.0 / (1.0 - beta_two**adam_step))) + adam_eps)
        stages[1][i] = one
        stages[2][i] = two

    copies = []

    def ship(low, high):
        for a in range(3):
            copy = pltpu.make_async_copy(
                stages[a].at[low:high], outs[a].at[low:high], sems.at[len(copies)]
            )
            copy.start()
            copies.append(copy)

    for c in range(3):
        for k in range(SH):
            store(11 + SH * c + k, grads[6 + c] * slope_ref[27 + SH * c + k])
        ship(11 + SH * c, 11 + SH * (c + 1))
    store(0, grads[0] * slope_ref[0])
    store(1, grads[1] * slope_ref[1])
    for i in range(8):
        at = 2 + 3 * i
        store(2 + i, grads[2] * slope_ref[at] + grads[3] * slope_ref[at + 1] + grads[4] * slope_ref[at + 2])
    store(10, grads[5] * slope_ref[26])
    ship(0, 11)
    for copy in copies:
        copy.wait()
    picture.wait()


def on_device(params, first_moment, second_moment, view_basis, target, tile_blocks, moving):
    blocks, rows, lanes = params.shape
    peers = lax.axis_size("tile")
    listed = tile_blocks.shape[1]
    moves = moving.shape[1]
    pixels = target.shape[2]
    chunks = pixels // lanes
    width = listed * lanes
    f32 = jnp.float32
    vmem = pl.BlockSpec(memory_space=pltpu.VMEM)
    sds = jax.ShapeDtypeStruct

    hbm = pl.BlockSpec(memory_space=pltpu.HBM)
    stay = lambda value: pltpu.with_memory_space_constraint(value, pltpu.HBM)
    dma = pltpu.SemaphoreType.DMA
    turned = [jnp.transpose(a, (1, 0, 2)) for a in (params, first_moment, second_moment)]
    projected = pl.pallas_call(
        project_kernel,
        out_shape=sds((NPROJ, blocks, lanes), f32),
        in_specs=[hbm, hbm],
        out_specs=vmem,
        scratch_shapes=[pltpu.VMEM((rows, blocks, lanes), f32), pltpu.SMEM(view_basis.shape, f32), dma((5,))],
        compiler_params=pltpu.CompilerParams(vmem_limit_bytes=2 << 20),
        name="project",
    )(stay(view_basis), stay(turned[0]))

    def swapped(value, d):
        return lax.ppermute(value, "tile", [(i, i ^ d) for i in range(peers)])

    regions = lax.axis_size("region")
    onward = lambda value: lax.ppermute(value, "region", [(i, (i + 1) % regions) for i in range(regions)])

    leaving, state, mine, place = pl.pallas_call(
        pack_kernel,
        out_shape=(
            sds((3 * rows + 1, moves, lanes), f32),
            sds((3 * rows, blocks, lanes), f32),
            sds((2, blocks, lanes), jnp.int32),
            sds((2, peers, blocks, lanes), jnp.int32),
        ),
        in_specs=[hbm] * 5,
        out_specs=(vmem,) * 4,
        scratch_shapes=[
            pltpu.SMEM(moving.shape, jnp.int32),
            pltpu.SMEM(tile_blocks.shape, jnp.int32),
            dma((3 * PIECES + 2,)),
        ],
        compiler_params=pltpu.CompilerParams(vmem_limit_bytes=4 << 20),
        name="pack",
    )(stay(moving), stay(tile_blocks), *[stay(a) for a in turned])
    away = {0: projected}
    for d in range(1, peers):
        away[d] = swapped(projected, d)
    leaving, *rest = lax.optimization_barrier((leaving, *[away[d] for d in range(1, peers)]))
    for d in range(1, peers):
        away[d] = rest[d - 1]
    came = onward(leaving)
    image, slots = pl.pallas_call(
        composite_kernel,
        out_shape=(sds((3, chunks, lanes), f32), sds((peers, GRADS, lanes), f32)),
        in_specs=[vmem] * (peers + 2),
        out_specs=(vmem, vmem),
        scratch_shapes=[
            pltpu.VMEM((listed, GRADS, lanes), f32),
            pltpu.VMEM((5, width + 8, lanes), f32),
            pltpu.VMEM((chunks * width, lanes), f32),
            pltpu.VMEM((chunks * (width + 8), lanes), f32),
            pltpu.VMEM((chunks * (width + 8), lanes), f32),
            pltpu.VMEM((chunks * width, lanes), f32),
            pltpu.VMEM((8 * chunks, lanes), f32),
            pltpu.VMEM((6, width + 8, lanes), f32),
            pltpu.VMEM((listed, GRADS, lanes), f32),
            pltpu.VMEM((48, (chunks + 5) * lanes), jnp.bfloat16),
            pltpu.VMEM((width, 48), jnp.bfloat16),
        ],
        compiler_params=pltpu.CompilerParams(vmem_limit_bytes=(4 * chunks + 20) * (width + 8) * lanes * 4 + (3 << 20)),
        cost_estimate=pl.CostEstimate(
            flops=64 * width * pixels, transcendentals=width * pixels, bytes_accessed=48 * width * pixels
        ),
        name="composite",
    )(place, *[away[d] for d in reversed(range(peers))], target.reshape(3, chunks, lanes))
    passed = onward(slots)
    mixed, slope = pl.pallas_call(
        prepare_kernel,
        out_shape=(sds((3 * rows, blocks, lanes), f32), sds((TERMS + 2, blocks, lanes), f32)),
        in_specs=[vmem, hbm, vmem, vmem],
        out_specs=(vmem, vmem),
        scratch_shapes=[pltpu.VMEM((8, blocks, lanes), f32), pltpu.SMEM(view_basis.shape, f32), dma((1,))],
        compiler_params=pltpu.CompilerParams(vmem_limit_bytes=5 << 20),
        name="prepare",
    )(mine, stay(view_basis), state, came)
    pairs = jnp.stack([slots, passed], axis=1)
    gathered = {0: pairs[0]}
    for d in range(1, peers):
        gathered[d] = swapped(pairs[d], d)
    updated = pl.pallas_call(
        update_kernel,
        out_shape=(sds((rows, blocks, lanes), f32),) * 3 + (sds(image.shape, f32),),
        in_specs=[vmem] * (3 + peers),
        out_specs=(hbm,) * 4,
        scratch_shapes=[pltpu.VMEM((rows, blocks, lanes), f32)] * 3 + [dma((12,)), dma((1,))],
        compiler_params=pltpu.CompilerParams(vmem_limit_bytes=5 << 20),
        name="update",
    )(mixed, slope, image, *[gathered[d] for d in reversed(range(peers))])
    turned_back = [jnp.transpose(a, (1, 0, 2)) for a in updated[:3]]
    return (*turned_back, updated[3].reshape(1, 3, pixels))


def solution(mesh):
    three = P(("region", "tile"), None, None)
    two = P(("region", "tile"), None)
    return jax.shard_map(
        on_device,
        mesh=mesh,
        in_specs=(three, three, three, P(), three, two, two),
        out_specs=(three, three, three, three),
        check_vma=False,
    )
```

```python
import math
import jax
import jax.numpy as jnp
import numpy as np
from jax import lax
from jax.experimental import pallas as pl
from jax.experimental.pallas import tpu as pltpu
from jax.sharding import PartitionSpec as P

SH = 16
TILE_SIDE = 32
NPROJ = 9
GRADS = 16
HALF = TILE_SIDE / 2.0

beta_one = 0.9
beta_two = 0.999
adam_eps = 1e-08
adam_step = 10.0
LOG2E = math.log2(math.e)


def rate_of(row):
    if row < 3:
        return 0.002
    if row < 6:
        return 0.005
    if row < 10:
        return 0.001
    if row < 11:
        return 0.05
    return 0.0025


def sigmoid(x):
    return 1.0 / (1.0 + jnp.exp(-x))


def geometry(p):
    v = {}
    v["tx"] = jnp.tanh(p(0))
    v["ty"] = jnp.tanh(p(1))
    depth = p(2)
    softplus = jnp.maximum(depth, 0.0) + jnp.log(1.0 + jnp.exp(-jnp.abs(depth)))
    v["f"] = 3.0 / (1.0 + softplus)
    v["z"] = v["f"] * v["f"]
    v["ts"] = [jnp.tanh(p(3 + k)) for k in range(3)]
    v["e"] = [2.25 * jnp.exp(2.0 * t) for t in v["ts"]]
    q = [p(6 + k) for k in range(4)]
    norm = jnp.sqrt((q[0] * q[0] + q[1] * q[1]) + (q[2] * q[2] + q[3] * q[3]))
    inv = 1.0 / jnp.maximum(norm, 1.0)
    v["norm"] = norm
    v["inv"] = inv
    w, x, y, z = [a * inv for a in q]
    v["q"] = (w, x, y, z)
    U = [1.0 - 2.0 * (y * y + z * z), 2.0 * (x * y - w * z), 2.0 * (x * z + w * y)]
    L = [2.0 * (x * y + w * z), 1.0 - 2.0 * (x * x + z * z), 2.0 * (y * z - w * x)]
    v["U"], v["L"] = U, L
    e = v["e"]
    v["sxx"] = U[0] * U[0] * e[0] + U[1] * U[1] * e[1] + U[2] * U[2] * e[2]
    v["syy"] = L[0] * L[0] * e[0] + L[1] * L[1] * e[1] + L[2] * L[2] * e[2]
    v["sxy"] = U[0] * L[0] * e[0] + U[1] * L[1] * e[1] + U[2] * L[2] * e[2]
    v["xx"] = v["z"] * v["sxx"] + 0.3
    v["yy"] = v["z"] * v["syy"] + 0.3
    v["xy"] = v["z"] * v["sxy"]
    v["idet"] = 1.0 / (v["xx"] * v["yy"] - v["xy"] * v["xy"])
    v["A"] = v["yy"] * v["idet"]
    v["B"] = -v["xy"] * v["idet"]
    v["C"] = v["xx"] * v["idet"]
    v["so"] = sigmoid(p(10) - 4.0)
    return v


def colour(p, c, basis):
    total = p(11 + SH * c) * basis(0)
    for k in range(1, SH):
        total = total + p(11 + SH * c + k) * basis(k)
    return sigmoid(total)


def project_kernel(basis_hbm, p_hbm, proj_ref, p_ref, basis_ref, sems):
    head = 11
    copies = [
        pltpu.make_async_copy(p_hbm.at[:head], p_ref.at[:head], sems.at[0]),
        pltpu.make_async_copy(basis_hbm, basis_ref, sems.at[1]),
    ]
    for c in range(3):
        span = pl.ds(head + SH * c, SH)
        copies.append(pltpu.make_async_copy(p_hbm.at[span], p_ref.at[span], sems.at[2 + c]))
    for copy in copies:
        copy.start()
    p = lambda i: p_ref[i]
    copies[0].wait()
    v = geometry(p)
    proj_ref[0] = 0.375 * TILE_SIDE * v["tx"]
    proj_ref[1] = 0.375 * TILE_SIDE * v["ty"]
    proj_ref[2] = v["A"]
    proj_ref[3] = v["B"]
    proj_ref[4] = v["C"]
    proj_ref[5] = 0.99 * v["so"]
    copies[1].wait()
    for c in range(3):
        copies[2 + c].wait()
        proj_ref[6 + c] = colour(p, c, lambda k: basis_ref[k])


def picks(moving_ref, blocks, lanes):
    slot = lax.broadcasted_iota(jnp.int32, (blocks, lanes), 0)
    source = jnp.zeros((blocks, lanes), jnp.int32)
    taken = jnp.zeros((blocks, lanes), jnp.bool_)
    for m in range(moving_ref.shape[1]):
        here = slot == moving_ref[0, m]
        source = jnp.where(here, m, source)
        taken = jnp.logical_or(taken, here)
    return source, taken


PIECES = 4


def pieces(rows):
    cuts = [rows * n // PIECES for n in range(PIECES + 1)]
    return list(zip(cuts[:-1], cuts[1:]))


def pack_kernel(moving_hbm, listed_hbm, p_hbm, f_hbm, s_hbm, leave_ref, state_ref, mine_ref, place_ref, moving_ref, listed_ref, sems):
    total, moves, lanes = leave_ref.shape
    rows, blocks, _ = p_hbm.shape
    ids = pltpu.make_async_copy(moving_hbm, moving_ref, sems.at[3 * PIECES])
    ids.start()
    lists = pltpu.make_async_copy(listed_hbm, listed_ref, sems.at[3 * PIECES + 1])
    lists.start()
    spans = []
    copies = []
    for a, ref in enumerate((p_hbm, f_hbm, s_hbm)):
        for low, high in pieces(rows):
            span = (a * rows + low, a * rows + high)
            copy = pltpu.make_async_copy(ref.at[low:high], state_ref.at[span[0] : span[1]], sems.at[len(copies)])
            copy.start()
            spans.append(span)
            copies.append(copy)
    ids.wait()
    lists.wait()
    source, taken = picks(moving_ref, blocks, lanes)
    mine_ref[0] = source
    mine_ref[1] = taken.astype(jnp.int32)
    me = lax.axis_index("tile")
    for d in range(place_ref.shape[1]):
        place, named = jnp.int32(0), jnp.int32(0)
        for n in range(listed_ref.shape[1]):
            entry = listed_ref[0, n]
            here = lax.div(entry, jnp.int32(blocks)) == jnp.bitwise_xor(me, d)
            place = jnp.where(here, n, place)
            named = jnp.where(here, lax.rem(entry, jnp.int32(blocks)), named)
        place_ref[0, d] = jnp.zeros((blocks, lanes), jnp.int32) + place
        place_ref[1, d] = jnp.zeros((blocks, lanes), jnp.int32) + named
    slot = lax.broadcasted_iota(jnp.int32, (blocks, lanes), 0)
    pick = jnp.zeros((blocks, lanes), jnp.int32)
    for m in range(moves):
        pick = jnp.where(slot == m, moving_ref[0, m], pick)
    leave_ref[total - 1] = pick[:moves].astype(jnp.float32)
    for copy, span in zip(copies, spans):
        copy.wait()
        for i in range(*span):
            leave_ref[i] = jnp.take_along_axis(state_ref[i], pick, axis=0)[:moves]


def split(value):
    high = value.astype(jnp.bfloat16).astype(jnp.float32)
    rest = value - high
    middle = rest.astype(jnp.bfloat16).astype(jnp.float32)
    return high, middle, rest - middle


def composite_kernel(place_ref, *refs):
    peers = place_ref.shape[1]
    sources = refs[:peers][::-1]
    target_ref = refs[peers]
    image_ref = refs[peers + 1]
    slots_ref = refs[peers + 2]
    pbuf, qbuf, abuf, wbuf, ebuf, shbuf, errbuf, rbuf, gbuf, basis, lbuf = refs[peers + 3 :]
    listed, _, lanes = pbuf.shape
    width = listed * lanes
    groups = width // 8
    chunks = errbuf.shape[0] // 8
    spreads = qbuf.shape[0]
    assert chunks == 8
    at_place = [[place_ref[0, d] == j for d in range(peers)] for j in range(listed)]
    for r in range(NPROJ):
        found = [jnp.take_along_axis(sources[d][r], place_ref[1, d], axis=0) for d in range(peers)]
        for j in range(listed):
            row = found[0]
            for d in range(1, peers):
                row = jnp.where(at_place[j][d], found[d], row)
            pbuf[j, r : r + 1, :] = row[0:1]

    lane = lax.broadcasted_iota(jnp.int32, (8, lanes), 1)
    which = lax.broadcasted_iota(jnp.int32, (8, lanes), 0)
    px = (lane % TILE_SIDE).astype(jnp.float32) + (0.5 - HALF)
    py = (lane // TILE_SIDE).astype(jnp.float32) + (0.5 - HALF)
    step = float(lanes // TILE_SIDE)
    middle = py + step * ((chunks - 1) / 2.0)
    zero = jnp.zeros((8, lanes), jnp.float32)
    one = zero + 1.0

    def rows(*values):
        out = zero
        for r, value in enumerate(values):
            out = jnp.where(which == r, value, out)
        return out

    blank = jnp.zeros((24, lanes), jnp.bfloat16)
    for c in range(chunks):
        y = py + step * c
        high, low, _ = split(px * y)
        mono = rows(one, px, y, (px * px - 0.25) * 0.5, (y * y - 0.25) * 0.5, high, low)
        part = jnp.concatenate([mono, mono, mono], axis=0).astype(jnp.bfloat16)
        basis[0:24, c * lanes : (c + 1) * lanes] = part
        basis[24:48, c * lanes : (c + 1) * lanes] = blank
    for k in range(spreads):
        pick = jnp.where(which == k, one, zero)
        at = (chunks + k) * lanes
        basis[0:24, at : at + lanes] = blank
        basis[24:48, at : at + lanes] = jnp.concatenate([pick, pick, pick], axis=0).astype(jnp.bfloat16)

    def product(left, right):
        return jnp.dot(left, right, preferred_element_type=jnp.float32)

    def alphas(j, _):
        mx, my, ca, cb, cc, op = [pbuf[j, r : r + 1, :] for r in range(6)]
        a = -0.5 * LOG2E * ca
        b = -LOG2E * cb
        c = -0.5 * LOG2E * cc
        bx = b * mx
        by = b * my
        ax = a * mx
        cy = c * my
        flat = (ax + by) * mx + cy * my + 0.25 * (a + c) + jnp.log(op) * LOG2E
        power = rows(flat, -(2.0 * ax + by), -(2.0 * cy + bx), 2.0 * a, 2.0 * c, b, b)
        plain = rows(mx, my, *[pbuf[j, 6 + k : 7 + k, :] for k in range(3)])
        colours = rows(*[pbuf[j, 6 + k : 7 + k, :] for k in range(3)])
        high, mid, low = split(colours)
        left = jnp.concatenate([*split(power), *split(plain)], axis=0).T.astype(jnp.bfloat16)
        lbuf[pl.ds(pl.multiple_of(j * lanes, lanes), lanes), :] = jnp.concatenate(
            [high, high, mid, mid, high, low], axis=0
        ).T.astype(jnp.bfloat16)
        out = product(left, basis[...])
        for u in range(lanes // 8):
            row = pl.multiple_of(j * lanes + u * 8, 8)
            for n in range(chunks):
                part = out[u * 8 : (u + 1) * 8, n * lanes : (n + 1) * lanes]
                abuf[pl.ds(row * chunks + n * 8, 8), :] = jnp.exp2(part)
            for k in range(spreads):
                qbuf[k, pl.ds(row, 8), :] = out[u * 8 : (u + 1) * 8, (chunks + k) * lanes : (chunks + k + 1) * lanes]
        return 0

    lax.fori_loop(0, listed, alphas, 0, unroll=min(listed, 4))

    batch = 32

    def forward(n, running):
        trans, image = running
        base = pl.multiple_of(n * (batch * chunks), batch * chunks)
        for i in range(batch):
            alpha = abuf[pl.ds(base + (i // 8) * (8 * chunks) + i % 8, chunks, stride=8), :]
            weight = trans * alpha
            trans = trans * (1.0 - alpha)
            wbuf[pl.ds(base + i * chunks, chunks), :] = weight
            image = tuple(
                image[k] + weight * jnp.broadcast_to(qbuf[2 + k, pl.ds(n * batch + i, 1), :], (chunks, lanes))
                for k in range(3)
            )
        return (trans, image)

    _, image = lax.fori_loop(0, width // batch, forward, (one, (zero, zero, zero)))
    for k in range(8):
        if k < 3:
            image_ref[k] = image[k]
            errbuf[k * chunks : (k + 1) * chunks, :] = 2.0 * (image[k] - target_ref[k])
        else:
            errbuf[k * chunks : (k + 1) * chunks, :] = zero
    for c in range(chunks):
        high, mid, low = split(errbuf[pl.ds(c, 8, stride=chunks), :])
        basis[:, c * lanes : (c + 1) * lanes] = jnp.concatenate([high, mid, high, mid, low, high], axis=0).astype(
            jnp.bfloat16
        )

    def shading(j, _):
        out = product(lbuf[pl.ds(pl.multiple_of(j * lanes, lanes), lanes), :], basis[:, : chunks * lanes])
        for u in range(lanes // 8):
            row = pl.multiple_of(j * lanes + u * 8, 8)
            for n in range(chunks):
                shbuf[pl.ds(row * chunks + n * 8, 8), :] = out[u * 8 : (u + 1) * 8, n * lanes : (n + 1) * lanes]
        return 0

    lax.fori_loop(0, listed, shading, 0, unroll=min(listed, 4))
    for buf in (wbuf, ebuf):
        buf[pl.ds(width * chunks, 8 * chunks), :] = jnp.zeros((8 * chunks, lanes), jnp.float32)
    for k in range(2):
        qbuf[k, pl.ds(width, 8), :] = zero

    def reduce_pixels(u):
        row = pl.multiple_of(u * 8, 8)
        base = pl.multiple_of(u * (8 * chunks), 8 * chunks)
        part = [ebuf[pl.ds(base + c, 8, stride=chunks), :] for c in range(chunks)]
        dx = px - qbuf[0, pl.ds(row, 8), :]
        dy = middle - qbuf[1, pl.ds(row, 8), :]
        half = chunks // 2
        away = [((chunks - 1) / 2.0 - c) * step for c in range(half)]
        even = [part[c] + part[chunks - 1 - c] for c in range(half)]
        odd = [part[chunks - 1 - c] - part[c] for c in range(half)]
        plain = (even[0] + even[1]) + (even[2] + even[3])
        tilt = (away[0] * odd[0] + away[1] * odd[1]) + (away[2] * odd[2] + away[3] * odd[3])
        bend = (away[0] ** 2 * even[0] + away[1] ** 2 * even[1]) + (away[2] ** 2 * even[2] + away[3] ** 2 * even[3])
        sum_y = dy * plain + tilt
        sum_yy = dy * (sum_y + tilt) + bend
        sum_x = dx * plain
        sums = [plain, sum_x, sum_y, dx * sum_x, dx * sum_y, sum_yy]
        for r, value in enumerate(sums):
            rbuf[r, pl.ds(row, 8), :] = value

    def backward(n, behind):
        u = groups - 1 - n
        base = pl.multiple_of(u * (8 * chunks), 8 * chunks)
        reduce_pixels(u + 1)
        for i in reversed(range(8)):
            alpha = abuf[pl.ds(base + i, chunks, stride=8), :]
            shade = shbuf[pl.ds(base + i, chunks, stride=8), :]
            weight = wbuf[pl.ds(base + i * chunks, chunks), :]
            ebuf[pl.ds(base + i * chunks, chunks), :] = weight * (shade - behind)
            behind = (1.0 - alpha) * behind + alpha * shade
        return behind

    lax.fori_loop(0, groups, backward, zero, unroll=16)
    reduce_pixels(0)

    def finish(j, _):
        at = pl.ds(pl.multiple_of(j * lanes, lanes), lanes)
        part = [jnp.sum(rbuf[r, at, :].T, axis=0, keepdims=True) for r in range(6)]
        first = pl.multiple_of(j * lanes * chunks, lanes * chunks)
        lights = [wbuf[pl.ds(first + c, lanes, stride=chunks), :] for c in range(chunks)]
        lit = jnp.zeros((lanes, 48), jnp.float32)
        for n in range(2):
            terms = [light.astype(jnp.bfloat16) for light in lights]
            lights = [light - term.astype(jnp.float32) for light, term in zip(lights, terms)]
            lit = lit + lax.dot_general(
                jnp.concatenate(terms, axis=1),
                basis[:, : chunks * lanes],
                (((1,), (1,)), ((), ())),
                preferred_element_type=jnp.float32,
            )
        lit = lit.T
        part += [lit[k : k + 1] + lit[8 + k : 9 + k] + lit[32 + k : 33 + k] for k in range(3)]
        s0, sx, sy, sxx, sxy, syy = part[:6]
        ca, cb, cc, op = [pbuf[j, r : r + 1, :] for r in range(2, 6)]
        gbuf[j, 0:1, :] = ca * sx + cb * sy
        gbuf[j, 1:2, :] = cb * sx + cc * sy
        gbuf[j, 2:3, :] = -0.5 * sxx
        gbuf[j, 3:4, :] = -sxy
        gbuf[j, 4:5, :] = -0.5 * syy
        gbuf[j, 5:6, :] = s0 / op
        for k in range(3):
            gbuf[j, 6 + k : 7 + k, :] = part[6 + k]
        gbuf[j, 9:16, :] = jnp.zeros((7, lanes), jnp.float32)
        return 0

    lax.fori_loop(0, listed, finish, 0, unroll=min(listed, 4))
    for d in range(peers):
        for low in range(0, GRADS, 8):
            out = gbuf[0, low : low + 8, :]
            for j in range(1, listed):
                out = jnp.where(at_place[j][d], gbuf[j, low : low + 8, :], out)
            slots_ref[d, low : low + 8, :] = out
        slots_ref[d, NPROJ : NPROJ + 1, :] = place_ref[1, d][0:1].astype(jnp.float32)


TERMS = 2 + 3 * 8 + 1 + 3 * SH


def gather_grads(grads, ref, want, taken):
    wide = lambda row: jnp.broadcast_to(row, want.shape)
    for side in range(2):
        mask = jnp.logical_and(want == wide(ref[side, NPROJ : NPROJ + 1, :]), taken if side else ~taken)
        grads = [grads[r] + jnp.where(mask, wide(ref[side, r : r + 1, :]), 0.0) for r in range(NPROJ)]
    return grads


def prepare_kernel(mine_ref, basis_hbm, state_ref, came_ref, near_ref, mixed_ref, slope_ref, early_ref, kbuf, basis_ref, sem):
    fetch = pltpu.make_async_copy(basis_hbm, basis_ref, sem.at[0])
    fetch.start()
    total, blocks, lanes = state_ref.shape
    rows = total // 3
    moves = came_ref.shape[1]
    source = mine_ref[0]
    taken = mine_ref[1] > 0

    def arrived(i):
        kbuf[i % 8, 0:moves, :] = came_ref[i]
        return jnp.take_along_axis(kbuf[i % 8], source, axis=0)

    for a, factor in enumerate((None, beta_one, beta_two)):
        for i in range(a * rows, (a + 1) * rows):
            value = jnp.where(taken, arrived(i), state_ref[i])
            mixed_ref[i] = value if factor is None else factor * value
    slot = lax.broadcasted_iota(jnp.int32, (blocks, lanes), 0).astype(jnp.float32)
    slope_ref[TERMS] = jnp.where(taken, arrived(total), slot)
    slope_ref[TERMS + 1] = taken.astype(jnp.float32)
    start = [jnp.zeros((blocks, lanes), jnp.float32) for _ in range(NPROJ)]
    for r, value in enumerate(gather_grads(start, near_ref, slope_ref[TERMS], taken)):
        early_ref[r] = value

    part = 1.0 - beta_one
    p = lambda i: mixed_ref[i]
    v = geometry(p)
    slope_ref[0] = part * 0.375 * TILE_SIDE * (1.0 - v["tx"] * v["tx"])
    slope_ref[1] = part * 0.375 * TILE_SIDE * (1.0 - v["ty"] * v["ty"])
    slope_ref[26] = part * 0.99 * v["so"] * (1.0 - v["so"])
    fetch.wait()
    for c in range(3):
        shade = colour(p, c, lambda k: basis_ref[k])
        rise = part * shade * (1.0 - shade)
        for k in range(SH):
            slope_ref[27 + SH * c + k] = rise * basis_ref[k]
    U, L, e, f, idet = v["U"], v["L"], v["e"], v["f"], v["idet"]
    w, x, y, z = v["q"]
    share = jnp.where(v["norm"] > 1.0, 1.0, jnp.where(v["norm"] == 1.0, 0.5, 0.0))
    depth = (-2.0 / 3.0) * f * f * f * sigmoid(p(2)) * part
    for n, name in enumerate("ABC"):
        gdet = -v[name] * idet
        gxx = gdet * v["yy"]
        gyy = gdet * v["xx"]
        gxy = -2.0 * gdet * v["xy"]
        if name == "A":
            gyy = gyy + idet
        elif name == "B":
            gxy = gxy - idet
        else:
            gxx = gxx + idet
        slope_ref[2 + n] = (gxx * v["sxx"] + gyy * v["syy"] + gxy * v["sxy"]) * depth
        gU, gL = [], []
        for k in range(3):
            t = v["ts"][k]
            ze = v["z"] * e[k]
            ge = gxx * U[k] * U[k] + gyy * L[k] * L[k] + gxy * U[k] * L[k]
            slope_ref[5 + 3 * k + n] = (2.0 * part) * ge * ze * (1.0 - t * t)
            gU.append(ze * (2.0 * gxx * U[k] + gxy * L[k]))
            gL.append(ze * (2.0 * gyy * L[k] + gxy * U[k]))
        gq = [
            2.0 * (z * (gL[0] - gU[1]) + y * gU[2] - x * gL[2]),
            2.0 * (y * (gU[1] + gL[0]) + z * gU[2] - 2.0 * x * gL[1] - w * gL[2]),
            2.0 * (x * (gU[1] + gL[0]) - 2.0 * y * gU[0] + w * gU[2] + z * gL[2]),
            2.0 * (w * (gL[0] - gU[1]) - 2.0 * z * (gU[0] + gL[1]) + x * gU[2] + y * gL[2]),
        ]
        along = share * (w * gq[0] + x * gq[1] + y * gq[2] + z * gq[3])
        for k, unit in enumerate((w, x, y, z)):
            slope_ref[14 + 3 * k + n] = part * (gq[k] - unit * along) * v["inv"]


def update_kernel(mixed_ref, slope_ref, early_ref, image_ref, *refs):
    sources = refs[:-9]
    outs = refs[-9:-6]
    picture_hbm = refs[-6]
    stages = refs[-5:-2]
    sems, picture_sem = refs[-2:]
    total, blocks, lanes = mixed_ref.shape
    rows = total // 3
    picture = pltpu.make_async_copy(image_ref, picture_hbm, picture_sem.at[0])
    picture.start()
    want = slope_ref[TERMS]
    taken = slope_ref[TERMS + 1] > 0.5
    grads = [early_ref[r] for r in range(NPROJ)]
    for ref in sources:
        grads = gather_grads(grads, ref, want, taken)

    def store(i, grad):
        one = mixed_ref[rows + i] + grad
        two = mixed_ref[2 * rows + i] + ((1.0 - beta_two) / (1.0 - beta_one) ** 2) * (grad * grad)
        scaled = (rate_of(i) / (1.0 - beta_one**adam_step)) * one
        stages[0][i] = mixed_ref[i] - scaled / (jnp.sqrt(two * (1.0 / (1.0 - beta_two**adam_step))) + adam_eps)
        stages[1][i] = one
        stages[2][i] = two

    copies = []

    def ship(low, high):
        for a in range(3):
            copy = pltpu.make_async_copy(
                stages[a].at[low:high], outs[a].at[low:high], sems.at[len(copies)]
            )
            copy.start()
            copies.append(copy)

    for c in range(3):
        for k in range(SH):
            store(11 + SH * c + k, grads[6 + c] * slope_ref[27 + SH * c + k])
        ship(11 + SH * c, 11 + SH * (c + 1))
    store(0, grads[0] * slope_ref[0])
    store(1, grads[1] * slope_ref[1])
    for i in range(8):
        at = 2 + 3 * i
        store(2 + i, grads[2] * slope_ref[at] + grads[3] * slope_ref[at + 1] + grads[4] * slope_ref[at + 2])
    store(10, grads[5] * slope_ref[26])
    ship(0, 11)
    for copy in copies:
        copy.wait()
    picture.wait()


def on_device(params, first_moment, second_moment, view_basis, target, tile_blocks, moving):
    blocks, rows, lanes = params.shape
    peers = lax.axis_size("tile")
    listed = tile_blocks.shape[1]
    moves = moving.shape[1]
    pixels = target.shape[2]
    chunks = pixels // lanes
    width = listed * lanes
    f32 = jnp.float32
    vmem = pl.BlockSpec(memory_space=pltpu.VMEM)
    sds = jax.ShapeDtypeStruct

    hbm = pl.BlockSpec(memory_space=pltpu.HBM)
    stay = lambda value: pltpu.with_memory_space_constraint(value, pltpu.HBM)
    dma = pltpu.SemaphoreType.DMA
    turned = [jnp.transpose(a, (1, 0, 2)) for a in (params, first_moment, second_moment)]
    projected = pl.pallas_call(
        project_kernel,
        out_shape=sds((NPROJ, blocks, lanes), f32),
        in_specs=[hbm, hbm],
        out_specs=vmem,
        scratch_shapes=[pltpu.VMEM((rows, blocks, lanes), f32), pltpu.SMEM(view_basis.shape, f32), dma((5,))],
        compiler_params=pltpu.CompilerParams(vmem_limit_bytes=2 << 20),
        name="project",
    )(stay(view_basis), stay(turned[0]))

    def swapped(value, d):
        return lax.ppermute(value, "tile", [(i, i ^ d) for i in range(peers)])

    regions = lax.axis_size("region")
    onward = lambda value: lax.ppermute(value, "region", [(i, (i + 1) % regions) for i in range(regions)])

    leaving, state, mine, place = pl.pallas_call(
        pack_kernel,
        out_shape=(
            sds((3 * rows + 1, moves, lanes), f32),
            sds((3 * rows, blocks, lanes), f32),
            sds((2, blocks, lanes), jnp.int32),
            sds((2, peers, blocks, lanes), jnp.int32),
        ),
        in_specs=[hbm] * 5,
        out_specs=(vmem,) * 4,
        scratch_shapes=[
            pltpu.SMEM(moving.shape, jnp.int32),
            pltpu.SMEM(tile_blocks.shape, jnp.int32),
            dma((3 * PIECES + 2,)),
        ],
        compiler_params=pltpu.CompilerParams(vmem_limit_bytes=4 << 20),
        name="pack",
    )(stay(moving), stay(tile_blocks), *[stay(a) for a in turned])
    away = {0: projected}
    for d in range(1, peers):
        away[d] = swapped(projected, d)
    leaving, *rest = lax.optimization_barrier((leaving, *[away[d] for d in range(1, peers)]))
    for d in range(1, peers):
        away[d] = rest[d - 1]
    came = onward(leaving)
    image, slots = pl.pallas_call(
        composite_kernel,
        out_shape=(sds((3, chunks, lanes), f32), sds((peers, GRADS, lanes), f32)),
        in_specs=[vmem] * (peers + 2),
        out_specs=(vmem, vmem),
        scratch_shapes=[
            pltpu.VMEM((listed, GRADS, lanes), f32),
            pltpu.VMEM((5, width + 8, lanes), f32),
            pltpu.VMEM((chunks * width, lanes), f32),
            pltpu.VMEM((chunks * (width + 8), lanes), f32),
            pltpu.VMEM((chunks * (width + 8), lanes), f32),
            pltpu.VMEM((chunks * width, lanes), f32),
            pltpu.VMEM((8 * chunks, lanes), f32),
            pltpu.VMEM((6, width + 8, lanes), f32),
            pltpu.VMEM((listed, GRADS, lanes), f32),
            pltpu.VMEM((48, (chunks + 5) * lanes), jnp.bfloat16),
            pltpu.VMEM((width, 48), jnp.bfloat16),
        ],
        compiler_params=pltpu.CompilerParams(vmem_limit_bytes=(4 * chunks + 20) * (width + 8) * lanes * 4 + (3 << 20)),
        cost_estimate=pl.CostEstimate(
            flops=64 * width * pixels, transcendentals=width * pixels, bytes_accessed=48 * width * pixels
        ),
        name="composite",
    )(place, *[away[d] for d in reversed(range(peers))], target.reshape(3, chunks, lanes))
    passed = onward(slots)
    pairs = jnp.stack([slots, passed], axis=1)
    mixed, slope, early = pl.pallas_call(
        prepare_kernel,
        out_shape=(sds((3 * rows, blocks, lanes), f32), sds((TERMS + 2, blocks, lanes), f32), sds((NPROJ, blocks, lanes), f32)),
        in_specs=[vmem, hbm, vmem, vmem, vmem],
        out_specs=(vmem,) * 3,
        scratch_shapes=[pltpu.VMEM((8, blocks, lanes), f32), pltpu.SMEM(view_basis.shape, f32), dma((1,))],
        compiler_params=pltpu.CompilerParams(vmem_limit_bytes=5 << 20),
        name="prepare",
    )(mine, stay(view_basis), state, came, pairs[0])
    gathered = {}
    for d in range(1, peers):
        gathered[d] = swapped(pairs[d], d)
    updated = pl.pallas_call(
        update_kernel,
        out_shape=(sds((rows, blocks, lanes), f32),) * 3 + (sds(image.shape, f32),),
        in_specs=[vmem] * (3 + peers),
        out_specs=(hbm,) * 4,
        scratch_shapes=[pltpu.VMEM((rows, blocks, lanes), f32)] * 3 + [dma((12,)), dma((1,))],
        compiler_params=pltpu.CompilerParams(vmem_limit_bytes=5 << 20),
        name="update",
    )(mixed, slope, early, image, *[gathered[d] for d in reversed(range(1, peers))])
    turned_back = [jnp.transpose(a, (1, 0, 2)) for a in updated[:3]]
    return (*turned_back, updated[3].reshape(1, 3, pixels))


def solution(mesh):
    three = P(("region", "tile"), None, None)
    two = P(("region", "tile"), None)
    return jax.shard_map(
        on_device,
        mesh=mesh,
        in_specs=(three, three, three, P(), three, two, two),
        out_specs=(three, three, three, three),
        check_vma=False,
    )
```
